32 devices in a mesh: ens: 4 (over x, core), lat: 8 (over z, y).
Axes of the slice: x: 2, y: 2, z: 4, core: 2. Of those that a mesh axis runs over, the one named last changes fastest.
Arguments:
- fields: bfloat16 [8, 24, 48, 1440], P('ens', None, 'lat'), may hold values from -6 to 6
- depth_kernel: float32 [24, 7, 7], replicated, may hold values from -0.875 to 0.875
- mix_weight: bfloat16 [24, 24], replicated, may hold values from -1.25 to 1.25
- legendre: bfloat16 [48, 160, 160], P('lat'), may hold values from -1.25 to 1.25
- truth: bfloat16 [24, 2, 160, 160], replicated, may hold values from -6 to 6
- degree_order: int32 [160], replicated, may hold values from 0 to 159, each once
Outputs:
- grad_fields: bfloat16 [8, 24, 48, 1440], P('ens', None, 'lat')
- score_grad: float32 [8, 24, 2, 160, 160], P('ens', None, None, None, 'lat')
The draws below stay inside these ranges and needn't reach their ends.
Inputs may be any that keep to these rules, and one draw needn't show every extreme that they name: `degree_order`: each degree appears once.
All inputs are finite; a program needn't handle non-finite values.
Results may differ from the reference program's by a relative error of at most 0.02.
Values may be sent and summed in bfloat16 or wider, within the bound.
No kernel may reach another device: no remote copies, remote signals or barrier semaphores. Data moves between devices by JAX's collectives and lax.ppermute only.
A program may use at most 128 MiB of HBM per device.

```python
import math
import jax
import jax.numpy as jnp
from jax import lax

C = 24
NLON = 1440
M = 160
L = 160
NLAT = 48
MEMBERS = 8


def strengthened(result, own_key, source, target, shards_of, factor):
    def block_of(dim):
        return (jnp.arange(result.shape[dim]) // (result.shape[dim] // shards_of)).reshape((-1,) + (1,) * (result.ndim - 1 - dim))

    first = jax.random.permutation(own_key, shards_of)[block_of(target)]
    other_side = (block_of(target) + shards_of // 2) % shards_of
    return jnp.where((block_of(source) == first) | (block_of(source) == other_side), factor * result, result)


def level_of(key, extent, pieces, smallest, top_value):
    def one(axis_at, shards_of):
        draws = jax.random.uniform(jax.random.fold_in(jax.random.fold_in(key, 6), axis_at), (shards_of,), jnp.float32, smallest / len(pieces), top_value / len(pieces))
        return jnp.repeat(jnp.exp(draws), extent[axis_at] // shards_of).reshape((-1,) + (1,) * (len(extent) - axis_at - 1))

    loudness = one(*pieces[0])
    for cut in pieces[1:]:
        loudness = loudness * one(*cut)
    return loudness


def gaussian(rng, shape, spread, most, cuts=(), kind=jnp.bfloat16):
    result = jax.random.normal(rng, shape, jnp.float32) * spread
    if len(cuts) > 0:
        result = level_of(rng, shape, cuts, -0.22, 0.18) * result
    return jnp.clip(result, min=-most, max=most).astype(kind)


def heavy_noise(stream_key, dims, deviation, limit, shards, heavy, held_as=jnp.bfloat16):
    drawn = deviation * jax.random.normal(stream_key, dims, jnp.float32)
    if shards:
        drawn = drawn * level_of(stream_key, dims, shards, -0.22, 0.18)
    return jnp.clip(strengthened(drawn, jax.random.fold_in(stream_key, 3), *heavy), -limit, limit).astype(held_as)


def setup_inputs(seed: int = 0) -> dict:
    splits = jax.random.split(jax.random.key(seed), 7)
    return {
        "fields": gaussian(splits[0], (MEMBERS, C, NLAT, NLON), 1.0, 6.0, ((0, 4), (2, 8))),
        "depth_kernel": gaussian(splits[1], (C, 7, 7), 49 ** -0.5, 0.875, (), jnp.float32),
        "mix_weight": gaussian(splits[2], (C, C), C ** -0.5, 1.25),
        "legendre": heavy_noise(splits[3], (NLAT, M, L), NLAT ** -0.5, 1.25, ((0, 8),), (0, 2, 8, 2.0)),
        "truth": gaussian(splits[4], (C, 2, M, L), 1.0, 6.0),
        "degree_order": jax.random.permutation(splits[5], L).astype(jnp.int32),
    }


smooth_width = 0.5

def wave_table():
    columns = jnp.arange(NLON, dtype=jnp.int32)
    orders = jnp.arange(M, dtype=jnp.int32)
    angles = (columns[:, None] * orders[None, :] % NLON).astype(jnp.float32) * (2.0 * math.pi / NLON)
    return (jnp.concatenate([jnp.cos(angles), -jnp.sin(angles)], axis=1) / math.sqrt(NLON)).astype(jnp.bfloat16)

def depthwise(padded, kernel):
    height = padded.shape[-2] - 6
    breadth = padded.shape[-1]
    widened = jnp.concatenate([padded[..., -3:], padded, padded[..., :3]], axis=-1)
    running = jnp.zeros(padded.shape[:-2] + (height, breadth), jnp.float32)
    for row_off in range(7):
        for col_off in range(7):
            running = running + kernel[:, row_off, col_off][:, None, None] * widened[..., row_off:row_off + height, col_off:col_off + breadth]
    return running

def soft_sign(gaps):
    return gaps / jnp.sqrt(gaps * gaps + smooth_width * smooth_width)

def hidden_of(member, kernel):
    padded = jnp.pad(member.astype(jnp.float32), ((0, 0), (3, 3), (0, 0)))
    return padded[:, 3:-3] + depthwise(padded, kernel)

def reference(fields, depth_kernel, mix_weight, legendre, truth, degree_order):
    table = wave_table()
    table_full = legendre.astype(jnp.float32)
    mixing = mix_weight.astype(jnp.float32)

    def forward(member):
        hidden = hidden_of(member, depth_kernel)
        activation = jax.nn.gelu(hidden).astype(jnp.bfloat16)
        mixed_out = jnp.einsum('oc,cij->oij', mixing, activation.astype(jnp.float32)).astype(jnp.bfloat16)
        spectral = jnp.dot(mixed_out, table, preferred_element_type=jnp.float32).astype(jnp.bfloat16)
        spectral = spectral.reshape(C, NLAT, 2, M).astype(jnp.float32)
        return jnp.einsum('cirm,iml->crml', spectral, table_full)
    coeff = lax.map(forward, fields)
    target = truth.astype(jnp.float32)
    ens_count = MEMBERS

    def member_grad(own_coeff):
        pair_sum = lax.optimization_barrier(jnp.sum(soft_sign(own_coeff[None] - coeff), axis=0))
        return soft_sign(own_coeff - target) / ens_count - pair_sum / (ens_count * (ens_count - 1))
    gradient = lax.map(member_grad, coeff)
    score_grad = jnp.take(gradient, degree_order, axis=4)
    sent = gradient.astype(jnp.bfloat16)
    flipped = depth_kernel[:, ::-1, ::-1]

    def backward(inputs):
        member, coeff_grad = inputs
        hidden = hidden_of(member, depth_kernel)
        spec_grad = jnp.einsum('crml,iml->cirm', coeff_grad.astype(jnp.float32), table_full).astype(jnp.bfloat16)
        spec_grad = spec_grad.reshape(C, NLAT, 2 * M)
        mix_grad = jnp.dot(spec_grad, table.T, preferred_element_type=jnp.float32).astype(jnp.bfloat16)
        act_grad = jnp.einsum('oc,oij->cij', mixing, mix_grad.astype(jnp.float32))
        hid_grad = jax.vjp(jax.nn.gelu, hidden)[1](act_grad)[0]
        padded_grad = jnp.pad(hid_grad, ((0, 0), (3, 3), (0, 0)))
        return (hid_grad + depthwise(padded_grad, flipped)).astype(jnp.bfloat16)
    grad_fields = lax.map(backward, (fields, sent))
    return (grad_fields, score_grad)
```

```python
import functools
import math

import jax
import jax.numpy as jnp
import numpy as np
from jax import lax
from jax.experimental import pallas as pl
from jax.experimental.pallas import tpu as pltpu
from jax.sharding import PartitionSpec as P

smooth_width = 0.5
LEAD = 8
F32 = jnp.float32
BF16 = jnp.bfloat16


def up(value, step):
    return -(-value // step) * step


def full(shape):
    return pl.BlockSpec(shape, lambda *_: (0,) * len(shape), memory_space=pltpu.VMEM)


def wave_table(nlon, orders, groups, order_pad):
    share = orders // groups
    columns = np.arange(nlon, dtype=np.int64)
    number = np.arange(orders, dtype=np.int64)
    angles = (columns[:, None] * number[None, :] % nlon) * (2.0 * math.pi / nlon)
    table = np.zeros((nlon, 2, groups, order_pad), np.float32)
    for part, values in enumerate((np.cos(angles), -np.sin(angles))):
        table[:, part, :, :share] = (values / math.sqrt(nlon)).reshape(nlon, groups, share)
    return table.reshape(nlon, 2 * groups * order_pad).astype(jnp.bfloat16)


def neighbours(block, width):
    count = lax.axis_size("lat")
    forward = [(i, i + 1) for i in range(count - 1)]
    backward = [(target, source) for source, target in forward]
    low = lax.ppermute(block[:, block.shape[1] - width :], "lat", forward)
    high = lax.ppermute(block[:, :width], "lat", backward)
    return low, high


def convolve(own, low, high, taps, padded, emit):
    members, rows, chans, nlon = own.shape
    wide = padded.shape[-1]
    pad = low.shape[1]

    def fill(row, value):
        value = value.astype(F32)
        ext = jnp.concatenate(
            [value[:, nlon - LEAD :], value, value[:, : wide - nlon - LEAD]], axis=-1
        )
        padded[row] = ext

    @pl.loop(0, members)
    def _(b):
        for row in range(pad):
            fill(row, low[b, row])
            fill(row + pad + rows, high[b, row])
        for row in range(rows):
            fill(row + pad, own[b, row])

        @pl.loop(0, chans // 8)
        def _(ct):
            c0 = pl.multiple_of(ct * 8, 8)

            @pl.loop(0, rows)
            def _(i):
                total = None
                for q in range(7):
                    part = None
                    for p in range(7):
                        weight = jnp.tile(taps[p * 7 + q, pl.ds(c0, 8), :], (1, wide // 128))
                        term = weight * padded[i + p, pl.ds(c0, 8), :]
                        part = term if part is None else part + term
                    if q != 3:
                        part = pltpu.roll(part, (3 - q) % wide, 1)
                    total = part if total is None else total + part
                emit(b, i, c0, total[:, LEAD : LEAD + nlon])


def gelu_pair(x):
    scale = math.sqrt(2.0 / math.pi)
    square = x * x
    t = jnp.tanh(scale * x * (1.0 + 0.044715 * square))
    half = 0.5 * (1.0 + t)
    slope = half + 0.5 * x * (1.0 - t * t) * (scale * (1.0 + 3 * 0.044715 * square))
    return x * half, slope


def forward_kernel(own, low, high, taps, table, mixer, out, slope, padded, act):
    members, rows, chans, nlon = own.shape
    owners, groups, order_pad, lanes = out.shape

    def emit(b, i, c0, value):
        value, grad = gelu_pair(value)
        act[b, i, pl.ds(c0, 8), :] = value
        slope[b, i, pl.ds(c0, 8), :] = grad

    convolve(own, low, high, taps, padded, emit)
    rows_all = members * rows * chans
    flat = act[...].reshape(rows_all, nlon).astype(BF16)
    spectral = jnp.dot(flat, table[...], preferred_element_type=F32).astype(BF16)
    half = groups * order_pad
    mixed = None
    for r in range(2):
        part = lax.dot_general(
            spectral[:, r * half : (r + 1) * half],
            mixer[r],
            (((0,), (0,)), ((), ())),
            preferred_element_type=F32,
        )
        mixed = part if mixed is None else mixed + part
    for e in range(owners):
        out[e] = mixed[:, e * lanes : (e + 1) * lanes].reshape(groups, order_pad, lanes).astype(BF16)


def soft_sign(gaps):
    return gaps * lax.rsqrt(gaps * gaps + smooth_width * smooth_width)


def score_kernel(rows, got, legendre, target, order, back, grads, spread, gather):
    owners, groups, order_pad, lanes = got.shape
    orders, nlat, degrees = legendre.shape
    slots = target.shape[1]
    ens = spread.shape[1] // slots
    local = ens // owners
    width = local * slots
    for t in range(groups):
        for i in range(rows):
            pieces = [got[e, t, :, i * width : (i + 1) * width] for e in range(owners)]
            at = (t * rows + i) * order_pad
            spread[at : at + order_pad, :] = jnp.concatenate(pieces, axis=-1).astype(F32)
    gather[...] = jnp.zeros(gather.shape, F32)

    @pl.loop(0, orders)
    def _(m):
        block = spread[pl.ds(m, nlat, stride=order_pad), :].astype(BF16)
        leg = legendre[m]
        coeff = lax.dot_general(
            block, leg, (((0,), (0,)), ((), ())), preferred_element_type=F32
        )
        own = [coeff[k * slots : (k + 1) * slots] for k in range(ens)]
        truth = target[m].astype(F32)
        sums = [None] * ens
        for k in range(ens):
            for n in range(k + 1, ens):
                sign = soft_sign(own[k] - own[n])
                sums[k] = sign if sums[k] is None else sums[k] + sign
                sums[n] = -sign if sums[n] is None else sums[n] - sign
        grad = jnp.concatenate(
            [
                soft_sign(own[k] - truth) * (1.0 / ens) - sums[k] * (1.0 / (ens * (ens - 1)))
                for k in range(ens)
            ],
            axis=0,
        ).astype(BF16)
        spec = lax.dot_general(
            leg, grad, (((1,), (1,)), ((), ())), preferred_element_type=F32
        )
        gather[pl.ds(m, nlat, stride=order_pad), :] = spec
        grads[m] = jnp.dot(grad, order[...], preferred_element_type=F32).astype(BF16)

    for t in range(groups):
        for e in range(owners):
            pieces = []
            for i in range(rows):
                at = (t * rows + i) * order_pad
                pieces.append(gather[at : at + order_pad, e * width : (e + 1) * width])
            if lanes > rows * width:
                pieces.append(jnp.zeros((order_pad, lanes - rows * width), F32))
            back[e, t] = jnp.concatenate(pieces, axis=-1).astype(BF16)


def backward_kernel(got, mixer, table, slope, out, flat):
    owners, groups, order_pad, lanes = got.shape
    members, rows, chans, nlon = slope.shape
    half = groups * order_pad
    spectra = jnp.concatenate(
        [got[e].reshape(half, lanes) for e in range(owners)], axis=-1
    )
    parts = []
    for r in range(2):
        parts.append(
            lax.dot_general(
                mixer[r], spectra, (((1,), (1,)), ((), ())), preferred_element_type=F32
            ).astype(BF16)
        )
    unmixed = jnp.concatenate(parts, axis=-1)
    flat[...] = lax.dot_general(
        unmixed, table[...], (((1,), (1,)), ((), ())), preferred_element_type=F32
    ).reshape(flat.shape)
    for b in range(members):
        for i in range(rows):
            out[b, i] = (flat[b, i] * slope[b, i]).astype(BF16)


def convolve_kernel(own, low, high, taps, out, padded, stage):
    members, rows, chans, nlon = own.shape

    def emit(b, i, c0, value):
        stage[b, i, pl.ds(c0, 8), :] = value

    convolve(own, low, high, taps, padded, emit)
    out[...] = stage[...].astype(BF16)


def tap_planes(kernel):
    chans, size, _ = kernel.shape
    planes = kernel.transpose(1, 2, 0).reshape(size * size, chans)
    planes = planes.at[(size * size) // 2].add(1.0)
    return jnp.broadcast_to(planes[:, :, None], (size * size, chans, 128))


def local(fields, depth_kernel, mix_weight, legendre, truth, degree_order):
    ens_parts, groups = lax.axis_size("ens"), lax.axis_size("lat")
    ens_at, lat_at = lax.axis_index("ens"), lax.axis_index("lat")
    members, chans, rows, nlon = fields.shape
    _, orders, degrees = legendre.shape
    ens = members * ens_parts
    nlat = rows * groups
    share, per_owner, chan_share = orders // groups, degrees // groups, chans // ens_parts
    order_pad = up(share, 8)
    slots = up(2 * chan_share, 8)
    lanes = up(rows * members * slots, 128)
    wide = up(nlon + 2 * LEAD, 128)
    halo = depth_kernel.shape[1] // 2

    table = jnp.asarray(wave_table(nlon, orders, groups, order_pad))
    own = fields.transpose(0, 2, 1, 3)
    low, high = neighbours(own, halo)

    picked = mix_weight.reshape(ens_parts, chan_share, chans)
    slotted = jnp.stack(
        [
            jnp.pad(picked, ((0, 0), (r * chan_share, slots - (r + 1) * chan_share), (0, 0)))
            for r in range(2)
        ]
    )
    same_row = jnp.asarray(np.eye(rows), BF16)
    same_member = jnp.asarray(np.eye(members), BF16)
    mixer = jnp.einsum("reoc,ij,bd->rbicejdo", slotted, same_row, same_member)
    mixer = mixer.reshape(2, members * rows * chans, ens_parts, rows * members * slots)
    mixer = jnp.pad(mixer, ((0, 0), (0, 0), (0, 0), (0, lanes - rows * members * slots)))
    mixer = mixer.reshape(2, members * rows * chans, ens_parts * lanes).astype(BF16)

    order_legendre = lax.all_to_all(legendre, "lat", split_axis=1, concat_axis=0, tiled=True)
    order_legendre = order_legendre.transpose(1, 0, 2)
    target = lax.dynamic_slice(
        truth, (ens_at * chan_share, 0, lat_at * share, 0), (chan_share, 2, share, degrees)
    )
    target = target.transpose(2, 1, 0, 3).reshape(share, 2 * chan_share, degrees)
    target = jnp.pad(target, ((0, 0), (0, slots - 2 * chan_share), (0, 0)))
    reorder = (jnp.arange(degrees)[:, None] == degree_order[None, :]).astype(BF16)

    vmem = pltpu.CompilerParams(vmem_limit_bytes=60 * 1024 * 1024)
    grid_shape = (members, rows, chans, nlon)
    chunk = jax.ShapeDtypeStruct((ens_parts, groups, order_pad, lanes), BF16)
    sent, slope = pl.pallas_call(
        forward_kernel,
        out_shape=(chunk, jax.ShapeDtypeStruct(grid_shape, F32)),
        scratch_shapes=[
            pltpu.VMEM((rows + 2 * halo, chans, wide), F32),
            pltpu.VMEM(grid_shape, F32),
        ],
        compiler_params=vmem,
        name="forward",
    )(own, low, high, tap_planes(depth_kernel), table, mixer)

    def swap(x):
        flat = x.reshape((ens_parts * groups,) + x.shape[2:])
        flat = lax.all_to_all(flat, ("ens", "lat"), split_axis=0, concat_axis=0, tiled=True)
        return flat.reshape(x.shape)

    got = swap(sent)
    back, grads = pl.pallas_call(
        functools.partial(score_kernel, rows),
        out_shape=(chunk, jax.ShapeDtypeStruct((share, ens * slots, degrees), BF16)),
        scratch_shapes=[
            pltpu.VMEM((nlat * order_pad, ens * slots), F32),
            pltpu.VMEM((nlat * order_pad, ens * slots), F32),
        ],
        compiler_params=vmem,
        name="score",
    )(got, order_legendre, target, reorder)
    returned = swap(back)

    hid_grad = pl.pallas_call(
        backward_kernel,
        out_shape=jax.ShapeDtypeStruct(grid_shape, BF16),
        scratch_shapes=[pltpu.VMEM(grid_shape, F32)],
        compiler_params=vmem,
        name="backward",
    )(returned, mixer, table, slope)
    low, high = neighbours(hid_grad, halo)
    grad_fields = pl.pallas_call(
        convolve_kernel,
        out_shape=jax.ShapeDtypeStruct(grid_shape, BF16),
        scratch_shapes=[
            pltpu.VMEM((rows + 2 * halo, chans, wide), F32),
            pltpu.VMEM(grid_shape, F32),
        ],
        compiler_params=vmem,
        name="convolve",
    )(hid_grad, low, high, tap_planes(depth_kernel[:, ::-1, ::-1]))

    grads = grads.reshape(share, ens_parts, members, slots, groups, per_owner)
    grads = grads[:, :, :, : 2 * chan_share].transpose(1, 4, 2, 0, 3, 5)
    grads = grads.reshape(ens_parts, groups, members * share, 2 * chan_share * per_owner)
    grads = swap(grads).reshape(
        ens_parts, groups, members, share, 2, chan_share, per_owner
    )
    score_grad = grads.transpose(2, 0, 5, 4, 1, 3, 6).reshape(
        members, chans, 2, orders, per_owner
    )
    return grad_fields.transpose(0, 2, 1, 3), score_grad.astype(F32)


def solution(mesh):
    placed = (P("ens", None, "lat", None), P(), P(), P("lat", None, None), P(), P())
    return jax.shard_map(
        local,
        mesh=mesh,
        in_specs=placed,
        out_specs=(P("ens", None, "lat", None), P("ens", None, None, None, "lat")),
        check_vma=False,
    )
```

```python
import functools
import math

import jax
import jax.numpy as jnp
import numpy as np
from jax import lax
from jax.experimental import pallas as pl
from jax.experimental.pallas import tpu as pltpu
from jax.sharding import PartitionSpec as P

smooth_width = 0.5
LEAD = 8
F32 = jnp.float32
BF16 = jnp.bfloat16


def up(value, step):
    return -(-value // step) * step


def full(shape):
    return pl.BlockSpec(shape, lambda *_: (0,) * len(shape), memory_space=pltpu.VMEM)


def wave_table(nlon, orders, groups, order_pad):
    share = orders // groups
    columns = np.arange(nlon, dtype=np.int64)
    number = np.arange(orders, dtype=np.int64)
    angles = (columns[:, None] * number[None, :] % nlon) * (2.0 * math.pi / nlon)
    table = np.zeros((nlon, 2, groups, order_pad), np.float32)
    for part, values in enumerate((np.cos(angles), -np.sin(angles))):
        table[:, part, :, :share] = (values / math.sqrt(nlon)).reshape(nlon, groups, share)
    return table.reshape(nlon, 2 * groups * order_pad).astype(jnp.bfloat16)


def edges(block, width):
    odd = lax.axis_index("lat") % 2
    last = block.shape[1] - width
    count = lax.axis_size("lat")
    near = [(i, i ^ 1) for i in range(count)]
    far = [(i, (i + (1 if i % 2 else -1)) % count) for i in range(count)]
    inner = lax.dynamic_slice_in_dim(block, (1 - odd) * last, width, 1)
    outer = lax.dynamic_slice_in_dim(block, odd * last, width, 1)
    return lax.ppermute(inner, "lat", near), lax.ppermute(outer, "lat", far)


def place():
    at, count = lax.axis_index("lat"), lax.axis_size("lat")
    return jnp.stack([at % 2, at > 0, at < count - 1]).astype(jnp.int32)


def fill_row(padded, row, value):
    nlon, wide = value.shape[-1], padded.shape[-1]
    padded[row] = jnp.concatenate(
        [value[:, nlon - LEAD :], value, value[:, : wide - nlon - LEAD]], axis=-1
    )


def tap_sum(padded, taps, c0, lines, size):
    wide = padded.shape[-1]
    total = None
    for q in range(size):
        part = None
        for row, p in lines:
            weight = jnp.tile(taps[p * size + q, pl.ds(c0, 8), :], (1, wide // 128))
            term = weight * padded[row, pl.ds(c0, 8), :]
            part = term if part is None else part + term
        shift = (size // 2 - q) % wide
        if shift:
            part = pltpu.roll(part, shift, 1)
        total = part if total is None else total + part
    return total


def spread_taps(kernel, taps, flip):
    size, _, chans = kernel.shape
    for p in range(size):
        plane = kernel[p].T
        for q in range(size):
            value = plane[:, q : q + 1]
            if p == q == size // 2:
                value = value + 1.0
            at = p * size + q
            at = size * size - 1 - at if flip else at
            taps[at] = jnp.broadcast_to(value, (chans, 128))


def own_part(own, taps, partial, padded, size):
    members, rows, chans, nlon = own.shape
    half = size // 2

    @pl.loop(0, members)
    def _(b):
        for row in range(rows):
            fill_row(padded, row, own[b, row].astype(F32))

        @pl.loop(0, chans // 8)
        def _(ct):
            c0 = pl.multiple_of(ct * 8, 8)
            for i in range(rows):
                lines = [(i + p - half, p) for p in range(size) if 0 <= i + p - half < rows]
                total = tap_sum(padded, taps, c0, lines, size)
                partial[b, i, pl.ds(c0, 8), :] = total[:, LEAD : LEAD + nlon]


def halo_part(flags, near, far, taps, partial, padded, size, emit):
    members, rows, chans, nlon = partial.shape
    half = size // 2
    odd, below, above = flags[0] == 1, flags[1] == 1, flags[2] == 1

    @pl.loop(0, members)
    def _(b):
        for row in range(half):
            one, other = near[b, row].astype(F32), far[b, row].astype(F32)
            zero = jnp.zeros_like(one)
            fill_row(padded, row, jnp.where(below, jnp.where(odd, one, other), zero))
            fill_row(padded, half + row, jnp.where(above, jnp.where(odd, other, one), zero))

        @pl.loop(0, chans // 8)
        def _(ct):
            c0 = pl.multiple_of(ct * 8, 8)
            for i in range(rows):
                lines = []
                for p in range(size):
                    at = i + p - half
                    if at < 0:
                        lines.append((at + half, p))
                    elif at >= rows:
                        lines.append((at - rows + half, p))
                value = partial[b, i, pl.ds(c0, 8), :]
                if lines:
                    total = tap_sum(padded, taps, c0, lines, size)
                    value = value + total[:, LEAD : LEAD + nlon]
                emit(b, i, c0, value)


def gelu_pair(x):
    scale = math.sqrt(2.0 / math.pi)
    square = x * x
    t = jnp.tanh(scale * x * (1.0 + 0.044715 * square))
    half = 0.5 * (1.0 + t)
    slope = half + 0.5 * x * (1.0 - t * t) * (scale * (1.0 + 3 * 0.044715 * square))
    return x * half, slope


def prepare_kernel(owners, own, kernel, weight, pick, partial, taps, mixer, padded):
    members, rows, chans, nlon = own.shape
    size = kernel.shape[0]
    spread_taps(kernel, taps, False)
    own_part(own, taps, partial, padded, size)
    lanes = mixer.shape[2] // owners
    slots = pick.shape[2] // owners
    span = owners * slots
    across = members * rows * chans
    lane = lax.broadcasted_iota(jnp.int32, (chans, mixer.shape[2]), 1)
    within = lane % lanes
    for r in range(2):
        table = lax.dot_general(
            weight[...], pick[r], (((0,), (0,)), ((), ())), preferred_element_type=F32
        )
        wide = jnp.concatenate(
            [jnp.tile(table[:, e * slots : (e + 1) * slots], (1, lanes // slots)) for e in range(owners)],
            axis=1,
        )
        for b in range(members):
            for i in range(rows):
                kept = (within // slots) == i * members + b
                at = (b * rows + i) * chans
                mixer[r, at : at + chans, :] = jnp.where(kept, wide, 0.0).astype(BF16)


def forward_kernel(flags, near, far, partial, taps, table, mixer, out, slope, padded, act):
    members, rows, chans, nlon = partial.shape
    owners, groups, order_pad, lanes = out.shape
    size = math.isqrt(taps.shape[0])

    def emit(b, i, c0, value):
        value, grad = gelu_pair(value)
        act[b, i, pl.ds(c0, 8), :] = value
        slope[b, i, pl.ds(c0, 8), :] = grad

    halo_part(flags, near, far, taps, partial, padded, size, emit)
    flat = act[...].reshape(members * rows * chans, nlon).astype(BF16)
    spectral = jnp.dot(flat, table[...], preferred_element_type=F32).astype(BF16)
    half = groups * order_pad
    mixed = None
    for r in range(2):
        part = lax.dot_general(
            spectral[:, r * half : (r + 1) * half],
            mixer[r],
            (((0,), (0,)), ((), ())),
            preferred_element_type=F32,
        )
        mixed = part if mixed is None else mixed + part
    for e in range(owners):
        out[e] = mixed[:, e * lanes : (e + 1) * lanes].reshape(groups, order_pad, lanes).astype(BF16)


def soft_sign(gaps):
    return gaps * lax.rsqrt(gaps * gaps + smooth_width * smooth_width)


def score_kernel(rows, got, legendre, target, order, back, grads, spread, gather):
    owners, groups, order_pad, lanes = got.shape
    orders, nlat, degrees = legendre.shape
    slots = target.shape[1]
    ens = spread.shape[1] // slots
    local = ens // owners
    width = local * slots
    for t in range(groups):
        for i in range(rows):
            pieces = [got[e, t, :, i * width : (i + 1) * width] for e in range(owners)]
            at = (t * rows + i) * order_pad
            spread[at : at + order_pad, :] = jnp.concatenate(pieces, axis=-1).astype(F32)
    gather[...] = jnp.zeros(gather.shape, F32)

    @pl.loop(0, orders)
    def _(m):
        block = spread[pl.ds(m, nlat, stride=order_pad), :].astype(BF16)
        leg = legendre[m]
        coeff = lax.dot_general(
            block, leg, (((0,), (0,)), ((), ())), preferred_element_type=F32
        )
        own = [coeff[k * slots : (k + 1) * slots] for k in range(ens)]
        truth = target[m].astype(F32)
        sums = [None] * ens
        for k in range(ens):
            for n in range(k + 1, ens):
                sign = soft_sign(own[k] - own[n])
                sums[k] = sign if sums[k] is None else sums[k] + sign
                sums[n] = -sign if sums[n] is None else sums[n] - sign
        grad = jnp.concatenate(
            [
                soft_sign(own[k] - truth) * (1.0 / ens) - sums[k] * (1.0 / (ens * (ens - 1)))
                for k in range(ens)
            ],
            axis=0,
        ).astype(BF16)
        spec = lax.dot_general(
            leg, grad, (((1,), (1,)), ((), ())), preferred_element_type=F32
        )
        gather[pl.ds(m, nlat, stride=order_pad), :] = spec
        at = pl.multiple_of(m * ens * slots, 8)
        ordered = jnp.dot(grad, order[...], preferred_element_type=F32)
        for j in range(grads.shape[0]):
            last = min(degrees, (j + 1) * 128)
            grads[j, pl.ds(at, ens * slots), : last - j * 128] = ordered[:, j * 128 : last]

    for t in range(groups):
        for e in range(owners):
            pieces = []
            for i in range(rows):
                at = (t * rows + i) * order_pad
                pieces.append(gather[at : at + order_pad, e * width : (e + 1) * width])
            if lanes > rows * width:
                pieces.append(jnp.zeros((order_pad, lanes - rows * width), F32))
            back[e, t] = jnp.concatenate(pieces, axis=-1).astype(BF16)


def backward_kernel(got, mixer, table, slope, out, flat):
    owners, groups, order_pad, lanes = got.shape
    members, rows, chans, nlon = slope.shape
    half = groups * order_pad
    spectra = jnp.concatenate(
        [got[e].reshape(half, lanes) for e in range(owners)], axis=-1
    )
    parts = []
    for r in range(2):
        parts.append(
            lax.dot_general(
                mixer[r], spectra, (((1,), (1,)), ((), ())), preferred_element_type=F32
            ).astype(BF16)
        )
    unmixed = jnp.concatenate(parts, axis=-1)
    flat[...] = lax.dot_general(
        unmixed, table[...], (((1,), (1,)), ((), ())), preferred_element_type=F32
    ).reshape(flat.shape)
    for b in range(members):
        for i in range(rows):
            out[b, i] = (flat[b, i] * slope[b, i]).astype(BF16)


def own_kernel(own, kernel, partial, taps, padded):
    spread_taps(kernel, taps, True)
    own_part(own, taps, partial, padded, kernel.shape[0])


def halo_kernel(flags, near, far, partial, taps, out, padded, stage):
    def emit(b, i, c0, value):
        stage[b, i, pl.ds(c0, 8), :] = value

    halo_part(flags, near, far, taps, partial, padded, math.isqrt(taps.shape[0]), emit)
    out[...] = stage[...].astype(BF16)


def pack_kernel(members, used, per_owner, grads, out):
    owners, groups, depth, lanes = out.shape
    share = depth // members
    stride = grads.shape[1] // share
    slots = stride // (owners * members)
    for e in range(owners):
        for b in range(members):
            at = (e * members + b) * slots
            planes = [
                jnp.concatenate(
                    [grads[j, pl.ds(at + s, share, stride=stride), :] for j in range(grads.shape[0])],
                    axis=1,
                )
                for s in range(used)
            ]
            for t in range(groups):
                pieces = [x[:, t * per_owner : (t + 1) * per_owner] for x in planes]
                if lanes > used * per_owner:
                    pieces.append(jnp.zeros((share, lanes - used * per_owner), F32))
                out[e, t, b * share : (b + 1) * share, :] = jnp.concatenate(pieces, axis=1).astype(BF16)


def unpack_kernel(members, got, out):
    owners, groups, depth, lanes = got.shape
    _, chans, per_owner, _, orders = out.shape
    share, chan_share = depth // members, chans // owners
    row = lax.broadcasted_iota(jnp.int32, (groups * depth, orders), 0)
    column = lax.broadcasted_iota(jnp.int32, (groups * depth, orders), 1)
    for b in range(members):
        wanted = (column // share) * depth + b * share + column % share
        picker = jnp.where(row == wanted, 1.0, 0.0).astype(BF16)
        for e in range(owners):
            block = lax.dot_general(
                got[e].reshape(groups * depth, lanes),
                picker,
                (((0,), (0,)), ((), ())),
                preferred_element_type=F32,
            )
            for c in range(chan_share):
                for r in range(2):
                    at = (r * chan_share + c) * per_owner
                    out[b, e * chan_share + c, :, r, :] = block[at : at + per_owner]


def local(fields, depth_kernel, mix_weight, legendre, truth, degree_order):
    ens_parts, groups = lax.axis_size("ens"), lax.axis_size("lat")
    ens_at, lat_at = lax.axis_index("ens"), lax.axis_index("lat")
    members, chans, rows, nlon = fields.shape
    _, orders, degrees = legendre.shape
    ens = members * ens_parts
    nlat = rows * groups
    share, per_owner, chan_share = orders // groups, degrees // groups, chans // ens_parts
    order_pad = up(share, 8)
    slots = up(2 * chan_share, 8)
    lanes = up(rows * members * slots, 128)
    wide = up(nlon + 2 * LEAD, 128)
    size = depth_kernel.shape[1]
    halo = size // 2
    used = 2 * chan_share

    table = jnp.asarray(wave_table(nlon, orders, groups, order_pad))
    kernel = depth_kernel.transpose(1, 2, 0)
    flags = place()
    own = fields.transpose(0, 2, 1, 3)
    with jax.named_scope("first"):
        near, far = edges(own, halo)

    pick = np.zeros((2, chans, ens_parts, slots), np.float32)
    for r in range(2):
        for o in range(chans):
            pick[r, o, o // chan_share, r * chan_share + o % chan_share] = 1.0
    pick = jnp.asarray(pick.reshape(2, chans, ens_parts * slots).astype(jnp.bfloat16))

    with jax.named_scope("orders"):
        order_legendre = lax.all_to_all(legendre, "lat", split_axis=1, concat_axis=0, tiled=True)
    order_legendre = order_legendre.transpose(1, 0, 2)
    target = lax.dynamic_slice(
        truth, (ens_at * chan_share, 0, lat_at * share, 0), (chan_share, 2, share, degrees)
    )
    target = target.transpose(2, 1, 0, 3).reshape(share, used, degrees)
    target = jnp.pad(target, ((0, 0), (0, slots - used), (0, 0)))
    reorder = (jnp.arange(degrees)[:, None] == degree_order[None, :]).astype(BF16)

    vmem = pltpu.CompilerParams(vmem_limit_bytes=60 * 1024 * 1024)
    scalars = pl.BlockSpec(memory_space=pltpu.SMEM)
    whole = pl.BlockSpec(memory_space=pltpu.VMEM)
    grid_shape = (members, rows, chans, nlon)
    count = members * rows * chans
    chunk = jax.ShapeDtypeStruct((ens_parts, groups, order_pad, lanes), BF16)
    partial_out = jax.ShapeDtypeStruct(grid_shape, F32)
    taps_out = jax.ShapeDtypeStruct((size * size, chans, 128), F32)
    own_rows = pltpu.VMEM((rows, chans, wide), F32)
    halo_rows = pltpu.VMEM((2 * halo, chans, wide), F32)

    def call(body, outs, scratch, name, work, *args):
        specs = [scalars if a is flags else whole for a in args]
        return pl.pallas_call(
            body,
            out_shape=outs,
            in_specs=specs,
            scratch_shapes=scratch,
            compiler_params=vmem,
            cost_estimate=pl.CostEstimate(
                flops=work, transcendentals=0, bytes_accessed=8 * count * nlon
            ),
            name=name,
        )(*args)

    work = 2 * size * size * count * nlon
    partial, taps, mixer = call(
        functools.partial(prepare_kernel, ens_parts),
        (partial_out, taps_out, jax.ShapeDtypeStruct((2, count, ens_parts * lanes), BF16)),
        [own_rows],
        "prepare",
        work,
        own,
        kernel,
        mix_weight,
        pick,
    )
    sent, slope = call(
        forward_kernel,
        (chunk, partial_out),
        [halo_rows, pltpu.VMEM(grid_shape, F32)],
        "forward",
        work,
        flags,
        near,
        far,
        partial,
        taps,
        table,
        mixer,
    )

    def swap(x):
        flat = x.reshape((ens_parts * groups,) + x.shape[2:])
        flat = lax.all_to_all(flat, ("ens", "lat"), split_axis=0, concat_axis=0, tiled=True)
        return flat.reshape(x.shape)

    got = swap(sent)
    spread = pltpu.VMEM((nlat * order_pad, ens * slots), F32)
    back, grads = call(
        functools.partial(score_kernel, rows),
        (chunk, jax.ShapeDtypeStruct((up(degrees, 128) // 128, share * ens * slots, 128), F32)),
        [spread, spread],
        "score",
        work,
        got,
        order_legendre,
        target,
        reorder,
    )
    returned = swap(back)
    packed = call(
        functools.partial(pack_kernel, members, used, per_owner),
        jax.ShapeDtypeStruct(
            (ens_parts, groups, members * share, up(used * per_owner, 128)), BF16
        ),
        [],
        "pack",
        work,
        grads,
    )
    owned = swap(packed)

    hid_grad = call(
        backward_kernel,
        jax.ShapeDtypeStruct(grid_shape, BF16),
        [pltpu.VMEM(grid_shape, F32)],
        "backward",
        work,
        returned,
        mixer,
        table,
        slope,
    )
    near, far = edges(hid_grad, halo)
    partial, taps = call(
        own_kernel, (partial_out, taps_out), [own_rows], "own", work, hid_grad, kernel
    )
    score_grad = call(
        functools.partial(unpack_kernel, members),
        jax.ShapeDtypeStruct((members, chans, per_owner, 2, orders), F32),
        [],
        "unpack",
        work,
        owned,
    )
    grad_fields = call(
        halo_kernel,
        jax.ShapeDtypeStruct(grid_shape, BF16),
        [halo_rows, pltpu.VMEM(grid_shape, F32)],
        "halo",
        work,
        flags,
        near,
        far,
        partial,
        taps,
    )
    return grad_fields.transpose(0, 2, 1, 3), score_grad.transpose(0, 1, 3, 4, 2)


def solution(mesh):
    placed = (P("ens", None, "lat", None), P(), P(), P("lat", None, None), P(), P())
    return jax.shard_map(
        local,
        mesh=mesh,
        in_specs=placed,
        out_specs=(P("ens", None, "lat", None), P("ens", None, None, None, "lat")),
        check_vma=False,
    )
```

```python
import functools
import math

import jax
import jax.numpy as jnp
import numpy as np
from jax import lax
from jax.experimental import pallas as pl
from jax.experimental.pallas import tpu as pltpu
from jax.sharding import PartitionSpec as P

smooth_width = 0.5
LEAD = 8
F32 = jnp.float32
BF16 = jnp.bfloat16


def up(value, step):
    return -(-value // step) * step


def full(shape):
    return pl.BlockSpec(shape, lambda *_: (0,) * len(shape), memory_space=pltpu.VMEM)


def wave_table(nlon, orders, span):
    columns = np.arange(nlon, dtype=np.int64)
    number = np.arange(orders, dtype=np.int64)
    angles = (columns[:, None] * number[None, :] % nlon) * (2.0 * math.pi / nlon)
    table = np.zeros((nlon, 2, span), np.float32)
    for part, values in enumerate((np.cos(angles), -np.sin(angles))):
        table[:, part, :orders] = values / math.sqrt(nlon)
    return table.reshape(nlon, 2 * span).astype(jnp.bfloat16)


def partners(inner, outer):
    count = lax.axis_size("lat")
    near = [(i, i ^ 1) for i in range(count)]
    far = [(i, (i + (1 if i % 2 else -1)) % count) for i in range(count)]
    return lax.ppermute(inner, "lat", near), lax.ppermute(outer, "lat", far)


def place():
    at, count = lax.axis_index("lat"), lax.axis_size("lat")
    return jnp.stack([at % 2, at > 0, at < count - 1]).astype(jnp.int32)


def fill_row(padded, row, value):
    nlon, wide = value.shape[-1], padded.shape[-1]
    padded[row] = jnp.concatenate(
        [value[:, nlon - LEAD :], value, value[:, : wide - nlon - LEAD]], axis=-1
    )


def tap_sum(padded, taps, c0, lines, size):
    wide = padded.shape[-1]
    total = None
    for q in range(size):
        part = None
        for row, p in lines:
            weight = jnp.tile(taps[p * size + q, pl.ds(c0, 8), :], (1, wide // 128))
            term = weight * padded[row, pl.ds(c0, 8), :]
            part = term if part is None else part + term
        shift = (size // 2 - q) % wide
        if shift:
            part = pltpu.roll(part, shift, 1)
        total = part if total is None else total + part
    return total


def spread_taps(kernel, taps, flip):
    size, _, chans = kernel.shape
    for p in range(size):
        plane = kernel[p].T
        for q in range(size):
            value = plane[:, q : q + 1]
            if p == q == size // 2:
                value = value + 1.0
            at = p * size + q
            at = size * size - 1 - at if flip else at
            value = jnp.broadcast_to(value, (chans, 128))
            taps[at] = jnp.concatenate([value] * (taps.shape[1] // chans), axis=0)


def own_part(taps, partial, padded, size):
    rows, depth, nlon = partial.shape
    half = size // 2

    @pl.loop(0, depth // 8)
    def _(ct):
        c0 = pl.multiple_of(ct * 8, 8)
        for i in range(rows):
            lines = [(i + p - half, p) for p in range(size) if 0 <= i + p - half < rows]
            total = tap_sum(padded, taps, c0, lines, size)
            partial[i, pl.ds(c0, 8), :] = total[:, LEAD : LEAD + nlon]


def halo_part(flags, near, far, taps, partial, padded, size, emit):
    rows, depth, nlon = partial.shape
    half = size // 2
    odd, below, above = flags[0] == 1, flags[1] == 1, flags[2] == 1
    for row in range(half):
        one, other = joined(near, row), joined(far, row)
        zero = jnp.zeros_like(one)
        fill_row(padded, row, jnp.where(below, jnp.where(odd, one, other), zero))
        fill_row(padded, half + row, jnp.where(above, jnp.where(odd, other, one), zero))

    @pl.loop(0, depth // 8)
    def _(ct):
        c0 = pl.multiple_of(ct * 8, 8)
        for i in range(rows):
            lines = []
            for p in range(size):
                at = i + p - half
                if at < 0:
                    lines.append((at + half, p))
                elif at >= rows:
                    lines.append((at - rows + half, p))
            value = partial[i, pl.ds(c0, 8), :]
            if lines:
                total = tap_sum(padded, taps, c0, lines, size)
                value = value + total[:, LEAD : LEAD + nlon]
            emit(i, c0, value)


def joined(block, row):
    return jnp.concatenate([block[b, row].astype(F32) for b in range(block.shape[0])], axis=0)


def gelu_pair(x):
    scale = math.sqrt(2.0 / math.pi)
    square = x * x
    t = jnp.tanh(scale * x * (1.0 + 0.044715 * square))
    half = 0.5 * (1.0 + t)
    slope = half + 0.5 * x * (1.0 - t * t) * (scale * (1.0 + 3 * 0.044715 * square))
    return x * half, slope


def prepare_kernel(own, kernel, weight, pick, partial, taps, mixer, padded):
    members, rows, chans, nlon = own.shape
    size = kernel.shape[0]
    spread_taps(kernel, taps, False)
    for row in range(rows):
        fill_row(padded, row, joined(own, row))
    own_part(taps, partial, padded, size)
    for r in range(2):
        lines = []
        for b in range(members):
            lines.append(jnp.dot(pick[r, b], weight[...], preferred_element_type=F32))
        mixer[r] = jnp.concatenate(lines, axis=1).astype(BF16)


def forward_kernel(share, flags, near, far, partial, taps, table, mixer, out, slope, inner, outer, padded, act):
    rows, depth, nlon = partial.shape
    owners, groups, height, lanes = out.shape
    members, width, chans, _ = inner.shape
    size = math.isqrt(taps.shape[0])
    span = table.shape[1] // 2

    def emit(i, c0, value):
        value, grad = gelu_pair(value)
        act[i, pl.ds(c0, 8), :] = value
        slope[i, pl.ds(c0, 8), :] = grad

    halo_part(flags, near, far, taps, partial, padded, size, emit)
    odd = flags[0] == 1
    for row in range(width):
        first, last = slope[row], slope[rows - width + row]
        ours, theirs = jnp.where(odd, first, last), jnp.where(odd, last, first)
        for b in range(members):
            inner[b, row] = ours[b * chans : (b + 1) * chans].astype(BF16)
            outer[b, row] = theirs[b * chans : (b + 1) * chans].astype(BF16)
    flat = act[...].reshape(rows * depth, nlon).astype(BF16)
    spectral = jnp.dot(flat, table[...], preferred_element_type=F32).astype(BF16)
    mixed = []
    for i in range(rows):
        line = spectral[i * depth : (i + 1) * depth]
        mixed.append(
            jnp.dot(mixer[0], line[:, :span], preferred_element_type=F32)
            + jnp.dot(mixer[1], line[:, span:], preferred_element_type=F32)
        )
    for t in range(groups):
        pieces = [x[:, t * share : (t + 1) * share] for x in mixed]
        if lanes > rows * share:
            pieces.append(jnp.zeros((owners * height, lanes - rows * share), F32))
        block = jnp.concatenate(pieces, axis=1)
        for e in range(owners):
            out[e, t] = block[e * height : (e + 1) * height].astype(BF16)


def soft_sign(gaps):
    return gaps * lax.rsqrt(gaps * gaps + smooth_width * smooth_width)


def score_kernel(members, used, rows, halo, got, legendre, target, order, back, grads, spread, gather):
    owners, groups, height, lanes = got.shape
    orders, nlat, degrees = legendre.shape
    slots = target.shape[1]
    ens = owners * members
    for t in range(groups):
        pieces = []
        for e in range(owners):
            block = got[e, t].astype(F32)
            for b in range(members):
                pieces.append(block[b * used : (b + 1) * used])
                if slots > used:
                    pieces.append(jnp.zeros((slots - used, lanes), F32))
        block = jnp.concatenate(pieces, axis=0).T
        at = t * rows * orders
        spread[at : at + rows * orders, :] = block[: rows * orders]
    edge = halo * orders
    gather[:edge, :] = jnp.zeros((edge, ens * slots), F32)
    gather[edge + nlat * orders :, :] = jnp.zeros((edge, ens * slots), F32)

    @pl.loop(0, orders)
    def _(m):
        block = spread[pl.ds(m, nlat, stride=orders), :].astype(BF16)
        leg = legendre[m]
        coeff = lax.dot_general(
            block, leg, (((0,), (0,)), ((), ())), preferred_element_type=F32
        )
        own = [coeff[k * slots : (k + 1) * slots] for k in range(ens)]
        truth = target[m].astype(F32)
        sums = [None] * ens
        for k in range(ens):
            for n in range(k + 1, ens):
                sign = soft_sign(own[k] - own[n])
                sums[k] = sign if sums[k] is None else sums[k] + sign
                sums[n] = -sign if sums[n] is None else sums[n] - sign
        grad = jnp.concatenate(
            [
                soft_sign(own[k] - truth) * (1.0 / ens) - sums[k] * (1.0 / (ens * (ens - 1)))
                for k in range(ens)
            ],
            axis=0,
        ).astype(BF16)
        spec = lax.dot_general(
            leg, grad, (((1,), (1,)), ((), ())), preferred_element_type=F32
        )
        gather[pl.ds(edge + m, nlat, stride=orders), :] = spec
        at = pl.multiple_of(m * ens * slots, 8)
        ordered = jnp.dot(grad, order[...], preferred_element_type=F32)
        for j in range(grads.shape[0]):
            last = min(degrees, (j + 1) * 128)
            grads[j, pl.ds(at, ens * slots), : last - j * 128] = ordered[:, j * 128 : last]

    wide = back.shape[3]
    tall = (rows + 2 * halo) * orders
    for t in range(groups):
        at = t * rows * orders
        block = gather[at : at + tall, :]
        if wide > tall:
            block = jnp.concatenate([block, jnp.zeros((wide - tall, ens * slots), F32)], axis=0)
        block = block.T
        for e in range(owners):
            pieces = []
            for b in range(members):
                at = (e * members + b) * slots
                pieces.append(block[at : at + used])
            if height > members * used:
                pieces.append(jnp.zeros((height - members * used, wide), F32))
            back[e, t] = jnp.concatenate(pieces, axis=0).astype(BF16)


def backward_kernel(share, flags, got, near, far, kernel, mixer, table, slope, out, padded, taps, flat, stage):
    owners, groups, height, lanes = got.shape
    rows, depth, nlon = slope.shape
    members, _, chans, _ = out.shape
    size = kernel.shape[0]
    half = size // 2
    span = table.shape[1] // 2
    total = rows + 2 * half
    spread_taps(kernel, taps, True)
    blocks = [
        jnp.concatenate([got[e, t].astype(F32) for e in range(owners)], axis=0) for t in range(groups)
    ]
    lines = []
    for i in range(total):
        pieces = [x[:, i * share : (i + 1) * share] for x in blocks]
        pieces.append(jnp.zeros((owners * height, span - groups * share), F32))
        line = jnp.concatenate(pieces, axis=1).astype(BF16)
        lines.append(
            jnp.concatenate(
                [
                    lax.dot_general(
                        mixer[r], line, (((0,), (0,)), ((), ())), preferred_element_type=F32
                    ).astype(BF16)
                    for r in range(2)
                ],
                axis=1,
            )
        )
    flat[...] = lax.dot_general(
        jnp.concatenate(lines, axis=0),
        table[...],
        (((1,), (1,)), ((), ())),
        preferred_element_type=F32,
    ).reshape(flat.shape)
    odd = flags[0] == 1
    for row in range(half):
        one, other = joined(near, row), joined(far, row)
        fill_row(padded, row, flat[row] * jnp.where(odd, one, other))
        at = half + rows + row
        fill_row(padded, at, flat[at] * jnp.where(odd, other, one))
    for row in range(rows):
        fill_row(padded, half + row, flat[half + row] * slope[row])

    @pl.loop(0, depth // 8)
    def _(ct):
        c0 = pl.multiple_of(ct * 8, 8)

        @pl.loop(0, rows)
        def _(i):
            value = tap_sum(padded, taps, c0, [(i + p, p) for p in range(size)], size)
            stage[i, pl.ds(c0, 8), :] = value[:, LEAD : LEAD + nlon]

    for b in range(members):
        for i in range(rows):
            out[b, i] = stage[i, b * chans : (b + 1) * chans, :].astype(BF16)


def pack_kernel(members, used, per_owner, grads, out):
    owners, groups, depth, lanes = out.shape
    share = depth // members
    stride = grads.shape[1] // share
    slots = stride // (owners * members)
    for e in range(owners):
        for b in range(members):
            at = (e * members + b) * slots
            planes = [
                jnp.concatenate(
                    [grads[j, pl.ds(at + s, share, stride=stride), :] for j in range(grads.shape[0])],
                    axis=1,
                )
                for s in range(used)
            ]
            for t in range(groups):
                pieces = [x[:, t * per_owner : (t + 1) * per_owner] for x in planes]
                if lanes > used * per_owner:
                    pieces.append(jnp.zeros((share, lanes - used * per_owner), F32))
                out[e, t, b * share : (b + 1) * share, :] = jnp.concatenate(pieces, axis=1).astype(BF16)


def unpack_kernel(members, got, out):
    owners, groups, depth, lanes = got.shape
    _, chans, per_owner, _, orders = out.shape
    share, chan_share = depth // members, chans // owners
    row = lax.broadcasted_iota(jnp.int32, (groups * depth, orders), 0)
    column = lax.broadcasted_iota(jnp.int32, (groups * depth, orders), 1)
    for b in range(members):
        wanted = (column // share) * depth + b * share + column % share
        picker = jnp.where(row == wanted, 1.0, 0.0).astype(BF16)
        for e in range(owners):
            block = lax.dot_general(
                got[e].reshape(groups * depth, lanes),
                picker,
                (((0,), (0,)), ((), ())),
                preferred_element_type=F32,
            )
            for c in range(chan_share):
                for r in range(2):
                    at = (r * chan_share + c) * per_owner
                    out[b, e * chan_share + c, :, r, :] = block[at : at + per_owner]


def local(fields, depth_kernel, mix_weight, legendre, truth, degree_order):
    ens_parts, groups = lax.axis_size("ens"), lax.axis_size("lat")
    ens_at, lat_at = lax.axis_index("ens"), lax.axis_index("lat")
    members, chans, rows, nlon = fields.shape
    _, orders, degrees = legendre.shape
    ens = members * ens_parts
    nlat = rows * groups
    share, per_owner, chan_share = orders // groups, degrees // groups, chans // ens_parts
    used = 2 * chan_share
    slots = up(used, 8)
    height = up(members * used, 8)
    wide = up(nlon + 2 * LEAD, 128)
    span = up(orders, 128)
    size = depth_kernel.shape[1]
    halo = size // 2
    depth = members * chans

    table = jnp.asarray(wave_table(nlon, orders, span))
    kernel = depth_kernel.transpose(1, 2, 0)
    flags = place()
    own = fields.transpose(0, 2, 1, 3)
    odd = lat_at % 2
    near, far = partners(
        lax.dynamic_slice_in_dim(own, (1 - odd) * (rows - halo), halo, 1),
        lax.dynamic_slice_in_dim(own, odd * (rows - halo), halo, 1),
    )

    pick = np.zeros((2, members, ens_parts, height, chans), np.float32)
    for r in range(2):
        for b in range(members):
            for o in range(chans):
                at = b * used + r * chan_share + o % chan_share
                pick[r, b, o // chan_share, at, o] = 1.0
    pick = jnp.asarray(pick.reshape(2, members, ens_parts * height, chans).astype(jnp.bfloat16))

    vmem = pltpu.CompilerParams(vmem_limit_bytes=60 * 1024 * 1024)
    scalars = pl.BlockSpec(memory_space=pltpu.SMEM)
    whole = pl.BlockSpec(memory_space=pltpu.VMEM)
    grid_shape = (members, rows, chans, nlon)
    lined = jax.ShapeDtypeStruct((rows, depth, nlon), F32)
    edge = jax.ShapeDtypeStruct((members, halo, chans, nlon), BF16)
    taps_out = jax.ShapeDtypeStruct((size * size, depth, 128), F32)

    def call(body, outs, scratch, name, work, *args):
        specs = [scalars if a is flags else whole for a in args]
        return pl.pallas_call(
            body,
            out_shape=outs,
            in_specs=specs,
            scratch_shapes=scratch,
            compiler_params=vmem,
            cost_estimate=pl.CostEstimate(
                flops=work, transcendentals=0, bytes_accessed=8 * rows * depth * nlon
            ),
            name=name,
        )(*args)

    def swap(x):
        flat = x.reshape((ens_parts * groups,) + x.shape[2:])
        flat = lax.all_to_all(flat, ("ens", "lat"), split_axis=0, concat_axis=0, tiled=True)
        return flat.reshape(x.shape)

    work = 2 * size * size * rows * depth * nlon
    partial, taps, mixer = call(
        prepare_kernel,
        (lined, taps_out, jax.ShapeDtypeStruct((2, ens_parts * height, depth), BF16)),
        [pltpu.VMEM((rows, depth, wide), F32)],
        "prepare",
        work,
        own,
        kernel,
        mix_weight,
        pick,
    )
    legendre, partial = lax.optimization_barrier((legendre, partial))
    order_legendre = lax.all_to_all(legendre, "lat", split_axis=1, concat_axis=0, tiled=True)
    order_legendre = order_legendre.transpose(1, 0, 2)
    target = lax.dynamic_slice(
        truth, (ens_at * chan_share, 0, lat_at * share, 0), (chan_share, 2, share, degrees)
    )
    target = target.transpose(2, 1, 0, 3).reshape(share, used, degrees)
    target = jnp.pad(target, ((0, 0), (0, slots - used), (0, 0)))
    reorder = (jnp.arange(degrees)[:, None] == degree_order[None, :]).astype(BF16)

    def chunk(lines):
        return jax.ShapeDtypeStruct((ens_parts, groups, height, up(lines * share, 128)), BF16)

    sent, slope, inner, outer = call(
        functools.partial(forward_kernel, share),
        (chunk(rows), lined, edge, edge),
        [pltpu.VMEM((2 * halo, depth, wide), F32), pltpu.VMEM((rows, depth, nlon), F32)],
        "forward",
        work,
        flags,
        near,
        far,
        partial,
        taps,
        table,
        mixer,
    )
    got = swap(sent)
    near, far = partners(inner, outer)
    back, grads = call(
        functools.partial(score_kernel, members, used, rows, halo),
        (
            chunk(rows + 2 * halo),
            jax.ShapeDtypeStruct((up(degrees, 128) // 128, share * ens * slots, 128), F32),
        ),
        [
            pltpu.VMEM((nlat * share, ens * slots), F32),
            pltpu.VMEM(((nlat + 2 * halo) * share, ens * slots), F32),
        ],
        "score",
        work,
        got,
        order_legendre,
        target,
        reorder,
    )
    returned = swap(back)
    packed = call(
        functools.partial(pack_kernel, members, used, per_owner),
        jax.ShapeDtypeStruct(
            (ens_parts, groups, members * share, up(used * per_owner, 128)), BF16
        ),
        [],
        "pack",
        work,
        grads,
    )
    owned = swap(packed)
    grad_fields = call(
        functools.partial(backward_kernel, share),
        jax.ShapeDtypeStruct(grid_shape, BF16),
        [
            pltpu.VMEM((rows + 2 * halo, depth, wide), F32),
            pltpu.VMEM(taps_out.shape, F32),
            pltpu.VMEM((rows + 2 * halo, depth, nlon), F32),
            pltpu.VMEM((rows, depth, nlon), F32),
        ],
        "backward",
        work,
        flags,
        returned,
        near,
        far,
        kernel,
        mixer,
        table,
        slope,
    )
    score_grad = call(
        functools.partial(unpack_kernel, members),
        jax.ShapeDtypeStruct((members, chans, per_owner, 2, orders), F32),
        [],
        "unpack",
        work,
        owned,
    )
    return grad_fields.transpose(0, 2, 1, 3), score_grad.transpose(0, 1, 3, 4, 2)


def solution(mesh):
    placed = (P("ens", None, "lat", None), P(), P(), P("lat", None, None), P(), P())
    return jax.shard_map(
        local,
        mesh=mesh,
        in_specs=placed,
        out_specs=(P("ens", None, "lat", None), P("ens", None, None, None, "lat")),
        check_vma=False,
    )
```

```python
import functools
import math

import jax
import jax.numpy as jnp
import numpy as np
from jax import lax
from jax.experimental import pallas as pl
from jax.experimental.pallas import tpu as pltpu
from jax.sharding import PartitionSpec as P


smooth_width = 0.5
LEAD = 8
F32 = jnp.float32
BF16 = jnp.bfloat16


def up(value, step):
    return -(-value // step) * step


def wave_table(nlon, orders, span):
    columns = np.arange(nlon, dtype=np.int64)
    number = np.arange(orders, dtype=np.int64)
    angles = (columns[:, None] * number[None, :] % nlon) * (2.0 * math.pi / nlon)
    table = np.zeros((nlon, 2, span), np.float32)
    for part, values in enumerate((np.cos(angles), -np.sin(angles))):
        table[:, part, :orders] = values / math.sqrt(nlon)
    return table.reshape(nlon, 2 * span).astype(jnp.bfloat16)


def partners(inner, outer):
    count = lax.axis_size("lat")
    near = [(i, i ^ 1) for i in range(count)]
    far = [(i, (i + (1 if i % 2 else -1)) % count) for i in range(count)]
    one = lax.ppermute(inner, "lat", near)
    other = lax.ppermute(outer, "lat", far)
    return one, other


def place():
    at, count = lax.axis_index("lat"), lax.axis_size("lat")
    return jnp.stack([at % 2, at > 0, at < count - 1]).astype(jnp.int32)


def fill_row(padded, row, value):
    nlon, wide = value.shape[-1], padded.shape[-1]
    padded[row] = jnp.concatenate(
        [value[:, nlon - LEAD :], value, value[:, : wide - nlon - LEAD]], axis=-1
    )


def tap_sum(padded, taps, c0, lines, size):
    wide = padded.shape[-1]
    total = None
    for q in range(size):
        part = None
        for row, p in lines:
            weight = jnp.tile(taps[p * size + q, pl.ds(c0, 8), :], (1, wide // 128))
            term = weight * padded[row, pl.ds(c0, 8), :]
            part = term if part is None else part + term
        shift = (size // 2 - q) % wide
        if shift:
            part = pltpu.roll(part, shift, 1)
        total = part if total is None else total + part
    return total


def spread_taps(kernel, taps, flip):
    size, _, chans = kernel.shape
    for p in range(size):
        plane = kernel[p].T
        for q in range(size):
            value = plane[:, q : q + 1]
            if p == q == size // 2:
                value = value + 1.0
            at = p * size + q
            at = size * size - 1 - at if flip else at
            value = jnp.broadcast_to(value, (chans, 128))
            taps[at] = jnp.concatenate([value] * (taps.shape[1] // chans), axis=0)


def own_part(taps, partial, padded, size):
    rows, depth, nlon = partial.shape
    half = size // 2

    @pl.loop(0, depth // 8)
    def _(ct):
        c0 = pl.multiple_of(ct * 8, 8)
        for i in range(rows):
            lines = [(i + p - half, p) for p in range(size) if 0 <= i + p - half < rows]
            total = tap_sum(padded, taps, c0, lines, size)
            partial[i, pl.ds(c0, 8), :] = total[:, LEAD : LEAD + nlon]


def halo_part(flags, near, far, taps, partial, padded, size, emit):
    rows, depth, nlon = partial.shape
    half = size // 2
    odd, below, above = flags[0] == 1, flags[1] == 1, flags[2] == 1
    for row in range(half):
        one, other = joined(near, row), joined(far, row)
        zero = jnp.zeros_like(one)
        fill_row(padded, row, jnp.where(below, jnp.where(odd, one, other), zero))
        fill_row(padded, half + row, jnp.where(above, jnp.where(odd, other, one), zero))

    @pl.loop(0, depth // 8)
    def _(ct):
        c0 = pl.multiple_of(ct * 8, 8)
        for i in range(rows):
            lines = []
            for p in range(size):
                at = i + p - half
                if at < 0:
                    lines.append((at + half, p))
                elif at >= rows:
                    lines.append((at - rows + half, p))
            value = partial[i, pl.ds(c0, 8), :]
            if lines:
                total = tap_sum(padded, taps, c0, lines, size)
                value = value + total[:, LEAD : LEAD + nlon]
            emit(i, c0, value)


def joined(block, row):
    return jnp.concatenate([block[b, row].astype(F32) for b in range(block.shape[0])], axis=0)


def gelu_pair(x):
    scale = math.sqrt(2.0 / math.pi)
    square = x * x
    t = jnp.tanh(scale * x * (1.0 + 0.044715 * square))
    half = 0.5 * (1.0 + t)
    slope = half + 0.5 * x * (1.0 - t * t) * (scale * (1.0 + 3 * 0.044715 * square))
    return x * half, slope


def prepare_kernel(own, kernel, weight, pick, partial, taps, mixer, padded):
    members, rows, _, _ = own.shape
    size = kernel.shape[0]
    spread_taps(kernel, taps, False)
    for row in range(rows):
        fill_row(padded, row, joined(own, row))
    own_part(taps, partial, padded, size)
    for r in range(2):
        lines = []
        for b in range(members):
            lines.append(jnp.dot(pick[r, b], weight[...], preferred_element_type=F32))
        mixer[r] = jnp.concatenate(lines, axis=1).astype(BF16)


def forward_kernel(share, flags, near, far, partial, taps, table, mixer, out, slope, inner, outer, padded, act):
    rows, depth, nlon = partial.shape
    owners, groups, height, lanes = out.shape
    members, width, chans, _ = inner.shape
    size = math.isqrt(taps.shape[0])
    span = table.shape[1] // 2

    def emit(i, c0, value):
        value, grad = gelu_pair(value)
        act[i, pl.ds(c0, 8), :] = value
        slope[i, pl.ds(c0, 8), :] = grad

    halo_part(flags, near, far, taps, partial, padded, size, emit)
    odd = flags[0] == 1
    for row in range(width):
        first, last = slope[row], slope[rows - width + row]
        ours, theirs = jnp.where(odd, first, last), jnp.where(odd, last, first)
        for b in range(members):
            inner[b, row] = ours[b * chans : (b + 1) * chans].astype(BF16)
            outer[b, row] = theirs[b * chans : (b + 1) * chans].astype(BF16)
    flat = act[...].reshape(rows * depth, nlon).astype(BF16)
    spectral = jnp.dot(flat, table[...], preferred_element_type=F32).astype(BF16)
    mixed = []
    for i in range(rows):
        line = spectral[i * depth : (i + 1) * depth]
        mixed.append(
            jnp.dot(mixer[0], line[:, :span], preferred_element_type=F32)
            + jnp.dot(mixer[1], line[:, span:], preferred_element_type=F32)
        )
    for t in range(groups):
        pieces = [x[:, t * share : (t + 1) * share] for x in mixed]
        if lanes > rows * share:
            pieces.append(jnp.zeros((owners * height, lanes - rows * share), F32))
        block = jnp.concatenate(pieces, axis=1)
        for e in range(owners):
            out[e, t] = block[e * height : (e + 1) * height].astype(BF16)


def soft_sign(gaps):
    return gaps * lax.rsqrt(gaps * gaps + smooth_width * smooth_width)


def score_kernel(members, used, rows, halo, got, legendre, target, order, back, grads, spread, gather):
    owners, groups, height, lanes = got.shape
    orders, nlat, degrees = legendre.shape
    slots = target.shape[1]
    ens = owners * members
    for t in range(groups):
        pieces = []
        for e in range(owners):
            block = got[e, t].astype(F32)
            for b in range(members):
                pieces.append(block[b * used : (b + 1) * used])
                if slots > used:
                    pieces.append(jnp.zeros((slots - used, lanes), F32))
        block = jnp.concatenate(pieces, axis=0).T
        at = t * rows * orders
        spread[at : at + rows * orders, :] = block[: rows * orders]
    edge = halo * orders
    gather[:edge, :] = jnp.zeros((edge, ens * slots), F32)
    gather[edge + nlat * orders :, :] = jnp.zeros((edge, ens * slots), F32)

    @pl.loop(0, orders)
    def _(m):
        block = spread[pl.ds(m, nlat, stride=orders), :].astype(BF16)
        leg = legendre[m]
        coeff = lax.dot_general(
            block, leg, (((0,), (0,)), ((), ())), preferred_element_type=F32
        )
        own = [coeff[k * slots : (k + 1) * slots] for k in range(ens)]
        truth = target[m].astype(F32)
        sums = [None] * ens
        for k in range(ens):
            for n in range(k + 1, ens):
                sign = soft_sign(own[k] - own[n])
                sums[k] = sign if sums[k] is None else sums[k] + sign
                sums[n] = -sign if sums[n] is None else sums[n] - sign
        grad = jnp.concatenate(
            [
                soft_sign(own[k] - truth) * (1.0 / ens) - sums[k] * (1.0 / (ens * (ens - 1)))
                for k in range(ens)
            ],
            axis=0,
        ).astype(BF16)
        spec = lax.dot_general(
            leg, grad, (((1,), (1,)), ((), ())), preferred_element_type=F32
        )
        gather[pl.ds(edge + m, nlat, stride=orders), :] = spec
        at = pl.multiple_of(m * ens * slots, 8)
        ordered = jnp.dot(grad, order[...], preferred_element_type=F32)
        for j in range(grads.shape[0]):
            last = min(degrees, (j + 1) * 128)
            grads[j, pl.ds(at, ens * slots), : last - j * 128] = ordered[:, j * 128 : last]

    wide = back.shape[3]
    tall = (rows + 2 * halo) * orders
    for t in range(groups):
        at = t * rows * orders
        block = gather[at : at + tall, :]
        if wide > tall:
            block = jnp.concatenate([block, jnp.zeros((wide - tall, ens * slots), F32)], axis=0)
        block = block.T
        for e in range(owners):
            pieces = []
            for b in range(members):
                at = (e * members + b) * slots
                pieces.append(block[at : at + used])
            if height > members * used:
                pieces.append(jnp.zeros((height - members * used, wide), F32))
            back[e, t] = jnp.concatenate(pieces, axis=0).astype(BF16)


def backward_kernel(share, flags, got, near, far, kernel, mixer, table, slope, out, padded, taps, flat, stage):
    owners, groups, height, _ = got.shape
    rows, depth, nlon = slope.shape
    members, _, chans, _ = out.shape
    size = kernel.shape[0]
    half = size // 2
    span = table.shape[1] // 2
    total = rows + 2 * half
    spread_taps(kernel, taps, True)
    blocks = [
        jnp.concatenate([got[e, t].astype(F32) for e in range(owners)], axis=0) for t in range(groups)
    ]
    lines = []
    for i in range(total):
        pieces = [x[:, i * share : (i + 1) * share] for x in blocks]
        pieces.append(jnp.zeros((owners * height, span - groups * share), F32))
        line = jnp.concatenate(pieces, axis=1).astype(BF16)
        lines.append(
            jnp.concatenate(
                [
                    lax.dot_general(
                        mixer[r], line, (((0,), (0,)), ((), ())), preferred_element_type=F32
                    ).astype(BF16)
                    for r in range(2)
                ],
                axis=1,
            )
        )
    flat[...] = lax.dot_general(
        jnp.concatenate(lines, axis=0),
        table[...],
        (((1,), (1,)), ((), ())),
        preferred_element_type=F32,
    ).reshape(flat.shape)
    odd = flags[0] == 1
    for row in range(half):
        one, other = joined(near, row), joined(far, row)
        fill_row(padded, row, flat[row] * jnp.where(odd, one, other))
        at = half + rows + row
        fill_row(padded, at, flat[at] * jnp.where(odd, other, one))
    for row in range(rows):
        fill_row(padded, half + row, flat[half + row] * slope[row])

    @pl.loop(0, depth // 8)
    def _(ct):
        c0 = pl.multiple_of(ct * 8, 8)

        @pl.loop(0, rows)
        def _(i):
            value = tap_sum(padded, taps, c0, [(i + p, p) for p in range(size)], size)
            stage[i, pl.ds(c0, 8), :] = value[:, LEAD : LEAD + nlon]

    for b in range(members):
        for i in range(rows):
            out[b, i] = stage[i, b * chans : (b + 1) * chans, :].astype(BF16)


def pack_kernel(members, used, per_owner, grads, out):
    owners, groups, depth, lanes = out.shape
    share = depth // members
    stride = grads.shape[1] // share
    slots = stride // (owners * members)
    for e in range(owners):
        for b in range(members):
            at = (e * members + b) * slots
            planes = [
                jnp.concatenate(
                    [grads[j, pl.ds(at + s, share, stride=stride), :] for j in range(grads.shape[0])],
                    axis=1,
                )
                for s in range(used)
            ]
            for t in range(groups):
                pieces = [x[:, t * per_owner : (t + 1) * per_owner] for x in planes]
                if lanes > used * per_owner:
                    pieces.append(jnp.zeros((share, lanes - used * per_owner), F32))
                out[e, t, b * share : (b + 1) * share, :] = jnp.concatenate(pieces, axis=1).astype(BF16)


def unpack_kernel(members, got, out):
    owners, groups, depth, lanes = got.shape
    _, chans, per_owner, _, orders = out.shape
    share, chan_share = depth // members, chans // owners
    row = lax.broadcasted_iota(jnp.int32, (groups * depth, orders), 0)
    column = lax.broadcasted_iota(jnp.int32, (groups * depth, orders), 1)
    for b in range(members):
        wanted = (column // share) * depth + b * share + column % share
        picker = jnp.where(row == wanted, 1.0, 0.0).astype(BF16)
        for e in range(owners):
            block = lax.dot_general(
                got[e].reshape(groups * depth, lanes),
                picker,
                (((0,), (0,)), ((), ())),
                preferred_element_type=F32,
            )
            for c in range(chan_share):
                for r in range(2):
                    at = (r * chan_share + c) * per_owner
                    out[b, e * chan_share + c, :, r, :] = block[at : at + per_owner]


def local(fields, depth_kernel, mix_weight, legendre, truth, degree_order):
    ens_parts, groups = lax.axis_size("ens"), lax.axis_size("lat")
    ens_at, lat_at = lax.axis_index("ens"), lax.axis_index("lat")
    members, chans, rows, nlon = fields.shape
    _, orders, degrees = legendre.shape
    ens = members * ens_parts
    nlat = rows * groups
    share, per_owner, chan_share = orders // groups, degrees // groups, chans // ens_parts
    used = 2 * chan_share
    slots = up(used, 8)
    height = up(members * used, 8)
    wide = up(nlon + 2 * LEAD, 128)
    span = up(orders, 128)
    size = depth_kernel.shape[1]
    halo = size // 2
    depth = members * chans

    table = jnp.asarray(wave_table(nlon, orders, span))
    kernel = depth_kernel.transpose(1, 2, 0)
    flags = place()
    own = fields.transpose(0, 2, 1, 3)
    odd = lat_at % 2
    near, far = partners(
        lax.dynamic_slice_in_dim(own, (1 - odd) * (rows - halo), halo, 1),
        lax.dynamic_slice_in_dim(own, odd * (rows - halo), halo, 1),
    )

    pick = np.zeros((2, members, ens_parts, height, chans), np.float32)
    for r in range(2):
        for b in range(members):
            for o in range(chans):
                at = b * used + r * chan_share + o % chan_share
                pick[r, b, o // chan_share, at, o] = 1.0
    pick = jnp.asarray(pick.reshape(2, members, ens_parts * height, chans).astype(jnp.bfloat16))

    vmem = pltpu.CompilerParams(vmem_limit_bytes=60 * 1024 * 1024)
    scalars = pl.BlockSpec(memory_space=pltpu.SMEM)
    whole = pl.BlockSpec(memory_space=pltpu.VMEM)
    grid_shape = (members, rows, chans, nlon)
    lined = jax.ShapeDtypeStruct((rows, depth, nlon), F32)
    edge = jax.ShapeDtypeStruct((members, halo, chans, nlon), BF16)
    taps_out = jax.ShapeDtypeStruct((size * size, depth, 128), F32)

    def call(body, outs, scratch, work, *args):
        specs = [scalars if a is flags else whole for a in args]
        return pl.pallas_call(
            body,
            out_shape=outs,
            in_specs=specs,
            scratch_shapes=scratch,
            compiler_params=vmem,
            cost_estimate=pl.CostEstimate(
                flops=work, transcendentals=0, bytes_accessed=8 * rows * depth * nlon
            ),
        )(*args)

    def swap(x):
        flat = x.reshape((ens_parts * groups,) + x.shape[2:])
        flat = lax.all_to_all(flat, ("ens", "lat"), split_axis=0, concat_axis=0, tiled=True)
        return flat.reshape(x.shape)

    work = 2 * size * size * rows * depth * nlon
    partial, taps, mixer = call(
        prepare_kernel,
        (lined, taps_out, jax.ShapeDtypeStruct((2, ens_parts * height, depth), BF16)),
        [pltpu.VMEM((rows, depth, wide), F32)],
        work,
        own,
        kernel,
        mix_weight,
        pick,
    )
    legendre, partial = lax.optimization_barrier((legendre, partial))
    order_legendre = lax.all_to_all(legendre, "lat", split_axis=1, concat_axis=0, tiled=True)
    order_legendre = order_legendre.transpose(1, 0, 2)
    target = lax.dynamic_slice(
        truth, (ens_at * chan_share, 0, lat_at * share, 0), (chan_share, 2, share, degrees)
    )
    target = target.transpose(2, 1, 0, 3).reshape(share, used, degrees)
    target = jnp.pad(target, ((0, 0), (0, slots - used), (0, 0)))
    reorder = (jnp.arange(degrees)[:, None] == degree_order[None, :]).astype(BF16)

    def chunk(lines):
        return jax.ShapeDtypeStruct((ens_parts, groups, height, up(lines * share, 128)), BF16)

    sent, slope, inner, outer = call(
        functools.partial(forward_kernel, share),
        (chunk(rows), lined, edge, edge),
        [pltpu.VMEM((2 * halo, depth, wide), F32), pltpu.VMEM((rows, depth, nlon), F32)],
        work,
        flags,
        near,
        far,
        partial,
        taps,
        table,
        mixer,
    )
    got = swap(sent)
    got, inner, outer = lax.optimization_barrier((got, inner, outer))
    near, far = partners(inner, outer)
    back, grads = call(
        functools.partial(score_kernel, members, used, rows, halo),
        (
            chunk(rows + 2 * halo),
            jax.ShapeDtypeStruct((up(degrees, 128) // 128, share * ens * slots, 128), F32),
        ),
        [
            pltpu.VMEM((nlat * share, ens * slots), F32),
            pltpu.VMEM(((nlat + 2 * halo) * share, ens * slots), F32),
        ],
        work,
        got,
        order_legendre,
        target,
        reorder,
    )
    returned = swap(back)
    packed = call(
        functools.partial(pack_kernel, members, used, per_owner),
        jax.ShapeDtypeStruct(
            (ens_parts, groups, members * share, up(used * per_owner, 128)), BF16
        ),
        [],
        work,
        grads,
    )
    owned = swap(packed)
    grad_fields = call(
        functools.partial(backward_kernel, share),
        jax.ShapeDtypeStruct(grid_shape, BF16),
        [
            pltpu.VMEM((rows + 2 * halo, depth, wide), F32),
            pltpu.VMEM(taps_out.shape, F32),
            pltpu.VMEM((rows + 2 * halo, depth, nlon), F32),
            pltpu.VMEM((rows, depth, nlon), F32),
        ],
        work,
        flags,
        returned,
        near,
        far,
        kernel,
        mixer,
        table,
        slope,
    )
    score_grad = call(
        functools.partial(unpack_kernel, members),
        jax.ShapeDtypeStruct((members, chans, per_owner, 2, orders), F32),
        [],
        work,
        owned,
    )
    return grad_fields.transpose(0, 2, 1, 3), score_grad.transpose(0, 1, 3, 4, 2)


def solution(mesh):
    placed = (P("ens", None, "lat", None), P(), P(), P("lat", None, None), P(), P())

    return jax.shard_map(
        local,
        mesh=mesh,
        in_specs=placed,
        out_specs=(P("ens", None, "lat", None), P("ens", None, None, None, "lat")),
        check_vma=False,
    )
```

```python
import functools
import math

import jax
import jax.numpy as jnp
import numpy as np
from jax import lax
from jax.experimental import pallas as pl
from jax.experimental.pallas import tpu as pltpu
from jax.sharding import PartitionSpec as P


smooth_width = 0.5
TILE = 16
F32 = jnp.float32
BF16 = jnp.bfloat16


def up(value, step):
    return -(-value // step) * step


def wave_table(nlon, orders, span):
    columns = np.arange(nlon, dtype=np.int64)
    number = np.arange(orders, dtype=np.int64)
    angles = (columns[:, None] * number[None, :] % nlon) * (2.0 * math.pi / nlon)
    table = np.zeros((nlon, 2, span), np.float32)
    for part, values in enumerate((np.cos(angles), -np.sin(angles))):
        table[:, part, :orders] = values / math.sqrt(nlon)
    return table.reshape(nlon, 2 * span).astype(jnp.bfloat16)


def partners(inner, outer):
    count = lax.axis_size("lat")
    near = [(i, i ^ 1) for i in range(count)]
    far = [(i, (i + (1 if i % 2 else -1)) % count) for i in range(count)]
    one = lax.ppermute(inner, "lat", near)
    other = lax.ppermute(outer, "lat", far)
    return one, other


def place():
    at, count = lax.axis_index("lat"), lax.axis_size("lat")
    return jnp.stack([at % 2, (at > 0) & (at < count - 1)]).astype(jnp.int32)


def fill_row(padded, row, value, half):
    depth, nlon = value.shape
    wide = padded.shape[-1]
    base = nlon // 128 * 128
    tail = [value[:, base:], value[:, :half]]
    if wide > nlon + 2 * half:
        tail.append(jnp.zeros((depth, wide - nlon - 2 * half), value.dtype))
    tail.append(value[:, nlon - half :])
    padded[row, :, :base] = value[:, :base].astype(padded.dtype)
    padded[row, :, base:] = jnp.concatenate(tail, axis=-1).astype(padded.dtype)


def tap_sum(padded, taps, c0, lines, size):
    wide = padded.shape[-1]
    total = None
    for q in range(size):
        part = None
        for row, p in lines:
            weight = jnp.tile(taps[p * size + q, pl.ds(c0, TILE), :], (1, wide // 128))
            term = weight * padded[row, pl.ds(c0, TILE), :]
            part = term if part is None else part + term
        part = part.astype(F32)
        shift = (size // 2 - q) % wide
        if shift:
            part = pltpu.roll(part, shift, 1)
        total = part if total is None else total + part
    return total


def spread_taps(kernel, taps, flip):
    size, _, chans = kernel.shape
    for p in range(size):
        plane = kernel[p].T
        for q in range(size):
            at = p * size + q
            at = size * size - 1 - at if flip else at
            value = jnp.broadcast_to(plane[:, q : q + 1], (chans, 128))
            value = jnp.concatenate([value] * (taps.shape[1] // chans), axis=0)
            taps[at] = value.astype(taps.dtype)


def joined(block, row):
    return jnp.concatenate([block[b, row].astype(F32) for b in range(block.shape[0])], axis=0)


def gelu_pair(x):
    scale = math.sqrt(2.0 / math.pi)
    square = x * x
    t = jnp.tanh(scale * x * (1.0 + 0.044715 * square))
    half = 0.5 * (1.0 + t)
    slope = half + 0.5 * x * (1.0 - t * t) * (scale * (1.0 + 3 * 0.044715 * square))
    return x * half, slope


def prepare_kernel(own, kernel, weight, pick, partial, taps, mixer, padded):
    members, rows, chans, nlon = own.shape
    depth = members * chans
    size = kernel.shape[0]
    half = size // 2
    spread_taps(kernel, taps, False)
    for row in range(rows):
        fill_row(padded, row, joined(own, row), half)

    @pl.loop(0, depth // TILE)
    def _(ct):
        c0 = pl.multiple_of(ct * TILE, TILE)
        for i in range(rows):
            lines = [(i + p - half, p) for p in range(size) if 0 <= i + p - half < rows]
            total = tap_sum(padded, taps, c0, lines, size)
            total = total + padded[i, pl.ds(c0, TILE), :].astype(F32)
            partial[i, pl.ds(c0, TILE), :] = total[:, :nlon]

    for r in range(2):
        lines = []
        for b in range(members):
            lines.append(jnp.dot(pick[r, b], weight[...], preferred_element_type=F32))
        mixer[r] = jnp.concatenate(lines, axis=1).astype(BF16)


def finish_rows(lower, present, edge, partial, taps, table, mixer, slope, padded, act):
    rows, depth, nlon = partial.shape
    size = math.isqrt(taps.shape[0])
    half = size // 2
    span = table.shape[1] // 2
    for row in range(half):
        at = jnp.where(lower, row, half - 1 - row)
        value = joined(edge, at)
        if present is not None:
            value = jnp.where(present, value, jnp.zeros_like(value))
        fill_row(padded, row, value, half)

    @pl.loop(0, depth // TILE)
    def _(ct):
        c0 = pl.multiple_of(ct * TILE, TILE)
        for j in range(half):
            lines = [
                (row, jnp.where(lower, row - j, size - 1 - (row - j))) for row in range(j, half)
            ]
            at = jnp.where(lower, j, half - 1 - j)
            value = partial[jnp.where(lower, j, rows - 1 - j), pl.ds(c0, TILE), :]
            value = value + tap_sum(padded, taps, c0, lines, size)[:, :nlon]
            value, grad = gelu_pair(value)
            act[at, pl.ds(c0, TILE), :] = value.astype(BF16)
            slope[at, pl.ds(c0, TILE), :] = grad.astype(BF16)

    flat = act[...].reshape(half * depth, nlon)
    spectral = jnp.dot(flat, table[...], preferred_element_type=F32).astype(BF16)
    mixed = []
    for j in range(half):
        line = spectral[j * depth : (j + 1) * depth]
        mixed.append(
            jnp.dot(mixer[0], line[:, :span], preferred_element_type=F32)
            + jnp.dot(mixer[1], line[:, span:], preferred_element_type=F32)
        )
    return mixed


def near_kernel(flags, edge, partial, taps, table, mixer, mixed, slope, padded, act):
    lines = finish_rows(flags[0] == 1, None, edge, partial, taps, table, mixer, slope, padded, act)
    for j, line in enumerate(lines):
        mixed[j] = line


def far_kernel(share, flags, edge, partial, taps, table, mixer, nearer, out, slope, padded, act):
    owners, groups, height, lanes = out.shape
    lines = finish_rows(
        flags[0] != 1, flags[1] == 1, edge, partial, taps, table, mixer, slope, padded, act
    )
    lines = [nearer[j] for j in range(nearer.shape[0])] + lines
    for t in range(groups):
        pieces = [x[:, t * share : (t + 1) * share] for x in lines]
        if lanes > len(lines) * share:
            pieces.append(jnp.zeros((owners * height, lanes - len(lines) * share), F32))
        block = jnp.concatenate(pieces, axis=1)
        for e in range(owners):
            out[e, t] = block[e * height : (e + 1) * height].astype(BF16)


def flip_kernel(kernel, taps):
    spread_taps(kernel, taps, True)


def soft_sign(gaps):
    return gaps * lax.rsqrt(gaps * gaps + smooth_width * smooth_width)


def score_kernel(members, used, rows, halo, got, legendre, target, order, back, grads, spread, gather):
    owners, groups, height, lanes = got.shape
    orders, nlat, degrees = legendre.shape
    slots = target.shape[1]
    ens = owners * members
    for t in range(groups):
        pieces = []
        for e in range(owners):
            block = got[e, t].astype(F32)
            for b in range(members):
                pieces.append(block[b * used : (b + 1) * used])
                if slots > used:
                    pieces.append(jnp.zeros((slots - used, lanes), F32))
        block = jnp.concatenate(pieces, axis=0).T
        at, part = t * rows * orders, halo * orders
        first, second = (at, at + part) if t % 2 else (at + part, at)
        spread[first : first + part, :] = block[:part]
        spread[second : second + part, :] = block[part : 2 * part]
    edge = halo * orders
    gather[:edge, :] = jnp.zeros((edge, ens * slots), F32)
    gather[edge + nlat * orders :, :] = jnp.zeros((edge, ens * slots), F32)

    def one(m):
        block = spread[pl.ds(m, nlat, stride=orders), :].astype(BF16)
        leg = legendre[m]
        coeff = lax.dot_general(
            block, leg, (((0,), (0,)), ((), ())), preferred_element_type=F32
        )
        own = [coeff[k * slots : (k + 1) * slots] for k in range(ens)]
        truth = target[m].astype(F32)
        sums = [None] * ens
        for k in range(ens):
            for n in range(k + 1, ens):
                sign = soft_sign(own[k] - own[n])
                sums[k] = sign if sums[k] is None else sums[k] + sign
                sums[n] = -sign if sums[n] is None else sums[n] - sign
        grad = jnp.concatenate(
            [
                soft_sign(own[k] - truth) * (1.0 / ens) - sums[k] * (1.0 / (ens * (ens - 1)))
                for k in range(ens)
            ],
            axis=0,
        ).astype(BF16)
        spec = lax.dot_general(
            leg, grad, (((1,), (1,)), ((), ())), preferred_element_type=F32
        )
        gather[pl.ds(edge + m, nlat, stride=orders), :] = spec
        at = pl.multiple_of(m * ens * slots, 8)
        ordered = jnp.dot(grad, order[...], preferred_element_type=F32)
        for j in range(grads.shape[0]):
            last = min(degrees, (j + 1) * 128)
            grads[j, pl.ds(at, ens * slots), : last - j * 128] = ordered[:, j * 128 : last]

    step = 4 if orders % 4 == 0 else 1

    @pl.loop(0, orders // step)
    def _(trip):
        for j in range(step):
            one(trip * step + j)

    wide = back.shape[3]
    tall = (rows + 2 * halo) * orders
    for t in range(groups):
        at = t * rows * orders
        block = gather[at : at + tall, :]
        if wide > tall:
            block = jnp.concatenate([block, jnp.zeros((wide - tall, ens * slots), F32)], axis=0)
        block = block.T
        for e in range(owners):
            pieces = []
            for b in range(members):
                at = (e * members + b) * slots
                pieces.append(block[at : at + used])
            if height > members * used:
                pieces.append(jnp.zeros((height - members * used, wide), F32))
            back[e, t] = jnp.concatenate(pieces, axis=0).astype(BF16)


def backward_kernel(share, flags, got, near, far, inner, outer, taps, mixer, table, out, padded, flat, stage):
    owners, groups, height, _ = got.shape
    half, depth, nlon = inner.shape
    members, rows, chans, _ = out.shape
    size = math.isqrt(taps.shape[0])
    span = table.shape[1] // 2
    total = rows + 2 * half
    blocks = [
        jnp.concatenate([got[e, t].astype(F32) for e in range(owners)], axis=0) for t in range(groups)
    ]
    lines = []
    for i in range(total):
        pieces = [x[:, i * share : (i + 1) * share] for x in blocks]
        pieces.append(jnp.zeros((owners * height, span - groups * share), F32))
        line = jnp.concatenate(pieces, axis=1).astype(BF16)
        lines.append(
            jnp.concatenate(
                [
                    lax.dot_general(
                        mixer[r], line, (((0,), (0,)), ((), ())), preferred_element_type=F32
                    ).astype(BF16)
                    for r in range(2)
                ],
                axis=1,
            )
        )
    flat[...] = lax.dot_general(
        jnp.concatenate(lines, axis=0),
        table[...],
        (((1,), (1,)), ((), ())),
        preferred_element_type=F32,
    ).reshape(flat.shape)
    odd = flags[0] == 1
    pairs = ((near, far), (inner, outer), (outer, inner), (far, near))
    for part, (one, other) in enumerate(pairs):
        for row in range(half):
            at = part * half + row
            slope = jnp.where(odd, one[row].astype(F32), other[row].astype(F32))
            fill_row(padded, at, flat[at] * slope, half)

    @pl.loop(0, depth // TILE)
    def _(ct):
        c0 = pl.multiple_of(ct * TILE, TILE)

        @pl.loop(0, rows)
        def _(i):
            value = tap_sum(padded, taps, c0, [(i + p, p) for p in range(size)], size)
            value = value + padded[i + half, pl.ds(c0, TILE), :].astype(F32)
            stage[i, pl.ds(c0, TILE), :] = value[:, :nlon]

    for b in range(members):
        for i in range(rows):
            out[b, i] = stage[i, b * chans : (b + 1) * chans, :].astype(BF16)


def pack_kernel(members, used, per_owner, grads, out):
    owners, groups, depth, lanes = out.shape
    share = depth // members
    stride = grads.shape[1] // share
    slots = stride // (owners * members)
    for e in range(owners):
        for b in range(members):
            at = (e * members + b) * slots
            planes = [
                jnp.concatenate(
                    [grads[j, pl.ds(at + s, share, stride=stride), :] for j in range(grads.shape[0])],
                    axis=1,
                )
                for s in range(used)
            ]
            for t in range(groups):
                pieces = [x[:, t * per_owner : (t + 1) * per_owner] for x in planes]
                if lanes > used * per_owner:
                    pieces.append(jnp.zeros((share, lanes - used * per_owner), F32))
                out[e, t, b * share : (b + 1) * share, :] = jnp.concatenate(pieces, axis=1).astype(BF16)


def unpack_kernel(members, got, out):
    owners, groups, depth, lanes = got.shape
    _, chans, per_owner, _, orders = out.shape
    share, chan_share = depth // members, chans // owners
    row = lax.broadcasted_iota(jnp.int32, (groups * depth, orders), 0)
    column = lax.broadcasted_iota(jnp.int32, (groups * depth, orders), 1)
    for b in range(members):
        wanted = (column // share) * depth + b * share + column % share
        picker = jnp.where(row == wanted, 1.0, 0.0).astype(BF16)
        for e in range(owners):
            block = lax.dot_general(
                got[e].reshape(groups * depth, lanes),
                picker,
                (((0,), (0,)), ((), ())),
                preferred_element_type=F32,
            )
            for c in range(chan_share):
                for r in range(2):
                    at = (r * chan_share + c) * per_owner
                    out[b, e * chan_share + c, :, r, :] = block[at : at + per_owner]


def local(fields, depth_kernel, mix_weight, legendre, truth, degree_order):
    ens_parts, groups = lax.axis_size("ens"), lax.axis_size("lat")
    ens_at, lat_at = lax.axis_index("ens"), lax.axis_index("lat")
    members, chans, rows, nlon = fields.shape
    _, orders, degrees = legendre.shape
    ens = members * ens_parts
    nlat = rows * groups
    share, per_owner, chan_share = orders // groups, degrees // groups, chans // ens_parts
    used = 2 * chan_share
    slots = up(used, 8)
    height = up(members * used, 8)
    span = up(orders, 128)
    size = depth_kernel.shape[1]
    halo = size // 2
    wide = up(nlon + 2 * halo, 128)
    depth = members * chans

    table = jnp.asarray(wave_table(nlon, orders, span))
    kernel = depth_kernel.transpose(1, 2, 0)
    flags = place()
    own = fields.transpose(0, 2, 1, 3)
    odd = lat_at % 2
    near, far = partners(
        lax.dynamic_slice_in_dim(own, (1 - odd) * (rows - halo), halo, 1),
        lax.dynamic_slice_in_dim(own, odd * (rows - halo), halo, 1),
    )

    pick = np.zeros((2, members, ens_parts, height, chans), np.float32)
    for r in range(2):
        for b in range(members):
            for o in range(chans):
                at = b * used + r * chan_share + o % chan_share
                pick[r, b, o // chan_share, at, o] = 1.0
    pick = jnp.asarray(pick.reshape(2, members, ens_parts * height, chans).astype(jnp.bfloat16))

    vmem = pltpu.CompilerParams(vmem_limit_bytes=60 * 1024 * 1024)
    scalars = pl.BlockSpec(memory_space=pltpu.SMEM)
    whole = pl.BlockSpec(memory_space=pltpu.VMEM)
    grid_shape = (members, rows, chans, nlon)
    lined = jax.ShapeDtypeStruct((rows, depth, nlon), F32)
    edge = jax.ShapeDtypeStruct((halo, depth, nlon), BF16)
    taps_out = jax.ShapeDtypeStruct((size * size, depth, 128), BF16)

    def call(body, outs, scratch, work, *args):
        specs = [scalars if a is flags else whole for a in args]
        return pl.pallas_call(
            body,
            out_shape=outs,
            in_specs=specs,
            scratch_shapes=scratch,
            compiler_params=vmem,
            cost_estimate=pl.CostEstimate(
                flops=work, transcendentals=0, bytes_accessed=8 * rows * depth * nlon
            ),
        )(*args)

    def swap(x):
        flat = x.reshape((ens_parts * groups,) + x.shape[2:])
        flat = lax.all_to_all(flat, ("ens", "lat"), split_axis=0, concat_axis=0, tiled=True)
        return flat.reshape(x.shape)

    work = 2 * size * size * rows * depth * nlon
    partial, taps, mixer = call(
        prepare_kernel,
        (lined, taps_out, jax.ShapeDtypeStruct((2, ens_parts * height, depth), BF16)),
        [pltpu.VMEM((rows, depth, wide), BF16)],
        work,
        own,
        kernel,
        mix_weight,
        pick,
    )
    legendre, partial = lax.optimization_barrier((legendre, partial))
    order_legendre = lax.all_to_all(legendre, "lat", split_axis=1, concat_axis=0, tiled=True)
    order_legendre = order_legendre.transpose(1, 0, 2)
    target = lax.dynamic_slice(
        truth, (ens_at * chan_share, 0, lat_at * share, 0), (chan_share, 2, share, degrees)
    )
    target = target.transpose(2, 1, 0, 3).reshape(share, used, degrees)
    target = jnp.pad(target, ((0, 0), (0, slots - used), (0, 0)))
    reorder = (jnp.arange(degrees)[:, None] == degree_order[None, :]).astype(BF16)

    def chunk(lines):
        return jax.ShapeDtypeStruct((ens_parts, groups, height, up(lines * share, 128)), BF16)

    half_scratch = [pltpu.VMEM((halo, depth, wide), BF16), pltpu.VMEM((halo, depth, nlon), BF16)]
    mixed, inner = call(
        near_kernel,
        (jax.ShapeDtypeStruct((halo, ens_parts * height, span), F32), edge),
        half_scratch,
        work // 2,
        flags,
        near,
        partial,
        taps,
        table,
        mixer,
    )
    sent, outer = call(
        functools.partial(far_kernel, share),
        (chunk(rows), edge),
        half_scratch,
        work // 2,
        flags,
        far,
        partial,
        taps,
        table,
        mixer,
        mixed,
    )
    got = swap(sent)
    got, inner, outer = lax.optimization_barrier((got, inner, outer))
    near, far = partners(inner, outer)
    back, grads = call(
        functools.partial(score_kernel, members, used, rows, halo),
        (
            chunk(rows + 2 * halo),
            jax.ShapeDtypeStruct((up(degrees, 128) // 128, share * ens * slots, 128), F32),
        ),
        [
            pltpu.VMEM((nlat * share, ens * slots), F32),
            pltpu.VMEM(((nlat + 2 * halo) * share, ens * slots), F32),
        ],
        work,
        got,
        order_legendre,
        target,
        reorder,
    )
    returned = swap(back)
    packed = call(
        functools.partial(pack_kernel, members, used, per_owner),
        jax.ShapeDtypeStruct(
            (ens_parts, groups, members * share, up(used * per_owner, 128)), BF16
        ),
        [],
        work,
        grads,
    )
    owned = swap(packed)
    flipped = call(flip_kernel, taps_out, [], work // 8, kernel)
    grad_fields = call(
        functools.partial(backward_kernel, share),
        jax.ShapeDtypeStruct(grid_shape, BF16),
        [
            pltpu.VMEM((rows + 2 * halo, depth, wide), BF16),
            pltpu.VMEM((rows + 2 * halo, depth, nlon), F32),
            pltpu.VMEM((rows, depth, nlon), F32),
        ],
        work,
        flags,
        returned,
        near,
        far,
        inner,
        outer,
        flipped,
        mixer,
        table,
    )
    score_grad = call(
        functools.partial(unpack_kernel, members),
        jax.ShapeDtypeStruct((members, chans, per_owner, 2, orders), F32),
        [],
        work,
        owned,
    )
    return grad_fields.transpose(0, 2, 1, 3), score_grad.transpose(0, 1, 3, 4, 2)


def solution(mesh):
    placed = (P("ens", None, "lat", None), P(), P(), P("lat", None, None), P(), P())

    return jax.shard_map(
        local,
        mesh=mesh,
        in_specs=placed,
        out_specs=(P("ens", None, "lat", None), P("ens", None, None, None, "lat")),
        check_vma=False,
    )
```

```python
import functools
import math

import jax
import jax.numpy as jnp
import numpy as np
from jax import lax
from jax.experimental import pallas as pl
from jax.experimental.pallas import tpu as pltpu
from jax.sharding import PartitionSpec as P


smooth_width = 0.5
TILE = 16
F32 = jnp.float32
BF16 = jnp.bfloat16


def up(value, step):
    return -(-value // step) * step


def wave_table(nlon, orders, span):
    columns = np.arange(nlon, dtype=np.int64)
    number = np.arange(orders, dtype=np.int64)
    angles = (columns[:, None] * number[None, :] % nlon) * (2.0 * math.pi / nlon)
    table = np.zeros((nlon, 2, span), np.float32)
    for part, values in enumerate((np.cos(angles), -np.sin(angles))):
        table[:, part, :orders] = values / math.sqrt(nlon)
    return table.reshape(nlon, 2 * span).astype(jnp.bfloat16)


def partners(inner, outer):
    count = lax.axis_size("lat")
    near = [(i, i ^ 1) for i in range(count)]
    far = [(i, (i + (1 if i % 2 else -1)) % count) for i in range(count)]
    one = lax.ppermute(inner, "lat", near)
    other = lax.ppermute(outer, "lat", far)
    return one, other


def place():
    at, count = lax.axis_index("lat"), lax.axis_size("lat")
    return jnp.stack([at % 2, (at > 0) & (at < count - 1)]).astype(jnp.int32)


def fill_row(padded, row, value, half):
    depth, nlon = value.shape
    wide = padded.shape[-1]
    base = nlon // 128 * 128
    tail = [value[:, base:], value[:, :half]]
    if wide > nlon + 2 * half:
        tail.append(jnp.zeros((depth, wide - nlon - 2 * half), value.dtype))
    tail.append(value[:, nlon - half :])
    padded[row, :, :base] = value[:, :base].astype(padded.dtype)
    padded[row, :, base:] = jnp.concatenate(tail, axis=-1).astype(padded.dtype)


def tap_sum(padded, taps, c0, lines, size):
    wide = padded.shape[-1]
    total = None
    for q in range(size):
        part = None
        for row, p in lines:
            weight = jnp.tile(taps[p * size + q, pl.ds(c0, TILE), :], (1, wide // 128))
            term = weight * padded[row, pl.ds(c0, TILE), :]
            part = term if part is None else part + term
        part = part.astype(F32)
        shift = (size // 2 - q) % wide
        if shift:
            part = pltpu.roll(part, shift, 1)
        total = part if total is None else total + part
    return total


def spread_taps(kernel, taps, flip):
    size, _, chans = kernel.shape
    for p in range(size):
        plane = kernel[p].T
        for q in range(size):
            at = p * size + q
            at = size * size - 1 - at if flip else at
            value = jnp.broadcast_to(plane[:, q : q + 1], (chans, 128))
            value = jnp.concatenate([value] * (taps.shape[1] // chans), axis=0)
            taps[at] = value.astype(taps.dtype)


def joined(block, row):
    return jnp.concatenate([block[b, row].astype(F32) for b in range(block.shape[0])], axis=0)


def gelu_pair(x):
    scale = math.sqrt(2.0 / math.pi)
    square = x * x
    t = jnp.tanh(scale * x * (1.0 + 0.044715 * square))
    half = 0.5 * (1.0 + t)
    slope = half + 0.5 * x * (1.0 - t * t) * (scale * (1.0 + 3 * 0.044715 * square))
    return x * half, slope


def prepare_kernel(own, kernel, weight, pick, partial, taps, mixer, padded):
    members, rows, chans, nlon = own.shape
    depth = members * chans
    size = kernel.shape[0]
    half = size // 2
    spread_taps(kernel, taps, False)
    for row in range(rows):
        fill_row(padded, row, joined(own, row), half)

    @pl.loop(0, depth // TILE)
    def _(ct):
        c0 = pl.multiple_of(ct * TILE, TILE)
        for i in range(rows):
            lines = [(i + p - half, p) for p in range(size) if 0 <= i + p - half < rows]
            total = tap_sum(padded, taps, c0, lines, size)
            total = total + padded[i, pl.ds(c0, TILE), :].astype(F32)
            partial[i, pl.ds(c0, TILE), :] = total[:, :nlon]

    for r in range(2):
        lines = []
        for b in range(members):
            lines.append(jnp.dot(pick[r, b], weight[...], preferred_element_type=F32))
        mixer[r] = jnp.concatenate(lines, axis=1).astype(BF16)


def finish_rows(lower, present, edge, partial, taps, table, mixer, slope, padded, act):
    rows, depth, nlon = partial.shape
    size = math.isqrt(taps.shape[0])
    half = size // 2
    span = table.shape[1] // 2
    for row in range(half):
        at = jnp.where(lower, row, half - 1 - row)
        value = joined(edge, at)
        if present is not None:
            value = jnp.where(present, value, jnp.zeros_like(value))
        fill_row(padded, row, value, half)

    @pl.loop(0, depth // TILE)
    def _(ct):
        c0 = pl.multiple_of(ct * TILE, TILE)
        for j in range(half):
            lines = [
                (row, jnp.where(lower, row - j, size - 1 - (row - j))) for row in range(j, half)
            ]
            at = jnp.where(lower, j, half - 1 - j)
            value = partial[jnp.where(lower, j, rows - 1 - j), pl.ds(c0, TILE), :]
            value = value + tap_sum(padded, taps, c0, lines, size)[:, :nlon]
            value, grad = gelu_pair(value)
            act[at, pl.ds(c0, TILE), :] = value.astype(BF16)
            slope[at, pl.ds(c0, TILE), :] = grad.astype(BF16)

    flat = act[...].reshape(half * depth, nlon)
    spectral = jnp.dot(flat, table[...], preferred_element_type=F32).astype(BF16)
    mixed = []
    for j in range(half):
        line = spectral[j * depth : (j + 1) * depth]
        mixed.append(
            jnp.dot(mixer[0], line[:, :span], preferred_element_type=F32)
            + jnp.dot(mixer[1], line[:, span:], preferred_element_type=F32)
        )
    return mixed


def near_kernel(flags, edge, partial, taps, table, mixer, mixed, slope, padded, act):
    lines = finish_rows(flags[0] == 1, None, edge, partial, taps, table, mixer, slope, padded, act)
    for j, line in enumerate(lines):
        mixed[j] = line


def far_kernel(share, flags, edge, partial, taps, table, mixer, nearer, out, slope, padded, act):
    owners, groups, height, lanes = out.shape
    lines = finish_rows(
        flags[0] != 1, flags[1] == 1, edge, partial, taps, table, mixer, slope, padded, act
    )
    lines = [nearer[j] for j in range(nearer.shape[0])] + lines
    for t in range(groups):
        pieces = [x[:, t * share : (t + 1) * share] for x in lines]
        if lanes > len(lines) * share:
            pieces.append(jnp.zeros((owners * height, lanes - len(lines) * share), F32))
        block = jnp.concatenate(pieces, axis=1)
        for e in range(owners):
            out[e, t] = block[e * height : (e + 1) * height].astype(BF16)


def flip_kernel(kernel, taps):
    spread_taps(kernel, taps, True)


def soft_sign(gaps):
    return gaps * lax.rsqrt(gaps * gaps + smooth_width * smooth_width)


def score_kernel(members, used, rows, halo, got, legendre, target, order, back, grads, spread, gather):
    owners, groups, height, lanes = got.shape
    orders, nlat, degrees = legendre.shape
    slots = target.shape[1]
    ens = owners * members
    for t in range(groups):
        pieces = []
        for e in range(owners):
            block = got[e, t].astype(F32)
            for b in range(members):
                pieces.append(block[b * used : (b + 1) * used])
                if slots > used:
                    pieces.append(jnp.zeros((slots - used, lanes), F32))
        block = jnp.concatenate(pieces, axis=0).T
        at, part = t * rows * orders, halo * orders
        first, second = (at, at + part) if t % 2 else (at + part, at)
        spread[first : first + part, :] = block[:part]
        spread[second : second + part, :] = block[part : 2 * part]
    edge = halo * orders
    gather[:edge, :] = jnp.zeros((edge, ens * slots), F32)
    gather[edge + nlat * orders :, :] = jnp.zeros((edge, ens * slots), F32)

    def one(m):
        block = spread[pl.ds(m, nlat, stride=orders), :].astype(BF16)
        leg = legendre[m]
        coeff = lax.dot_general(
            block, leg, (((0,), (0,)), ((), ())), preferred_element_type=F32
        )
        own = [coeff[k * slots : (k + 1) * slots] for k in range(ens)]
        truth = target[m].astype(F32)
        sums = [None] * ens
        for k in range(ens):
            for n in range(k + 1, ens):
                sign = soft_sign(own[k] - own[n])
                sums[k] = sign if sums[k] is None else sums[k] + sign
                sums[n] = -sign if sums[n] is None else sums[n] - sign
        grad = jnp.concatenate(
            [
                soft_sign(own[k] - truth) * (1.0 / ens) - sums[k] * (1.0 / (ens * (ens - 1)))
                for k in range(ens)
            ],
            axis=0,
        ).astype(BF16)
        spec = lax.dot_general(
            leg, grad, (((1,), (1,)), ((), ())), preferred_element_type=F32
        )
        gather[pl.ds(edge + m, nlat, stride=orders), :] = spec
        at = pl.multiple_of(m * ens * slots, 8)
        ordered = jnp.dot(grad, order[...], preferred_element_type=F32)
        for j in range(grads.shape[0]):
            last = min(degrees, (j + 1) * 128)
            grads[j, pl.ds(at, ens * slots), : last - j * 128] = ordered[:, j * 128 : last]

    step = 4 if orders % 4 == 0 else 1

    @pl.loop(0, orders // step)
    def _(trip):
        for j in range(step):
            one(trip * step + j)

    wide = back.shape[3]
    tall = (rows + 2 * halo) * orders
    for t in range(groups):
        at = t * rows * orders
        block = gather[at : at + tall, :]
        if wide > tall:
            block = jnp.concatenate([block, jnp.zeros((wide - tall, ens * slots), F32)], axis=0)
        block = block.T
        for e in range(owners):
            pieces = []
            for b in range(members):
                at = (e * members + b) * slots
                pieces.append(block[at : at + used])
            if height > members * used:
                pieces.append(jnp.zeros((height - members * used, wide), F32))
            back[e, t] = jnp.concatenate(pieces, axis=0).astype(BF16)


def backward_kernel(share, flags, got, near, far, inner, outer, taps, mixer, table, out, padded, flat, stage):
    owners, groups, height, _ = got.shape
    half, depth, nlon = inner.shape
    members, rows, chans, _ = out.shape
    size = math.isqrt(taps.shape[0])
    span = table.shape[1] // 2
    total = rows + 2 * half
    blocks = [
        jnp.concatenate([got[e, t].astype(F32) for e in range(owners)], axis=0) for t in range(groups)
    ]
    lines = []
    for i in range(total):
        pieces = [x[:, i * share : (i + 1) * share] for x in blocks]
        pieces.append(jnp.zeros((owners * height, span - groups * share), F32))
        line = jnp.concatenate(pieces, axis=1).astype(BF16)
        lines.append(
            jnp.concatenate(
                [
                    lax.dot_general(
                        mixer[r], line, (((0,), (0,)), ((), ())), preferred_element_type=F32
                    ).astype(BF16)
                    for r in range(2)
                ],
                axis=1,
            )
        )
    flat[...] = lax.dot_general(
        jnp.concatenate(lines, axis=0),
        table[...],
        (((1,), (1,)), ((), ())),
        preferred_element_type=F32,
    ).reshape(flat.shape)
    odd = flags[0] == 1
    pairs = ((near, far), (inner, outer), (outer, inner), (far, near))
    for part, (one, other) in enumerate(pairs):
        for row in range(half):
            at = part * half + row
            slope = jnp.where(odd, one[row].astype(F32), other[row].astype(F32))
            fill_row(padded, at, flat[at] * slope, half)

    @pl.loop(0, depth // TILE)
    def _(ct):
        c0 = pl.multiple_of(ct * TILE, TILE)

        @pl.loop(0, rows)
        def _(i):
            value = tap_sum(padded, taps, c0, [(i + p, p) for p in range(size)], size)
            value = value + padded[i + half, pl.ds(c0, TILE), :].astype(F32)
            stage[i, pl.ds(c0, TILE), :] = value[:, :nlon]

    for b in range(members):
        for i in range(rows):
            out[b, i] = stage[i, b * chans : (b + 1) * chans, :].astype(BF16)


def pack_kernel(members, used, per_owner, grads, out):
    owners, groups, depth, lanes = out.shape
    share = depth // members
    stride = grads.shape[1] // share
    slots = stride // (owners * members)
    for e in range(owners):
        for b in range(members):
            at = (e * members + b) * slots
            planes = [
                jnp.concatenate(
                    [grads[j, pl.ds(at + s, share, stride=stride), :] for j in range(grads.shape[0])],
                    axis=1,
                )
                for s in range(used)
            ]
            for t in range(groups):
                pieces = [x[:, t * per_owner : (t + 1) * per_owner] for x in planes]
                if lanes > used * per_owner:
                    pieces.append(jnp.zeros((share, lanes - used * per_owner), F32))
                out[e, t, b * share : (b + 1) * share, :] = jnp.concatenate(pieces, axis=1).astype(BF16)


def unpack_kernel(members, got, out):
    _, groups, depth, lanes = got.shape
    _, chan_share, per_owner, _, orders = out.shape
    share = depth // members
    row = lax.broadcasted_iota(jnp.int32, (groups * depth, orders), 0)
    column = lax.broadcasted_iota(jnp.int32, (groups * depth, orders), 1)
    block = got[0].reshape(groups * depth, lanes)
    for b in range(members):
        wanted = (column // share) * depth + b * share + column % share
        picker = jnp.where(row == wanted, 1.0, 0.0).astype(BF16)
        lines = lax.dot_general(
            block, picker, (((0,), (0,)), ((), ())), preferred_element_type=F32
        )
        for c in range(chan_share):
            for r in range(2):
                at = (r * chan_share + c) * per_owner
                out[b, c, :, r, :] = lines[at : at + per_owner]


def local(fields, depth_kernel, mix_weight, legendre, truth, degree_order):
    ens_parts, groups = lax.axis_size("ens"), lax.axis_size("lat")
    ens_at, lat_at = lax.axis_index("ens"), lax.axis_index("lat")
    members, chans, rows, nlon = fields.shape
    _, orders, degrees = legendre.shape
    ens = members * ens_parts
    nlat = rows * groups
    share, per_owner, chan_share = orders // groups, degrees // groups, chans // ens_parts
    used = 2 * chan_share
    slots = up(used, 8)
    height = up(members * used, 8)
    span = up(orders, 128)
    size = depth_kernel.shape[1]
    halo = size // 2
    wide = up(nlon + 2 * halo, 128)
    depth = members * chans

    table = jnp.asarray(wave_table(nlon, orders, span))
    kernel = depth_kernel.transpose(1, 2, 0)
    flags = place()
    own = fields.transpose(0, 2, 1, 3)
    odd = lat_at % 2
    near, far = partners(
        lax.dynamic_slice_in_dim(own, (1 - odd) * (rows - halo), halo, 1),
        lax.dynamic_slice_in_dim(own, odd * (rows - halo), halo, 1),
    )

    pick = np.zeros((2, members, ens_parts, height, chans), np.float32)
    for r in range(2):
        for b in range(members):
            for o in range(chans):
                at = b * used + r * chan_share + o % chan_share
                pick[r, b, o // chan_share, at, o] = 1.0
    pick = jnp.asarray(pick.reshape(2, members, ens_parts * height, chans).astype(jnp.bfloat16))

    vmem = pltpu.CompilerParams(vmem_limit_bytes=60 * 1024 * 1024)
    scalars = pl.BlockSpec(memory_space=pltpu.SMEM)
    whole = pl.BlockSpec(memory_space=pltpu.VMEM)
    grid_shape = (members, rows, chans, nlon)
    lined = jax.ShapeDtypeStruct((rows, depth, nlon), F32)
    edge = jax.ShapeDtypeStruct((halo, depth, nlon), BF16)
    taps_out = jax.ShapeDtypeStruct((size * size, depth, 128), BF16)

    def call(body, outs, scratch, work, *args):
        specs = [scalars if a is flags else whole for a in args]
        return pl.pallas_call(
            body,
            out_shape=outs,
            in_specs=specs,
            scratch_shapes=scratch,
            compiler_params=vmem,
            cost_estimate=pl.CostEstimate(
                flops=work, transcendentals=0, bytes_accessed=8 * rows * depth * nlon
            ),
        )(*args)

    def swap(x):
        flat = x.reshape((ens_parts * groups,) + x.shape[2:])
        flat = lax.all_to_all(flat, ("ens", "lat"), split_axis=0, concat_axis=0, tiled=True)
        return flat.reshape(x.shape)

    work = 2 * size * size * rows * depth * nlon
    partial, taps, mixer = call(
        prepare_kernel,
        (lined, taps_out, jax.ShapeDtypeStruct((2, ens_parts * height, depth), BF16)),
        [pltpu.VMEM((rows, depth, wide), BF16)],
        work,
        own,
        kernel,
        mix_weight,
        pick,
    )
    legendre, partial = lax.optimization_barrier((legendre, partial))
    order_legendre = lax.all_to_all(legendre, "lat", split_axis=1, concat_axis=0, tiled=True)
    order_legendre = order_legendre.transpose(1, 0, 2)
    target = lax.dynamic_slice(
        truth, (ens_at * chan_share, 0, lat_at * share, 0), (chan_share, 2, share, degrees)
    )
    target = target.transpose(2, 1, 0, 3).reshape(share, used, degrees)
    target = jnp.pad(target, ((0, 0), (0, slots - used), (0, 0)))
    reorder = (jnp.arange(degrees)[:, None] == degree_order[None, :]).astype(BF16)

    def chunk(lines):
        return jax.ShapeDtypeStruct((ens_parts, groups, height, up(lines * share, 128)), BF16)

    half_scratch = [pltpu.VMEM((halo, depth, wide), BF16), pltpu.VMEM((halo, depth, nlon), BF16)]
    mixed, inner = call(
        near_kernel,
        (jax.ShapeDtypeStruct((halo, ens_parts * height, span), F32), edge),
        half_scratch,
        work // 2,
        flags,
        near,
        partial,
        taps,
        table,
        mixer,
    )
    sent, outer = call(
        functools.partial(far_kernel, share),
        (chunk(rows), edge),
        half_scratch,
        work // 2,
        flags,
        far,
        partial,
        taps,
        table,
        mixer,
        mixed,
    )
    got = swap(sent)
    got, held = lax.optimization_barrier((got, outer))
    near, far = partners(inner, held)
    back, grads = call(
        functools.partial(score_kernel, members, used, rows, halo),
        (
            chunk(rows + 2 * halo),
            jax.ShapeDtypeStruct((up(degrees, 128) // 128, share * ens * slots, 128), F32),
        ),
        [
            pltpu.VMEM((nlat * share, ens * slots), F32),
            pltpu.VMEM(((nlat + 2 * halo) * share, ens * slots), F32),
        ],
        work,
        got,
        order_legendre,
        target,
        reorder,
    )
    returned = swap(back)
    packed = call(
        functools.partial(pack_kernel, members, used, per_owner),
        jax.ShapeDtypeStruct(
            (ens_parts, groups, members * share, up(used * per_owner, 128)), BF16
        ),
        [],
        work,
        grads,
    )
    owned = swap(packed)
    flipped = call(flip_kernel, taps_out, [], work // 8, kernel)
    grad_fields = call(
        functools.partial(backward_kernel, share),
        jax.ShapeDtypeStruct(grid_shape, BF16),
        [
            pltpu.VMEM((rows + 2 * halo, depth, wide), BF16),
            pltpu.VMEM((rows + 2 * halo, depth, nlon), F32),
            pltpu.VMEM((rows, depth, nlon), F32),
        ],
        work,
        flags,
        returned,
        near,
        far,
        inner,
        outer,
        flipped,
        mixer,
        table,
    )
    score_grad = pl.pallas_call(
        functools.partial(unpack_kernel, members),
        out_shape=jax.ShapeDtypeStruct((members, chans, per_owner, 2, orders), F32),
        grid=(ens_parts,),
        in_specs=[pl.BlockSpec((1,) + owned.shape[1:], lambda e: (e, 0, 0, 0))],
        out_specs=pl.BlockSpec(
            (members, chan_share, per_owner, 2, orders), lambda e: (0, e, 0, 0, 0)
        ),
        compiler_params=vmem,
        cost_estimate=pl.CostEstimate(flops=work, transcendentals=0, bytes_accessed=1),
        name="unpack",
    )(owned)
    return grad_fields.transpose(0, 2, 1, 3), score_grad.transpose(0, 1, 3, 4, 2)


def solution(mesh):
    placed = (P("ens", None, "lat", None), P(), P(), P("lat", None, None), P(), P())

    return jax.shard_map(
        local,
        mesh=mesh,
        in_specs=placed,
        out_specs=(P("ens", None, "lat", None), P("ens", None, None, None, "lat")),
        check_vma=False,
    )
```

```python
import functools
import math

import jax
import jax.numpy as jnp
import numpy as np
from jax import lax
from jax.experimental import pallas as pl
from jax.experimental.pallas import tpu as pltpu
from jax.sharding import PartitionSpec as P


smooth_width = 0.5
TILE = 16
F32 = jnp.float32
BF16 = jnp.bfloat16


def up(value, step):
    return -(-value // step) * step


def wave_table(nlon, orders, span):
    columns = np.arange(nlon, dtype=np.int64)
    number = np.arange(orders, dtype=np.int64)
    angles = (columns[:, None] * number[None, :] % nlon) * (2.0 * math.pi / nlon)
    table = np.zeros((nlon, 2, span), np.float32)
    for part, values in enumerate((np.cos(angles), -np.sin(angles))):
        table[:, part, :orders] = values / math.sqrt(nlon)
    return table.reshape(nlon, 2 * span).astype(jnp.bfloat16)


def partner(edge, pair):
    count = lax.axis_size("lat")
    if pair:
        steps = [(i, i ^ 1) for i in range(count)]
    else:
        steps = [(i, (i + (1 if i % 2 else -1)) % count) for i in range(count)]
    return lax.ppermute(edge, "lat", steps)


def place():
    at, count = lax.axis_index("lat"), lax.axis_size("lat")
    return jnp.stack([at % 2, (at > 0) & (at < count - 1)]).astype(jnp.int32)


def fill_row(padded, row, value, half):
    depth, nlon = value.shape
    wide = padded.shape[-1]
    base = nlon // 128 * 128
    tail = [value[:, base:], value[:, :half]]
    if wide > nlon + 2 * half:
        tail.append(jnp.zeros((depth, wide - nlon - 2 * half), value.dtype))
    tail.append(value[:, nlon - half :])
    padded[row, :, :base] = value[:, :base].astype(padded.dtype)
    padded[row, :, base:] = jnp.concatenate(tail, axis=-1).astype(padded.dtype)


def tap_sum(padded, taps, c0, lines, size):
    wide = padded.shape[-1]
    total = None
    for q in range(size):
        part = None
        for row, p in lines:
            weight = jnp.tile(taps[p * size + q, pl.ds(c0, TILE), :], (1, wide // 128))
            term = weight * padded[row, pl.ds(c0, TILE), :]
            part = term if part is None else part + term
        part = part.astype(F32)
        shift = (size // 2 - q) % wide
        if shift:
            part = pltpu.roll(part, shift, 1)
        total = part if total is None else total + part
    return total


def spread_taps(kernel, taps, flip):
    size, _, chans = kernel.shape
    for p in range(size):
        plane = kernel[p].T
        for q in range(size):
            at = p * size + q
            at = size * size - 1 - at if flip else at
            value = jnp.broadcast_to(plane[:, q : q + 1], (chans, 128))
            value = jnp.concatenate([value] * (taps.shape[1] // chans), axis=0)
            taps[at] = value.astype(taps.dtype)


def joined(block, row):
    return jnp.concatenate([block[b, row].astype(F32) for b in range(block.shape[0])], axis=0)


def gelu_pair(x):
    scale = math.sqrt(2.0 / math.pi)
    square = x * x
    t = jnp.tanh(scale * x * (1.0 + 0.044715 * square))
    half = 0.5 * (1.0 + t)
    slope = half + 0.5 * x * (1.0 - t * t) * (scale * (1.0 + 3 * 0.044715 * square))
    return x * half, slope


def prepare_kernel(own, kernel, weight, pick, partial, taps, mixer, padded):
    members, rows, chans, nlon = own.shape
    depth = members * chans
    size = kernel.shape[0]
    half = size // 2
    spread_taps(kernel, taps, False)
    for row in range(rows):
        fill_row(padded, row, joined(own, row), half)

    @pl.loop(0, depth // TILE)
    def _(ct):
        c0 = pl.multiple_of(ct * TILE, TILE)
        for i in range(rows):
            lines = [(i + p - half, p) for p in range(size) if 0 <= i + p - half < rows]
            total = tap_sum(padded, taps, c0, lines, size)
            total = total + padded[i, pl.ds(c0, TILE), :].astype(F32)
            partial[i, pl.ds(c0, TILE), :] = total[:, :nlon]

    for r in range(2):
        lines = []
        for b in range(members):
            lines.append(jnp.dot(pick[r, b], weight[...], preferred_element_type=F32))
        mixer[r] = jnp.concatenate(lines, axis=1).astype(BF16)


def finish_rows(lower, present, edge, partial, taps, table, mixer, slope, padded, act):
    rows, depth, nlon = partial.shape
    size = math.isqrt(taps.shape[0])
    half = size // 2
    span = table.shape[1] // 2
    for row in range(half):
        at = jnp.where(lower, row, half - 1 - row)
        value = joined(edge, at)
        if present is not None:
            value = jnp.where(present, value, jnp.zeros_like(value))
        fill_row(padded, row, value, half)

    @pl.loop(0, depth // TILE)
    def _(ct):
        c0 = pl.multiple_of(ct * TILE, TILE)
        for j in range(half):
            lines = [
                (row, jnp.where(lower, row - j, size - 1 - (row - j))) for row in range(j, half)
            ]
            at = jnp.where(lower, j, half - 1 - j)
            value = partial[jnp.where(lower, j, rows - 1 - j), pl.ds(c0, TILE), :]
            value = value + tap_sum(padded, taps, c0, lines, size)[:, :nlon]
            value, grad = gelu_pair(value)
            act[at, pl.ds(c0, TILE), :] = value.astype(BF16)
            slope[at, pl.ds(c0, TILE), :] = grad.astype(BF16)

    flat = act[...].reshape(half * depth, nlon)
    spectral = jnp.dot(flat, table[...], preferred_element_type=F32).astype(BF16)
    mixed = []
    for j in range(half):
        line = spectral[j * depth : (j + 1) * depth]
        mixed.append(
            jnp.dot(mixer[0], line[:, :span], preferred_element_type=F32)
            + jnp.dot(mixer[1], line[:, span:], preferred_element_type=F32)
        )
    return mixed


def near_kernel(flags, edge, partial, taps, table, mixer, mixed, slope, padded, act):
    lines = finish_rows(flags[0] == 1, None, edge, partial, taps, table, mixer, slope, padded, act)
    for j, line in enumerate(lines):
        mixed[j] = line


def far_kernel(share, flags, edge, partial, taps, table, mixer, nearer, out, slope, padded, act):
    owners, groups, height, lanes = out.shape
    lines = finish_rows(
        flags[0] != 1, flags[1] == 1, edge, partial, taps, table, mixer, slope, padded, act
    )
    lines = [nearer[j] for j in range(nearer.shape[0])] + lines
    for t in range(groups):
        pieces = [x[:, t * share : (t + 1) * share] for x in lines]
        if lanes > len(lines) * share:
            pieces.append(jnp.zeros((owners * height, lanes - len(lines) * share), F32))
        block = jnp.concatenate(pieces, axis=1)
        for e in range(owners):
            out[e, t] = block[e * height : (e + 1) * height].astype(BF16)


def flip_kernel(kernel, taps):
    spread_taps(kernel, taps, True)


def soft_sign(gaps):
    return gaps * lax.rsqrt(gaps * gaps + smooth_width * smooth_width)


def score_kernel(members, used, rows, halo, got, legendre, target, order, back, grads, spread, gather, picked):
    owners, groups, height, lanes = got.shape
    orders, nlat, degrees = legendre.shape
    slots = target.shape[1]
    ens = owners * members
    for t in range(groups):
        pieces = []
        for e in range(owners):
            block = got[e, t].astype(F32)
            for b in range(members):
                pieces.append(block[b * used : (b + 1) * used])
                if slots > used:
                    pieces.append(jnp.zeros((slots - used, lanes), F32))
        block = jnp.concatenate(pieces, axis=0).T
        at, part = t * rows * orders, halo * orders
        first, second = (at, at + part) if t % 2 else (at + part, at)
        spread[first : first + part, :] = block[:part]
        spread[second : second + part, :] = block[part : 2 * part]
    reorder = jnp.where(
        lax.broadcasted_iota(jnp.int32, (degrees, degrees), 0) == order[...], 1.0, 0.0
    )
    picked[...] = reorder.astype(BF16)
    edge = halo * orders
    gather[:edge, :] = jnp.zeros((edge, ens * slots), F32)
    gather[edge + nlat * orders :, :] = jnp.zeros((edge, ens * slots), F32)

    def score(values, truth):
        own = [values[k * slots : (k + 1) * slots] for k in range(ens)]
        sums = [None] * ens
        for k in range(ens):
            for n in range(k + 1, ens):
                sign = soft_sign(own[k] - own[n])
                sums[k] = sign if sums[k] is None else sums[k] + sign
                sums[n] = -sign if sums[n] is None else sums[n] - sign
        return jnp.concatenate(
            [
                soft_sign(own[k] - truth) * (1.0 / ens) - sums[k] * (1.0 / (ens * (ens - 1)))
                for k in range(ens)
            ],
            axis=0,
        )

    tail = degrees % 128
    packs = tail > 0 and 128 % tail == 0 and orders % (128 // tail) == 0
    step = 128 // tail if packs else 1
    body = degrees - tail if packs else degrees

    @pl.loop(0, orders // step)
    def _(trip):
        numbers = [trip * step + j for j in range(step)]
        coeffs = [
            lax.dot_general(
                spread[pl.ds(m, nlat, stride=orders), :].astype(BF16),
                legendre[m],
                (((0,), (0,)), ((), ())),
                preferred_element_type=F32,
            )
            for m in numbers
        ]
        truths = [target[m].astype(F32) for m in numbers]
        scored = [score(x[:, :body], y[:, :body]) for x, y in zip(coeffs, truths)]
        if packs:
            rest = score(
                jnp.concatenate([x[:, body:] for x in coeffs], axis=1),
                jnp.concatenate([y[:, body:] for y in truths], axis=1),
            )
            scored = [
                jnp.concatenate([x, rest[:, j * tail : (j + 1) * tail]], axis=1)
                for j, x in enumerate(scored)
            ]
        for m, grad in zip(numbers, scored):
            grad = grad.astype(BF16)
            gather[pl.ds(edge + m, nlat, stride=orders), :] = lax.dot_general(
                legendre[m], grad, (((1,), (1,)), ((), ())), preferred_element_type=F32
            )
            at = pl.multiple_of(m * ens * slots, 8)
            ordered = jnp.dot(grad, picked[...], preferred_element_type=F32)
            for j in range(grads.shape[0]):
                last = min(degrees, (j + 1) * 128)
                grads[j, pl.ds(at, ens * slots), : last - j * 128] = ordered[:, j * 128 : last]

    wide = back.shape[3]
    tall = (rows + 2 * halo) * orders
    for t in range(groups):
        at = t * rows * orders
        block = gather[at : at + tall, :]
        if wide > tall:
            block = jnp.concatenate([block, jnp.zeros((wide - tall, ens * slots), F32)], axis=0)
        block = block.T
        for e in range(owners):
            pieces = []
            for b in range(members):
                at = (e * members + b) * slots
                pieces.append(block[at : at + used])
            if height > members * used:
                pieces.append(jnp.zeros((height - members * used, wide), F32))
            back[e, t] = jnp.concatenate(pieces, axis=0).astype(BF16)


def backward_kernel(share, flags, got, near, far, inner, outer, taps, mixer, table, out, padded, flat, stage):
    owners, groups, height, _ = got.shape
    half, depth, nlon = inner.shape
    members, rows, chans, _ = out.shape
    size = math.isqrt(taps.shape[0])
    span = table.shape[1] // 2
    total = rows + 2 * half
    blocks = [
        jnp.concatenate([got[e, t].astype(F32) for e in range(owners)], axis=0) for t in range(groups)
    ]
    lines = []
    for i in range(total):
        pieces = [x[:, i * share : (i + 1) * share] for x in blocks]
        pieces.append(jnp.zeros((owners * height, span - groups * share), F32))
        line = jnp.concatenate(pieces, axis=1).astype(BF16)
        lines.append(
            jnp.concatenate(
                [
                    lax.dot_general(
                        mixer[r], line, (((0,), (0,)), ((), ())), preferred_element_type=F32
                    ).astype(BF16)
                    for r in range(2)
                ],
                axis=1,
            )
        )
    flat[...] = lax.dot_general(
        jnp.concatenate(lines, axis=0),
        table[...],
        (((1,), (1,)), ((), ())),
        preferred_element_type=F32,
    ).reshape(flat.shape)
    odd = flags[0] == 1
    pairs = ((near, far), (inner, outer), (outer, inner), (far, near))
    for part, (one, other) in enumerate(pairs):
        for row in range(half):
            at = part * half + row
            slope = jnp.where(odd, one[row].astype(F32), other[row].astype(F32))
            fill_row(padded, at, flat[at] * slope, half)

    @pl.loop(0, depth // TILE)
    def _(ct):
        c0 = pl.multiple_of(ct * TILE, TILE)

        @pl.loop(0, rows)
        def _(i):
            value = tap_sum(padded, taps, c0, [(i + p, p) for p in range(size)], size)
            value = value + padded[i + half, pl.ds(c0, TILE), :].astype(F32)
            stage[i, pl.ds(c0, TILE), :] = value[:, :nlon]

    for b in range(members):
        for i in range(rows):
            out[b, i] = stage[i, b * chans : (b + 1) * chans, :].astype(BF16)


def pack_kernel(members, used, per_owner, grads, out):
    owners, groups, depth, lanes = out.shape
    share = depth // members
    stride = grads.shape[1] // share
    slots = stride // (owners * members)
    for e in range(owners):
        for b in range(members):
            at = (e * members + b) * slots
            planes = [
                jnp.concatenate(
                    [grads[j, pl.ds(at + s, share, stride=stride), :] for j in range(grads.shape[0])],
                    axis=1,
                )
                for s in range(used)
            ]
            for t in range(groups):
                pieces = [x[:, t * per_owner : (t + 1) * per_owner] for x in planes]
                if lanes > used * per_owner:
                    pieces.append(jnp.zeros((share, lanes - used * per_owner), F32))
                out[e, t, b * share : (b + 1) * share, :] = jnp.concatenate(pieces, axis=1).astype(BF16)


def unpack_kernel(members, got, out, swapped, pickers):
    _, groups, depth, lanes = got.shape
    _, chan_share, per_owner, _, orders = out.shape
    share = depth // members
    pair = 2 * per_owner

    def iotas(shape):
        return (lax.broadcasted_iota(jnp.int32, shape, d) for d in range(2))

    @pl.when(pl.program_id(0) == 0)
    def _():
        row, column = iotas(swapped.shape)
        wanted = ((row % 2) * chan_share + row // pair) * per_owner + (row % pair) // 2
        swapped[...] = jnp.where(column == wanted, 1.0, 0.0).astype(BF16)
        row, column = iotas(pickers.shape[1:])
        start = (column // share) * depth + column % share
        for b in range(members):
            pickers[b] = jnp.where(row == start + b * share, 1.0, 0.0).astype(BF16)

    turned = lax.dot_general(
        swapped[...],
        got[0].reshape(groups * depth, lanes),
        (((1,), (1,)), ((), ())),
        preferred_element_type=F32,
    ).astype(BF16)
    for b in range(members):
        lines = jnp.dot(turned, pickers[b], preferred_element_type=F32)
        for c in range(chan_share):
            block = lines[c * pair : (c + 1) * pair]
            out[b, c] = block.reshape(per_owner, 2, orders)


def local(fields, depth_kernel, mix_weight, legendre, truth, degree_order):
    ens_parts, groups = lax.axis_size("ens"), lax.axis_size("lat")
    ens_at, lat_at = lax.axis_index("ens"), lax.axis_index("lat")
    members, chans, rows, nlon = fields.shape
    _, orders, degrees = legendre.shape
    ens = members * ens_parts
    nlat = rows * groups
    share, per_owner, chan_share = orders // groups, degrees // groups, chans // ens_parts
    used = 2 * chan_share
    slots = up(used, 8)
    height = up(members * used, 8)
    span = up(orders, 128)
    size = depth_kernel.shape[1]
    halo = size // 2
    wide = up(nlon + 2 * halo, 128)
    depth = members * chans

    table = jnp.asarray(wave_table(nlon, orders, span))
    kernel = depth_kernel.transpose(1, 2, 0)
    flags = place()
    own = fields.transpose(0, 2, 1, 3)
    odd = lat_at % 2
    inner = lax.dynamic_slice_in_dim(own, (1 - odd) * (rows - halo), halo, 1)
    near = partner(inner, True)

    pick = np.zeros((2, members, ens_parts, height, chans), np.float32)
    for r in range(2):
        for b in range(members):
            for o in range(chans):
                at = b * used + r * chan_share + o % chan_share
                pick[r, b, o // chan_share, at, o] = 1.0
    pick = jnp.asarray(pick.reshape(2, members, ens_parts * height, chans).astype(jnp.bfloat16))

    vmem = pltpu.CompilerParams(vmem_limit_bytes=60 * 1024 * 1024)
    scalars = pl.BlockSpec(memory_space=pltpu.SMEM)
    whole = pl.BlockSpec(memory_space=pltpu.VMEM)
    grid_shape = (members, rows, chans, nlon)
    lined = jax.ShapeDtypeStruct((rows, depth, nlon), F32)
    edge = jax.ShapeDtypeStruct((halo, depth, nlon), BF16)
    taps_out = jax.ShapeDtypeStruct((size * size, depth, 128), BF16)

    def call(body, outs, scratch, work, *args):
        specs = [scalars if a is flags else whole for a in args]
        return pl.pallas_call(
            body,
            out_shape=outs,
            in_specs=specs,
            scratch_shapes=scratch,
            compiler_params=vmem,
            cost_estimate=pl.CostEstimate(
                flops=work, transcendentals=0, bytes_accessed=8 * rows * depth * nlon
            ),
        )(*args)

    def swap(x):
        flat = x.reshape((ens_parts * groups,) + x.shape[2:])
        flat = lax.all_to_all(flat, ("ens", "lat"), split_axis=0, concat_axis=0, tiled=True)
        return flat.reshape(x.shape)

    work = 2 * size * size * rows * depth * nlon
    partial, taps, mixer = call(
        prepare_kernel,
        (lined, taps_out, jax.ShapeDtypeStruct((2, ens_parts * height, depth), BF16)),
        [pltpu.VMEM((rows, depth, wide), BF16)],
        work,
        own,
        kernel,
        mix_weight,
        pick,
    )
    target = lax.dynamic_slice(
        truth, (ens_at * chan_share, 0, lat_at * share, 0), (chan_share, 2, share, degrees)
    )
    target = target.transpose(2, 1, 0, 3).reshape(share, used, degrees)
    target = jnp.pad(target, ((0, 0), (0, slots - used), (0, 0)))

    slab = legendre.reshape(rows, groups, share * degrees).transpose(1, 0, 2)
    line = math.gcd(rows * share * degrees, 128)
    slab = slab.reshape(groups, rows * share * degrees // line, line)
    late, partial = lax.optimization_barrier((own, partial))
    outer = lax.dynamic_slice_in_dim(late, odd * (rows - halo), halo, 1)
    far = partner(outer, False)

    def chunk(lines):
        return jax.ShapeDtypeStruct((ens_parts, groups, height, up(lines * share, 128)), BF16)

    half_scratch = [pltpu.VMEM((halo, depth, wide), BF16), pltpu.VMEM((halo, depth, nlon), BF16)]
    mixed, inner = call(
        near_kernel,
        (jax.ShapeDtypeStruct((halo, ens_parts * height, span), F32), edge),
        half_scratch,
        work // 2,
        flags,
        near,
        partial,
        taps,
        table,
        mixer,
    )
    slab, mixed = lax.optimization_barrier((slab, mixed))
    slab = lax.all_to_all(slab, "lat", split_axis=0, concat_axis=0, tiled=True)
    order_legendre = slab.reshape(nlat, share, degrees).transpose(1, 0, 2)
    sent, outer = call(
        functools.partial(far_kernel, share),
        (chunk(rows), edge),
        half_scratch,
        work // 2,
        flags,
        far,
        partial,
        taps,
        table,
        mixer,
        mixed,
    )
    got = swap(sent)
    near, far = partner(inner, True), partner(outer, False)
    back, grads = call(
        functools.partial(score_kernel, members, used, rows, halo),
        (
            chunk(rows + 2 * halo),
            jax.ShapeDtypeStruct((up(degrees, 128) // 128, share * ens * slots, 128), F32),
        ),
        [
            pltpu.VMEM((nlat * share, ens * slots), F32),
            pltpu.VMEM(((nlat + 2 * halo) * share, ens * slots), F32),
            pltpu.VMEM((degrees, degrees), BF16),
        ],
        work,
        got,
        order_legendre,
        target,
        degree_order.reshape(1, degrees),
    )
    returned = swap(back)
    packed = call(
        functools.partial(pack_kernel, members, used, per_owner),
        jax.ShapeDtypeStruct(
            (ens_parts, groups, members * share, up(used * per_owner, 128)), BF16
        ),
        [],
        work,
        grads,
    )
    owned = swap(packed)
    flipped = call(flip_kernel, taps_out, [], work // 8, kernel)
    grad_fields = call(
        functools.partial(backward_kernel, share),
        jax.ShapeDtypeStruct(grid_shape, BF16),
        [
            pltpu.VMEM((rows + 2 * halo, depth, wide), BF16),
            pltpu.VMEM((rows + 2 * halo, depth, nlon), F32),
            pltpu.VMEM((rows, depth, nlon), F32),
        ],
        work,
        flags,
        returned,
        near,
        far,
        inner,
        outer,
        flipped,
        mixer,
        table,
    )
    score_grad = pl.pallas_call(
        functools.partial(unpack_kernel, members),
        out_shape=jax.ShapeDtypeStruct((members, chans, per_owner, 2, orders), F32),
        grid=(ens_parts,),
        in_specs=[pl.BlockSpec((1,) + owned.shape[1:], lambda e: (e, 0, 0, 0))],
        out_specs=pl.BlockSpec(
            (members, chan_share, per_owner, 2, orders), lambda e: (0, e, 0, 0, 0)
        ),
        scratch_shapes=[
            pltpu.VMEM((used * per_owner, owned.shape[3]), BF16),
            pltpu.VMEM((members, groups * owned.shape[2], orders), BF16),
        ],
        compiler_params=vmem,
        cost_estimate=pl.CostEstimate(flops=work, transcendentals=0, bytes_accessed=1),
        name="unpack",
    )(owned)
    return grad_fields.transpose(0, 2, 1, 3), score_grad.transpose(0, 1, 3, 4, 2)


def solution(mesh):
    placed = (P("ens", None, "lat", None), P(), P(), P("lat", None, None), P(), P())

    return jax.shard_map(
        local,
        mesh=mesh,
        in_specs=placed,
        out_specs=(P("ens", None, "lat", None), P("ens", None, None, None, "lat")),
        check_vma=False,
    )
```

```python
import functools
import math

import jax
import jax.numpy as jnp
import numpy as np
from jax import lax
from jax.experimental import pallas as pl
from jax.experimental.pallas import tpu as pltpu
from jax.sharding import PartitionSpec as P


smooth_width = 0.5
TILE = 16
F32 = jnp.float32
BF16 = jnp.bfloat16


def up(value, step):
    return -(-value // step) * step


def wave_table(nlon, orders, span):
    columns = np.arange(nlon, dtype=np.int64)
    number = np.arange(orders, dtype=np.int64)
    angles = (columns[:, None] * number[None, :] % nlon) * (2.0 * math.pi / nlon)
    table = np.zeros((nlon, 2, span), np.float32)
    for part, values in enumerate((np.cos(angles), -np.sin(angles))):
        table[:, part, :orders] = values / math.sqrt(nlon)
    return table.reshape(nlon, 2 * span).astype(jnp.bfloat16)


def partner(edge, pair):
    count = lax.axis_size("lat")
    if pair:
        steps = [(i, i ^ 1) for i in range(count)]
    else:
        steps = [(i, (i + (1 if i % 2 else -1)) % count) for i in range(count)]
    return lax.ppermute(edge, "lat", steps)


def place():
    at, count = lax.axis_index("lat"), lax.axis_size("lat")
    return jnp.stack([at % 2, (at > 0) & (at < count - 1)]).astype(jnp.int32)


def fill_row(padded, row, value, half):
    depth, nlon = value.shape
    wide = padded.shape[-1]
    base = nlon // 128 * 128
    tail = [value[:, base:], value[:, :half]]
    if wide > nlon + 2 * half:
        tail.append(jnp.zeros((depth, wide - nlon - 2 * half), value.dtype))
    tail.append(value[:, nlon - half :])
    padded[row, :, :base] = value[:, :base].astype(padded.dtype)
    padded[row, :, base:] = jnp.concatenate(tail, axis=-1).astype(padded.dtype)


def tap_sum(padded, taps, c0, lines, size):
    wide = padded.shape[-1]
    total = None
    for q in range(size):
        part = None
        for row, p in lines:
            weight = jnp.tile(taps[p * size + q, pl.ds(c0, TILE), :], (1, wide // 128))
            term = weight * padded[row, pl.ds(c0, TILE), :]
            part = term if part is None else part + term
        part = part.astype(F32)
        shift = (size // 2 - q) % wide
        if shift:
            part = pltpu.roll(part, shift, 1)
        total = part if total is None else total + part
    return total


def spread_taps(kernel, taps, flip):
    size, _, chans = kernel.shape
    for p in range(size):
        plane = kernel[p].T
        for q in range(size):
            at = p * size + q
            at = size * size - 1 - at if flip else at
            value = jnp.broadcast_to(plane[:, q : q + 1], (chans, 128))
            value = jnp.concatenate([value] * (taps.shape[1] // chans), axis=0)
            taps[at] = value.astype(taps.dtype)


def joined(block, row):
    return jnp.concatenate([block[b, row].astype(F32) for b in range(block.shape[0])], axis=0)


def gelu_pair(x):
    scale = math.sqrt(2.0 / math.pi)
    square = x * x
    t = jnp.tanh(scale * x * (1.0 + 0.044715 * square))
    half = 0.5 * (1.0 + t)
    slope = half + 0.5 * x * (1.0 - t * t) * (scale * (1.0 + 3 * 0.044715 * square))
    return x * half, slope


def prepare_kernel(own, kernel, weight, pick, partial, taps, mixer, padded):
    members, rows, chans, nlon = own.shape
    depth = members * chans
    size = kernel.shape[0]
    half = size // 2
    spread_taps(kernel, taps, False)
    for row in range(rows):
        fill_row(padded, row, joined(own, row), half)

    @pl.loop(0, depth // TILE)
    def _(ct):
        c0 = pl.multiple_of(ct * TILE, TILE)
        for i in range(rows):
            lines = [(i + p - half, p) for p in range(size) if 0 <= i + p - half < rows]
            total = tap_sum(padded, taps, c0, lines, size)
            total = total + padded[i, pl.ds(c0, TILE), :].astype(F32)
            partial[i, pl.ds(c0, TILE), :] = total[:, :nlon]

    for r in range(2):
        lines = []
        for b in range(members):
            lines.append(jnp.dot(pick[r, b], weight[...], preferred_element_type=F32))
        mixer[r] = jnp.concatenate(lines, axis=1).astype(BF16)


def finish_rows(lower, present, edge, partial, taps, table, mixer, slope, padded, act):
    rows, depth, nlon = partial.shape
    size = math.isqrt(taps.shape[0])
    half = size // 2
    span = table.shape[1] // 2
    for row in range(half):
        at = jnp.where(lower, row, half - 1 - row)
        value = joined(edge, at)
        if present is not None:
            value = jnp.where(present, value, jnp.zeros_like(value))
        fill_row(padded, row, value, half)

    @pl.loop(0, depth // TILE)
    def _(ct):
        c0 = pl.multiple_of(ct * TILE, TILE)
        for j in range(half):
            lines = [
                (row, jnp.where(lower, row - j, size - 1 - (row - j))) for row in range(j, half)
            ]
            at = jnp.where(lower, j, half - 1 - j)
            value = partial[jnp.where(lower, j, rows - 1 - j), pl.ds(c0, TILE), :]
            value = value + tap_sum(padded, taps, c0, lines, size)[:, :nlon]
            value, grad = gelu_pair(value)
            act[at, pl.ds(c0, TILE), :] = value.astype(BF16)
            slope[at, pl.ds(c0, TILE), :] = grad.astype(BF16)

    flat = act[...].reshape(half * depth, nlon)
    spectral = jnp.dot(flat, table[...], preferred_element_type=F32).astype(BF16)
    mixed = []
    for j in range(half):
        line = spectral[j * depth : (j + 1) * depth]
        mixed.append(
            jnp.dot(mixer[0], line[:, :span], preferred_element_type=F32)
            + jnp.dot(mixer[1], line[:, span:], preferred_element_type=F32)
        )
    return mixed


def near_kernel(flags, edge, partial, taps, table, mixer, mixed, slope, padded, act):
    lines = finish_rows(flags[0] == 1, None, edge, partial, taps, table, mixer, slope, padded, act)
    for j, line in enumerate(lines):
        mixed[j] = line


def far_kernel(share, flags, edge, partial, taps, table, mixer, nearer, out, slope, padded, act):
    owners, groups, height, lanes = out.shape
    lines = finish_rows(
        flags[0] != 1, flags[1] == 1, edge, partial, taps, table, mixer, slope, padded, act
    )
    lines = [nearer[j] for j in range(nearer.shape[0])] + lines
    for t in range(groups):
        pieces = [x[:, t * share : (t + 1) * share] for x in lines]
        if lanes > len(lines) * share:
            pieces.append(jnp.zeros((owners * height, lanes - len(lines) * share), F32))
        block = jnp.concatenate(pieces, axis=1)
        for e in range(owners):
            out[e, t] = block[e * height : (e + 1) * height].astype(BF16)


def flip_kernel(kernel, taps):
    spread_taps(kernel, taps, True)


def soft_sign(gaps):
    return gaps * lax.rsqrt(gaps * gaps + smooth_width * smooth_width)


def score_kernel(members, used, rows, halo, got, legendre, target, order, back, grads, spread, gather, picked):
    owners, groups, height, lanes = got.shape
    orders, nlat, degrees = legendre.shape
    slots = target.shape[1]
    ens = owners * members
    for t in range(groups):
        pieces = []
        for e in range(owners):
            block = got[e, t].astype(F32)
            for b in range(members):
                pieces.append(block[b * used : (b + 1) * used])
                if slots > used:
                    pieces.append(jnp.zeros((slots - used, lanes), F32))
        block = jnp.concatenate(pieces, axis=0).T
        at, part = t * rows * orders, halo * orders
        first, second = (at, at + part) if t % 2 else (at + part, at)
        spread[first : first + part, :] = block[:part]
        spread[second : second + part, :] = block[part : 2 * part]
    reorder = jnp.where(
        lax.broadcasted_iota(jnp.int32, (degrees, degrees), 0) == order[...], 1.0, 0.0
    )
    picked[...] = reorder.astype(BF16)
    edge = halo * orders
    gather[:edge, :] = jnp.zeros((edge, ens * slots), F32)
    gather[edge + nlat * orders :, :] = jnp.zeros((edge, ens * slots), F32)

    def score(values, truth):
        own = [values[k * slots : (k + 1) * slots] for k in range(ens)]
        sums = [None] * ens
        for k in range(ens):
            for n in range(k + 1, ens):
                sign = soft_sign(own[k] - own[n])
                sums[k] = sign if sums[k] is None else sums[k] + sign
                sums[n] = -sign if sums[n] is None else sums[n] - sign
        return jnp.concatenate(
            [
                soft_sign(own[k] - truth) * (1.0 / ens) - sums[k] * (1.0 / (ens * (ens - 1)))
                for k in range(ens)
            ],
            axis=0,
        )

    tail = degrees % 128
    packs = tail > 0 and 128 % tail == 0 and orders % (128 // tail) == 0
    step = 128 // tail if packs else 1
    body = degrees - tail if packs else degrees

    @pl.loop(0, orders // step)
    def _(trip):
        numbers = [trip * step + j for j in range(step)]
        coeffs = [
            lax.dot_general(
                spread[pl.ds(m, nlat, stride=orders), :].astype(BF16),
                legendre[m],
                (((0,), (0,)), ((), ())),
                preferred_element_type=F32,
            )
            for m in numbers
        ]
        truths = [target[m].astype(F32) for m in numbers]
        scored = [score(x[:, :body], y[:, :body]) for x, y in zip(coeffs, truths)]
        if packs:
            rest = score(
                jnp.concatenate([x[:, body:] for x in coeffs], axis=1),
                jnp.concatenate([y[:, body:] for y in truths], axis=1),
            )
            scored = [
                jnp.concatenate([x, rest[:, j * tail : (j + 1) * tail]], axis=1)
                for j, x in enumerate(scored)
            ]
        for m, grad in zip(numbers, scored):
            grad = grad.astype(BF16)
            gather[pl.ds(edge + m, nlat, stride=orders), :] = lax.dot_general(
                legendre[m], grad, (((1,), (1,)), ((), ())), preferred_element_type=F32
            )
            at = pl.multiple_of(m * ens * slots, 8)
            ordered = jnp.dot(grad, picked[...], preferred_element_type=F32)
            for j in range(grads.shape[0]):
                last = min(degrees, (j + 1) * 128)
                grads[j, pl.ds(at, ens * slots), : last - j * 128] = ordered[:, j * 128 : last]

    wide = back.shape[3]
    tall = (rows + 2 * halo) * orders
    for t in range(groups):
        at = t * rows * orders
        block = gather[at : at + tall, :]
        if wide > tall:
            block = jnp.concatenate([block, jnp.zeros((wide - tall, ens * slots), F32)], axis=0)
        block = block.T
        for e in range(owners):
            pieces = []
            for b in range(members):
                at = (e * members + b) * slots
                pieces.append(block[at : at + used])
            if height > members * used:
                pieces.append(jnp.zeros((height - members * used, wide), F32))
            back[e, t] = jnp.concatenate(pieces, axis=0).astype(BF16)


def backward_kernel(share, flags, got, near, far, inner, outer, taps, mixer, table, out, padded, flat, stage):
    owners, groups, height, _ = got.shape
    half, depth, nlon = inner.shape
    members, rows, chans, _ = out.shape
    size = math.isqrt(taps.shape[0])
    span = table.shape[1] // 2
    total = rows + 2 * half
    blocks = [
        jnp.concatenate([got[e, t].astype(F32) for e in range(owners)], axis=0) for t in range(groups)
    ]
    lines = []
    for i in range(total):
        pieces = [x[:, i * share : (i + 1) * share] for x in blocks]
        pieces.append(jnp.zeros((owners * height, span - groups * share), F32))
        line = jnp.concatenate(pieces, axis=1).astype(BF16)
        lines.append(
            jnp.concatenate(
                [
                    lax.dot_general(
                        mixer[r], line, (((0,), (0,)), ((), ())), preferred_element_type=F32
                    ).astype(BF16)
                    for r in range(2)
                ],
                axis=1,
            )
        )
    flat[...] = lax.dot_general(
        jnp.concatenate(lines, axis=0),
        table[...],
        (((1,), (1,)), ((), ())),
        preferred_element_type=F32,
    ).reshape(flat.shape)
    odd = flags[0] == 1
    pairs = ((near, far), (inner, outer), (outer, inner), (far, near))
    for part, (one, other) in enumerate(pairs):
        for row in range(half):
            at = part * half + row
            slope = jnp.where(odd, one[row].astype(F32), other[row].astype(F32))
            fill_row(padded, at, flat[at] * slope, half)

    @pl.loop(0, depth // TILE)
    def _(ct):
        c0 = pl.multiple_of(ct * TILE, TILE)

        @pl.loop(0, rows)
        def _(i):
            value = tap_sum(padded, taps, c0, [(i + p, p) for p in range(size)], size)
            value = value + padded[i + half, pl.ds(c0, TILE), :].astype(F32)
            stage[i, pl.ds(c0, TILE), :] = value[:, :nlon]

    for b in range(members):
        for i in range(rows):
            out[b, i] = stage[i, b * chans : (b + 1) * chans, :].astype(BF16)


def pack_kernel(members, used, per_owner, grads, out):
    owners, groups, depth, lanes = out.shape
    share = depth // members
    stride = grads.shape[1] // share
    slots = stride // (owners * members)
    for e in range(owners):
        for b in range(members):
            at = (e * members + b) * slots
            planes = [
                jnp.concatenate(
                    [grads[j, pl.ds(at + s, share, stride=stride), :] for j in range(grads.shape[0])],
                    axis=1,
                )
                for s in range(used)
            ]
            for t in range(groups):
                pieces = [x[:, t * per_owner : (t + 1) * per_owner] for x in planes]
                if lanes > used * per_owner:
                    pieces.append(jnp.zeros((share, lanes - used * per_owner), F32))
                out[e, t, b * share : (b + 1) * share, :] = jnp.concatenate(pieces, axis=1).astype(BF16)


def unpack_kernel(members, got, out):
    owners, groups, depth, lanes = got.shape
    _, chans, per_owner, _, orders = out.shape
    share, chan_share = depth // members, chans // owners
    pair = 2 * per_owner

    def iotas(shape):
        return (lax.broadcasted_iota(jnp.int32, shape, d) for d in range(2))

    row, column = iotas((chan_share * pair, lanes))
    wanted = ((row % 2) * chan_share + row // pair) * per_owner + (row % pair) // 2
    swapped = jnp.where(column == wanted, 1.0, 0.0).astype(BF16)
    row, column = iotas((groups * depth, orders))
    start = (column // share) * depth + column % share
    pickers = [jnp.where(row == start + b * share, 1.0, 0.0).astype(BF16) for b in range(members)]
    for e in range(owners):
        turned = lax.dot_general(
            swapped,
            got[e].reshape(groups * depth, lanes),
            (((1,), (1,)), ((), ())),
            preferred_element_type=F32,
        ).astype(BF16)
        for b in range(members):
            lines = jnp.dot(turned, pickers[b], preferred_element_type=F32)
            for c in range(chan_share):
                block = lines[c * pair : (c + 1) * pair]
                out[b, e * chan_share + c] = block.reshape(per_owner, 2, orders)


def local(fields, depth_kernel, mix_weight, legendre, truth, degree_order):
    ens_parts, groups = lax.axis_size("ens"), lax.axis_size("lat")
    ens_at, lat_at = lax.axis_index("ens"), lax.axis_index("lat")
    members, chans, rows, nlon = fields.shape
    _, orders, degrees = legendre.shape
    ens = members * ens_parts
    nlat = rows * groups
    share, per_owner, chan_share = orders // groups, degrees // groups, chans // ens_parts
    used = 2 * chan_share
    slots = up(used, 8)
    height = up(members * used, 8)
    span = up(orders, 128)
    size = depth_kernel.shape[1]
    halo = size // 2
    wide = up(nlon + 2 * halo, 128)
    depth = members * chans

    table = jnp.asarray(wave_table(nlon, orders, span))
    kernel = depth_kernel.transpose(1, 2, 0)
    flags = place()
    own = fields.transpose(0, 2, 1, 3)
    odd = lat_at % 2
    inner = lax.dynamic_slice_in_dim(own, (1 - odd) * (rows - halo), halo, 1)
    near = partner(inner, True)

    pick = np.zeros((2, members, ens_parts, height, chans), np.float32)
    for r in range(2):
        for b in range(members):
            for o in range(chans):
                at = b * used + r * chan_share + o % chan_share
                pick[r, b, o // chan_share, at, o] = 1.0
    pick = jnp.asarray(pick.reshape(2, members, ens_parts * height, chans).astype(jnp.bfloat16))

    vmem = pltpu.CompilerParams(vmem_limit_bytes=60 * 1024 * 1024)
    scalars = pl.BlockSpec(memory_space=pltpu.SMEM)
    whole = pl.BlockSpec(memory_space=pltpu.VMEM)
    grid_shape = (members, rows, chans, nlon)
    lined = jax.ShapeDtypeStruct((rows, depth, nlon), F32)
    edge = jax.ShapeDtypeStruct((halo, depth, nlon), BF16)
    taps_out = jax.ShapeDtypeStruct((size * size, depth, 128), BF16)

    def call(body, outs, scratch, work, *args):
        specs = [scalars if a is flags else whole for a in args]
        return pl.pallas_call(
            body,
            out_shape=outs,
            in_specs=specs,
            scratch_shapes=scratch,
            compiler_params=vmem,
            cost_estimate=pl.CostEstimate(
                flops=work, transcendentals=0, bytes_accessed=8 * rows * depth * nlon
            ),
        )(*args)

    def swap(x):
        flat = x.reshape((ens_parts * groups,) + x.shape[2:])
        flat = lax.all_to_all(flat, ("ens", "lat"), split_axis=0, concat_axis=0, tiled=True)
        return flat.reshape(x.shape)

    work = 2 * size * size * rows * depth * nlon
    partial, taps, mixer = call(
        prepare_kernel,
        (lined, taps_out, jax.ShapeDtypeStruct((2, ens_parts * height, depth), BF16)),
        [pltpu.VMEM((rows, depth, wide), BF16)],
        work,
        own,
        kernel,
        mix_weight,
        pick,
    )
    target = lax.dynamic_slice(
        truth, (ens_at * chan_share, 0, lat_at * share, 0), (chan_share, 2, share, degrees)
    )
    target = target.transpose(2, 1, 0, 3).reshape(share, used, degrees)
    target = jnp.pad(target, ((0, 0), (0, slots - used), (0, 0)))

    slab = legendre.reshape(rows, groups, share * degrees).transpose(1, 0, 2)
    line = math.gcd(rows * share * degrees, 128)
    slab = slab.reshape(groups, rows * share * degrees // line, line)
    late, partial = lax.optimization_barrier((own, partial))
    outer = lax.dynamic_slice_in_dim(late, odd * (rows - halo), halo, 1)
    far = partner(outer, False)

    def chunk(lines):
        return jax.ShapeDtypeStruct((ens_parts, groups, height, up(lines * share, 128)), BF16)

    half_scratch = [pltpu.VMEM((halo, depth, wide), BF16), pltpu.VMEM((halo, depth, nlon), BF16)]
    mixed, inner = call(
        near_kernel,
        (jax.ShapeDtypeStruct((halo, ens_parts * height, span), F32), edge),
        half_scratch,
        work // 2,
        flags,
        near,
        partial,
        taps,
        table,
        mixer,
    )
    slab, mixed = lax.optimization_barrier((slab, mixed))
    slab = lax.all_to_all(slab, "lat", split_axis=0, concat_axis=0, tiled=True)
    order_legendre = slab.reshape(nlat, share, degrees).transpose(1, 0, 2)
    sent, outer = call(
        functools.partial(far_kernel, share),
        (chunk(rows), edge),
        half_scratch,
        work // 2,
        flags,
        far,
        partial,
        taps,
        table,
        mixer,
        mixed,
    )
    got = swap(sent)
    near, far = partner(inner, True), partner(outer, False)
    back, grads = call(
        functools.partial(score_kernel, members, used, rows, halo),
        (
            chunk(rows + 2 * halo),
            jax.ShapeDtypeStruct((up(degrees, 128) // 128, share * ens * slots, 128), F32),
        ),
        [
            pltpu.VMEM((nlat * share, ens * slots), F32),
            pltpu.VMEM(((nlat + 2 * halo) * share, ens * slots), F32),
            pltpu.VMEM((degrees, degrees), BF16),
        ],
        work,
        got,
        order_legendre,
        target,
        degree_order.reshape(1, degrees),
    )
    returned = swap(back)
    packed = call(
        functools.partial(pack_kernel, members, used, per_owner),
        jax.ShapeDtypeStruct(
            (ens_parts, groups, members * share, up(used * per_owner, 128)), BF16
        ),
        [],
        work,
        grads,
    )
    owned = swap(packed)
    flipped = call(flip_kernel, taps_out, [], work // 8, kernel)
    grad_fields = call(
        functools.partial(backward_kernel, share),
        jax.ShapeDtypeStruct(grid_shape, BF16),
        [
            pltpu.VMEM((rows + 2 * halo, depth, wide), BF16),
            pltpu.VMEM((rows + 2 * halo, depth, nlon), F32),
            pltpu.VMEM((rows, depth, nlon), F32),
        ],
        work,
        flags,
        returned,
        near,
        far,
        inner,
        outer,
        flipped,
        mixer,
        table,
    )
    score_grad = call(
        functools.partial(unpack_kernel, members),
        jax.ShapeDtypeStruct((members, chans, per_owner, 2, orders), F32),
        [],
        work,
        owned,
    )
    return grad_fields.transpose(0, 2, 1, 3), score_grad.transpose(0, 1, 3, 4, 2)


def solution(mesh):
    placed = (P("ens", None, "lat", None), P(), P(), P("lat", None, None), P(), P())

    return jax.shard_map(
        local,
        mesh=mesh,
        in_specs=placed,
        out_specs=(P("ens", None, "lat", None), P("ens", None, None, None, "lat")),
        check_vma=False,
    )
```

```python
import functools
import math

import jax
import jax.numpy as jnp
import numpy as np
from jax import lax
from jax.experimental import pallas as pl
from jax.experimental.pallas import tpu as pltpu
from jax.sharding import PartitionSpec as P


smooth_width = 0.5
TILE = 16
F32 = jnp.float32
BF16 = jnp.bfloat16


def up(value, step):
    return -(-value // step) * step


def wave_table(nlon, orders, span):
    columns = np.arange(nlon, dtype=np.int64)
    number = np.arange(orders, dtype=np.int64)
    angles = (columns[:, None] * number[None, :] % nlon) * (2.0 * math.pi / nlon)
    table = np.zeros((nlon, 2, span), np.float32)
    for part, values in enumerate((np.cos(angles), -np.sin(angles))):
        table[:, part, :orders] = values / math.sqrt(nlon)
    return table.reshape(nlon, 2 * span).astype(jnp.bfloat16)


def pairs_of(count, shift):
    return [[i, (i + 1) % count] for i in range(shift, count, 2)]


def partner(edge, near):
    steps = []
    for one, other in pairs_of(lax.axis_size("lat"), 0 if near else 1):
        steps += [(one, other), (other, one)]
    return lax.ppermute(edge, "lat", steps)


def place():
    at, count = lax.axis_index("lat"), lax.axis_size("lat")
    return jnp.stack([at % 2, (at > 0) & (at < count - 1)]).astype(jnp.int32)


def fill_row(padded, row, value, half):
    depth, nlon = value.shape
    wide = padded.shape[-1]
    base = nlon // 128 * 128
    tail = [value[:, base:], value[:, :half]]
    if wide > nlon + 2 * half:
        tail.append(jnp.zeros((depth, wide - nlon - 2 * half), value.dtype))
    tail.append(value[:, nlon - half :])
    padded[row, :, :base] = value[:, :base].astype(padded.dtype)
    padded[row, :, base:] = jnp.concatenate(tail, axis=-1).astype(padded.dtype)


def tap_sum(padded, taps, c0, lines, size):
    wide = padded.shape[-1]
    total = None
    for q in range(size):
        part = None
        for row, p in lines:
            weight = jnp.tile(taps[p * size + q, pl.ds(c0, TILE), :], (1, wide // 128))
            term = weight * padded[row, pl.ds(c0, TILE), :]
            part = term if part is None else part + term
        part = part.astype(F32)
        shift = (size // 2 - q) % wide
        if shift:
            part = pltpu.roll(part, shift, 1)
        total = part if total is None else total + part
    return total


def spread_taps(kernel, taps, flip):
    size, _, chans = kernel.shape
    for p in range(size):
        plane = kernel[p].T
        for q in range(size):
            at = p * size + q
            at = size * size - 1 - at if flip else at
            value = jnp.broadcast_to(plane[:, q : q + 1], (chans, 128))
            value = jnp.concatenate([value] * (taps.shape[1] // chans), axis=0)
            taps[at] = value.astype(taps.dtype)


def joined(block, row):
    return jnp.concatenate([block[b, row].astype(F32) for b in range(block.shape[0])], axis=0)


def gelu_pair(x):
    scale = math.sqrt(2.0 / math.pi)
    square = x * x
    t = jnp.tanh(scale * x * (1.0 + 0.044715 * square))
    half = 0.5 * (1.0 + t)
    slope = half + 0.5 * x * (1.0 - t * t) * (scale * (1.0 + 3 * 0.044715 * square))
    return x * half, slope


def prepare_kernel(own, kernel, weight, pick, partial, taps, mixer, padded):
    members, rows, chans, nlon = own.shape
    depth = members * chans
    size = kernel.shape[0]
    half = size // 2
    spread_taps(kernel, taps, False)
    for row in range(rows):
        fill_row(padded, row, joined(own, row), half)

    @pl.loop(0, depth // TILE)
    def _(ct):
        c0 = pl.multiple_of(ct * TILE, TILE)
        for i in range(rows):
            lines = [(i + p - half, p) for p in range(size) if 0 <= i + p - half < rows]
            total = tap_sum(padded, taps, c0, lines, size)
            total = total + padded[i, pl.ds(c0, TILE), :].astype(F32)
            partial[i, pl.ds(c0, TILE), :] = total[:, :nlon]

    for r in range(2):
        lines = []
        for b in range(members):
            lines.append(jnp.dot(pick[r, b], weight[...], preferred_element_type=F32))
        mixer[r] = jnp.concatenate(lines, axis=1).astype(BF16)


def finish_rows(lower, present, edge, partial, taps, table, mixer, slope, padded, act):
    rows, depth, nlon = partial.shape
    size = math.isqrt(taps.shape[0])
    half = size // 2
    span = table.shape[1] // 2
    for row in range(half):
        at = jnp.where(lower, row, half - 1 - row)
        value = joined(edge, at)
        if present is not None:
            value = jnp.where(present, value, jnp.zeros_like(value))
        fill_row(padded, row, value, half)

    @pl.loop(0, depth // TILE)
    def _(ct):
        c0 = pl.multiple_of(ct * TILE, TILE)
        for j in range(half):
            lines = [
                (row, jnp.where(lower, row - j, size - 1 - (row - j))) for row in range(j, half)
            ]
            at = jnp.where(lower, j, half - 1 - j)
            value = partial[jnp.where(lower, j, rows - 1 - j), pl.ds(c0, TILE), :]
            value = value + tap_sum(padded, taps, c0, lines, size)[:, :nlon]
            value, grad = gelu_pair(value)
            act[at, pl.ds(c0, TILE), :] = value.astype(BF16)
            slope[at, pl.ds(c0, TILE), :] = grad.astype(BF16)

    flat = act[...].reshape(half * depth, nlon)
    spectral = jnp.dot(flat, table[...], preferred_element_type=F32).astype(BF16)
    mixed = []
    for j in range(half):
        line = spectral[j * depth : (j + 1) * depth]
        mixed.append(
            jnp.dot(mixer[0], line[:, :span], preferred_element_type=F32)
            + jnp.dot(mixer[1], line[:, span:], preferred_element_type=F32)
        )
    return mixed


def near_kernel(flags, edge, partial, taps, table, mixer, mixed, slope, padded, act):
    odd = flags[0]
    lines = finish_rows(odd == 1, None, edge.at[1 - odd], partial, taps, table, mixer, slope, padded, act)
    for j, line in enumerate(lines):
        mixed[j] = line


def far_kernel(share, flags, edge, partial, taps, table, mixer, nearer, out, slope, padded, act):
    owners, groups, height, lanes = out.shape
    lines = finish_rows(
        flags[0] != 1, flags[1] == 1, edge, partial, taps, table, mixer, slope, padded, act
    )
    lines = [nearer[j] for j in range(nearer.shape[0])] + lines
    for t in range(groups):
        pieces = [x[:, t * share : (t + 1) * share] for x in lines]
        if lanes > len(lines) * share:
            pieces.append(jnp.zeros((owners * height, lanes - len(lines) * share), F32))
        block = jnp.concatenate(pieces, axis=1)
        for e in range(owners):
            out[e, t] = block[e * height : (e + 1) * height].astype(BF16)


def flip_kernel(kernel, taps):
    spread_taps(kernel, taps, True)


def soft_sign(gaps):
    return gaps * lax.rsqrt(gaps * gaps + smooth_width * smooth_width)


def score_kernel(members, used, rows, halo, got, legendre, target, order, back, grads, spread, gather, picked):
    owners, groups, height, lanes = got.shape
    orders, nlat, degrees = legendre.shape
    slots = target.shape[1]
    ens = owners * members
    for t in range(groups):
        pieces = []
        for e in range(owners):
            block = got[e, t].astype(F32)
            for b in range(members):
                pieces.append(block[b * used : (b + 1) * used])
                if slots > used:
                    pieces.append(jnp.zeros((slots - used, lanes), F32))
        block = jnp.concatenate(pieces, axis=0).T
        at, part = t * rows * orders, halo * orders
        first, second = (at, at + part) if t % 2 else (at + part, at)
        spread[first : first + part, :] = block[:part]
        spread[second : second + part, :] = block[part : 2 * part]
    reorder = jnp.where(
        lax.broadcasted_iota(jnp.int32, (degrees, degrees), 0) == order[...], 1.0, 0.0
    )
    picked[...] = reorder.astype(BF16)
    edge = halo * orders
    gather[:edge, :] = jnp.zeros((edge, ens * slots), F32)
    gather[edge + nlat * orders :, :] = jnp.zeros((edge, ens * slots), F32)

    def score(values, truth):
        own = [values[k * slots : (k + 1) * slots] for k in range(ens)]
        sums = [None] * ens
        for k in range(ens):
            for n in range(k + 1, ens):
                sign = soft_sign(own[k] - own[n])
                sums[k] = sign if sums[k] is None else sums[k] + sign
                sums[n] = -sign if sums[n] is None else sums[n] - sign
        return jnp.concatenate(
            [
                soft_sign(own[k] - truth) * (1.0 / ens) - sums[k] * (1.0 / (ens * (ens - 1)))
                for k in range(ens)
            ],
            axis=0,
        )

    tail = degrees % 128
    packs = tail > 0 and 128 % tail == 0 and orders % (128 // tail) == 0
    step = 128 // tail if packs else 1
    body = degrees - tail if packs else degrees

    @pl.loop(0, orders // step)
    def _(trip):
        numbers = [trip * step + j for j in range(step)]
        coeffs = [
            lax.dot_general(
                spread[pl.ds(m, nlat, stride=orders), :].astype(BF16),
                legendre[m],
                (((0,), (0,)), ((), ())),
                preferred_element_type=F32,
            )
            for m in numbers
        ]
        truths = [target[m].astype(F32) for m in numbers]
        scored = [score(x[:, :body], y[:, :body]) for x, y in zip(coeffs, truths)]
        if packs:
            rest = score(
                jnp.concatenate([x[:, body:] for x in coeffs], axis=1),
                jnp.concatenate([y[:, body:] for y in truths], axis=1),
            )
            scored = [
                jnp.concatenate([x, rest[:, j * tail : (j + 1) * tail]], axis=1)
                for j, x in enumerate(scored)
            ]
        for m, grad in zip(numbers, scored):
            grad = grad.astype(BF16)
            gather[pl.ds(edge + m, nlat, stride=orders), :] = lax.dot_general(
                legendre[m], grad, (((1,), (1,)), ((), ())), preferred_element_type=F32
            )
            at = pl.multiple_of(m * ens * slots, 8)
            ordered = jnp.dot(grad, picked[...], preferred_element_type=F32)
            for j in range(grads.shape[0]):
                last = min(degrees, (j + 1) * 128)
                grads[j, pl.ds(at, ens * slots), : last - j * 128] = ordered[:, j * 128 : last]

    wide = back.shape[3]
    tall = (rows + 2 * halo) * orders
    for t in range(groups):
        at = t * rows * orders
        block = gather[at : at + tall, :]
        if wide > tall:
            block = jnp.concatenate([block, jnp.zeros((wide - tall, ens * slots), F32)], axis=0)
        block = block.T
        for e in range(owners):
            pieces = []
            for b in range(members):
                at = (e * members + b) * slots
                pieces.append(block[at : at + used])
            if height > members * used:
                pieces.append(jnp.zeros((height - members * used, wide), F32))
            back[e, t] = jnp.concatenate(pieces, axis=0).astype(BF16)


def backward_kernel(share, flags, got, near, far, inner, outer, taps, mixer, table, out, padded, flat, stage):
    owners, groups, height, _ = got.shape
    half, depth, nlon = inner.shape
    members, rows, chans, _ = out.shape
    size = math.isqrt(taps.shape[0])
    span = table.shape[1] // 2
    total = rows + 2 * half
    blocks = [
        jnp.concatenate([got[e, t].astype(F32) for e in range(owners)], axis=0) for t in range(groups)
    ]
    lines = []
    for i in range(total):
        pieces = [x[:, i * share : (i + 1) * share] for x in blocks]
        pieces.append(jnp.zeros((owners * height, span - groups * share), F32))
        line = jnp.concatenate(pieces, axis=1).astype(BF16)
        lines.append(
            jnp.concatenate(
                [
                    lax.dot_general(
                        mixer[r], line, (((0,), (0,)), ((), ())), preferred_element_type=F32
                    ).astype(BF16)
                    for r in range(2)
                ],
                axis=1,
            )
        )
    flat[...] = lax.dot_general(
        jnp.concatenate(lines, axis=0),
        table[...],
        (((1,), (1,)), ((), ())),
        preferred_element_type=F32,
    ).reshape(flat.shape)
    odd = flags[0] == 1
    pairs = ((near, far), (inner, outer), (outer, inner), (far, near))
    for part, (one, other) in enumerate(pairs):
        for row in range(half):
            at = part * half + row
            slope = jnp.where(odd, one[row].astype(F32), other[row].astype(F32))
            fill_row(padded, at, flat[at] * slope, half)

    @pl.loop(0, depth // TILE)
    def _(ct):
        c0 = pl.multiple_of(ct * TILE, TILE)

        @pl.loop(0, rows)
        def _(i):
            value = tap_sum(padded, taps, c0, [(i + p, p) for p in range(size)], size)
            value = value + padded[i + half, pl.ds(c0, TILE), :].astype(F32)
            stage[i, pl.ds(c0, TILE), :] = value[:, :nlon]

    for b in range(members):
        for i in range(rows):
            out[b, i] = stage[i, b * chans : (b + 1) * chans, :].astype(BF16)


def pack_kernel(members, used, per_owner, grads, out):
    owners, groups, depth, lanes = out.shape
    share = depth // members
    stride = grads.shape[1] // share
    slots = stride // (owners * members)
    for e in range(owners):
        for b in range(members):
            at = (e * members + b) * slots
            planes = [
                jnp.concatenate(
                    [grads[j, pl.ds(at + s, share, stride=stride), :] for j in range(grads.shape[0])],
                    axis=1,
                )
                for s in range(used)
            ]
            for t in range(groups):
                pieces = [x[:, t * per_owner : (t + 1) * per_owner] for x in planes]
                if lanes > used * per_owner:
                    pieces.append(jnp.zeros((share, lanes - used * per_owner), F32))
                out[e, t, b * share : (b + 1) * share, :] = jnp.concatenate(pieces, axis=1).astype(BF16)


def unpack_kernel(members, got, out):
    owners, groups, depth, lanes = got.shape
    _, chans, per_owner, _, orders = out.shape
    share, chan_share = depth // members, chans // owners
    pair = 2 * per_owner

    def iotas(shape):
        return (lax.broadcasted_iota(jnp.int32, shape, d) for d in range(2))

    row, column = iotas((chan_share * pair, lanes))
    wanted = ((row % 2) * chan_share + row // pair) * per_owner + (row % pair) // 2
    swapped = jnp.where(column == wanted, 1.0, 0.0).astype(BF16)
    row, column = iotas((groups * depth, orders))
    start = (column // share) * depth + column % share
    pickers = [jnp.where(row == start + b * share, 1.0, 0.0).astype(BF16) for b in range(members)]
    for e in range(owners):
        turned = lax.dot_general(
            swapped,
            got[e].reshape(groups * depth, lanes),
            (((1,), (1,)), ((), ())),
            preferred_element_type=F32,
        ).astype(BF16)
        for b in range(members):
            lines = jnp.dot(turned, pickers[b], preferred_element_type=F32)
            for c in range(chan_share):
                block = lines[c * pair : (c + 1) * pair]
                out[b, e * chan_share + c] = block.reshape(per_owner, 2, orders)


def local(fields, depth_kernel, mix_weight, legendre, truth, degree_order):
    ens_parts, groups = lax.axis_size("ens"), lax.axis_size("lat")
    ens_at, lat_at = lax.axis_index("ens"), lax.axis_index("lat")
    members, chans, rows, nlon = fields.shape
    _, orders, degrees = legendre.shape
    ens = members * ens_parts
    nlat = rows * groups
    share, per_owner, chan_share = orders // groups, degrees // groups, chans // ens_parts
    used = 2 * chan_share
    slots = up(used, 8)
    height = up(members * used, 8)
    span = up(orders, 128)
    size = depth_kernel.shape[1]
    halo = size // 2
    wide = up(nlon + 2 * halo, 128)
    depth = members * chans

    table = jnp.asarray(wave_table(nlon, orders, span))
    kernel = depth_kernel.transpose(1, 2, 0)
    flags = place()
    own = fields.transpose(0, 2, 1, 3)
    odd = lat_at % 2
    ends = jnp.stack([own[:, :halo], own[:, rows - halo :]])
    near = lax.all_to_all(ends, "lat", split_axis=0, concat_axis=0, tiled=True, axis_index_groups=pairs_of(groups, 0))
    far = partner(lax.dynamic_slice_in_dim(own, odd * (rows - halo), halo, 1), False)

    pick = np.zeros((2, members, ens_parts, height, chans), np.float32)
    for r in range(2):
        for b in range(members):
            for o in range(chans):
                at = b * used + r * chan_share + o % chan_share
                pick[r, b, o // chan_share, at, o] = 1.0
    pick = jnp.asarray(pick.reshape(2, members, ens_parts * height, chans).astype(jnp.bfloat16))

    vmem = pltpu.CompilerParams(vmem_limit_bytes=60 * 1024 * 1024)
    scalars = pl.BlockSpec(memory_space=pltpu.SMEM)
    whole = pl.BlockSpec(memory_space=pltpu.VMEM)
    grid_shape = (members, rows, chans, nlon)
    lined = jax.ShapeDtypeStruct((rows, depth, nlon), F32)
    edge = jax.ShapeDtypeStruct((halo, depth, nlon), BF16)
    taps_out = jax.ShapeDtypeStruct((size * size, depth, 128), BF16)

    def call(body, outs, scratch, work, *args):
        specs = [scalars if a is flags else whole for a in args]
        return pl.pallas_call(
            body,
            out_shape=outs,
            in_specs=specs,
            scratch_shapes=scratch,
            compiler_params=vmem,
            cost_estimate=pl.CostEstimate(
                flops=work, transcendentals=0, bytes_accessed=8 * rows * depth * nlon
            ),
        )(*args)

    def swap(x):
        flat = x.reshape((ens_parts * groups,) + x.shape[2:])
        flat = lax.all_to_all(flat, ("ens", "lat"), split_axis=0, concat_axis=0, tiled=True)
        return flat.reshape(x.shape)

    work = 2 * size * size * rows * depth * nlon
    partial, taps, mixer = call(
        prepare_kernel,
        (lined, taps_out, jax.ShapeDtypeStruct((2, ens_parts * height, depth), BF16)),
        [pltpu.VMEM((rows, depth, wide), BF16)],
        work,
        own,
        kernel,
        mix_weight,
        pick,
    )
    target = lax.dynamic_slice(
        truth, (ens_at * chan_share, 0, lat_at * share, 0), (chan_share, 2, share, degrees)
    )
    target = target.transpose(2, 1, 0, 3).reshape(share, used, degrees)
    target = jnp.pad(target, ((0, 0), (0, slots - used), (0, 0)))

    slab = legendre.reshape(rows, groups, share * degrees).transpose(1, 0, 2)
    line = math.gcd(rows * share * degrees, 128)
    slab = slab.reshape(groups, rows * share * degrees // line, line)

    def chunk(lines):
        return jax.ShapeDtypeStruct((ens_parts, groups, height, up(lines * share, 128)), BF16)

    half_scratch = [pltpu.VMEM((halo, depth, wide), BF16), pltpu.VMEM((halo, depth, nlon), BF16)]
    mixed, inner = call(
        near_kernel,
        (jax.ShapeDtypeStruct((halo, ens_parts * height, span), F32), edge),
        half_scratch,
        work // 2,
        flags,
        near,
        partial,
        taps,
        table,
        mixer,
    )
    slab, mixed = lax.optimization_barrier((slab, mixed))
    slab = lax.all_to_all(slab, "lat", split_axis=0, concat_axis=0, tiled=True)
    order_legendre = slab.reshape(nlat, share, degrees).transpose(1, 0, 2)
    sent, outer = call(
        functools.partial(far_kernel, share),
        (chunk(rows), edge),
        half_scratch,
        work // 2,
        flags,
        far,
        partial,
        taps,
        table,
        mixer,
        mixed,
    )
    got = swap(sent)
    got, held = lax.optimization_barrier((got, outer))
    near, far = partner(inner, True), partner(held, False)
    back, grads = call(
        functools.partial(score_kernel, members, used, rows, halo),
        (
            chunk(rows + 2 * halo),
            jax.ShapeDtypeStruct((up(degrees, 128) // 128, share * ens * slots, 128), F32),
        ),
        [
            pltpu.VMEM((nlat * share, ens * slots), F32),
            pltpu.VMEM(((nlat + 2 * halo) * share, ens * slots), F32),
            pltpu.VMEM((degrees, degrees), BF16),
        ],
        work,
        got,
        order_legendre,
        target,
        degree_order.reshape(1, degrees),
    )
    returned = swap(back)
    packed = call(
        functools.partial(pack_kernel, members, used, per_owner),
        jax.ShapeDtypeStruct(
            (ens_parts, groups, members * share, up(used * per_owner, 128)), BF16
        ),
        [],
        work,
        grads,
    )
    owned = swap(packed)
    flipped = call(flip_kernel, taps_out, [], work // 8, kernel)
    grad_fields = call(
        functools.partial(backward_kernel, share),
        jax.ShapeDtypeStruct(grid_shape, BF16),
        [
            pltpu.VMEM((rows + 2 * halo, depth, wide), BF16),
            pltpu.VMEM((rows + 2 * halo, depth, nlon), F32),
            pltpu.VMEM((rows, depth, nlon), F32),
        ],
        work,
        flags,
        returned,
        near,
        far,
        inner,
        outer,
        flipped,
        mixer,
        table,
    )
    score_grad = call(
        functools.partial(unpack_kernel, members),
        jax.ShapeDtypeStruct((members, chans, per_owner, 2, orders), F32),
        [],
        work,
        owned,
    )
    return grad_fields.transpose(0, 2, 1, 3), score_grad.transpose(0, 1, 3, 4, 2)


def solution(mesh):
    placed = (P("ens", None, "lat", None), P(), P(), P("lat", None, None), P(), P())

    return jax.shard_map(
        local,
        mesh=mesh,
        in_specs=placed,
        out_specs=(P("ens", None, "lat", None), P("ens", None, None, None, "lat")),
        check_vma=False,
    )
```

```python
import functools
import math

import jax
import jax.numpy as jnp
import numpy as np
from jax import lax
from jax.experimental import pallas as pl
from jax.experimental.pallas import tpu as pltpu
from jax.sharding import PartitionSpec as P


smooth_width = 0.5
TILE = 16
F32 = jnp.float32
BF16 = jnp.bfloat16


def up(value, step):
    return -(-value // step) * step


def wave_table(nlon, orders, span):
    columns = np.arange(nlon, dtype=np.int64)
    number = np.arange(orders, dtype=np.int64)
    angles = (columns[:, None] * number[None, :] % nlon) * (2.0 * math.pi / nlon)
    table = np.zeros((nlon, 2, span), np.float32)
    for part, values in enumerate((np.cos(angles), -np.sin(angles))):
        table[:, part, :orders] = values / math.sqrt(nlon)
    return table.reshape(nlon, 2 * span).astype(jnp.bfloat16)


def partners(inner, outer):
    count = lax.axis_size("lat")
    near = [(i, i ^ 1) for i in range(count)]
    far = [(i, (i + (1 if i % 2 else -1)) % count) for i in range(count)]
    one = lax.ppermute(inner, "lat", near)
    other = lax.ppermute(outer, "lat", far)
    return one, other


def place():
    at, count = lax.axis_index("lat"), lax.axis_size("lat")
    return jnp.stack([at % 2, (at > 0) & (at < count - 1)]).astype(jnp.int32)


def fill_row(padded, row, value, half):
    depth, nlon = value.shape
    wide = padded.shape[-1]
    base = nlon // 128 * 128
    tail = [value[:, base:], value[:, :half]]
    if wide > nlon + 2 * half:
        tail.append(jnp.zeros((depth, wide - nlon - 2 * half), value.dtype))
    tail.append(value[:, nlon - half :])
    padded[row, :, :base] = value[:, :base].astype(padded.dtype)
    padded[row, :, base:] = jnp.concatenate(tail, axis=-1).astype(padded.dtype)


def tap_sum(padded, taps, c0, lines, size):
    wide = padded.shape[-1]
    total = None
    for q in range(size):
        part = None
        for row, p in lines:
            weight = jnp.tile(taps[p * size + q, pl.ds(c0, TILE), :], (1, wide // 128))
            term = weight * padded[row, pl.ds(c0, TILE), :]
            part = term if part is None else part + term
        part = part.astype(F32)
        shift = (size // 2 - q) % wide
        if shift:
            part = pltpu.roll(part, shift, 1)
        total = part if total is None else total + part
    return total


def spread_taps(kernel, taps, flip):
    size, _, chans = kernel.shape
    for p in range(size):
        plane = kernel[p].T
        for q in range(size):
            at = p * size + q
            at = size * size - 1 - at if flip else at
            value = jnp.broadcast_to(plane[:, q : q + 1], (chans, 128))
            value = jnp.concatenate([value] * (taps.shape[1] // chans), axis=0)
            taps[at] = value.astype(taps.dtype)


def joined(block, row):
    return jnp.concatenate([block[b, row].astype(F32) for b in range(block.shape[0])], axis=0)


def gelu_pair(x):
    scale = math.sqrt(2.0 / math.pi)
    square = x * x
    t = jnp.tanh(scale * x * (1.0 + 0.044715 * square))
    half = 0.5 * (1.0 + t)
    slope = half + 0.5 * x * (1.0 - t * t) * (scale * (1.0 + 3 * 0.044715 * square))
    return x * half, slope


def prepare_kernel(own, kernel, weight, pick, partial, taps, mixer, padded):
    members, rows, chans, nlon = own.shape
    depth = members * chans
    size = kernel.shape[0]
    half = size // 2
    spread_taps(kernel, taps, False)
    for row in range(rows):
        fill_row(padded, row, joined(own, row), half)

    @pl.loop(0, depth // TILE)
    def _(ct):
        c0 = pl.multiple_of(ct * TILE, TILE)
        for i in range(rows):
            lines = [(i + p - half, p) for p in range(size) if 0 <= i + p - half < rows]
            total = tap_sum(padded, taps, c0, lines, size)
            total = total + padded[i, pl.ds(c0, TILE), :].astype(F32)
            partial[i, pl.ds(c0, TILE), :] = total[:, :nlon]

    for r in range(2):
        lines = []
        for b in range(members):
            lines.append(jnp.dot(pick[r, b], weight[...], preferred_element_type=F32))
        mixer[r] = jnp.concatenate(lines, axis=1).astype(BF16)


def finish_rows(lower, present, edge, partial, taps, table, mixer, slope, padded, act):
    rows, depth, nlon = partial.shape
    size = math.isqrt(taps.shape[0])
    half = size // 2
    span = table.shape[1] // 2
    for row in range(half):
        at = jnp.where(lower, row, half - 1 - row)
        value = joined(edge, at)
        if present is not None:
            value = jnp.where(present, value, jnp.zeros_like(value))
        fill_row(padded, row, value, half)

    @pl.loop(0, depth // TILE)
    def _(ct):
        c0 = pl.multiple_of(ct * TILE, TILE)
        for j in range(half):
            lines = [
                (row, jnp.where(lower, row - j, size - 1 - (row - j))) for row in range(j, half)
            ]
            at = jnp.where(lower, j, half - 1 - j)
            value = partial[jnp.where(lower, j, rows - 1 - j), pl.ds(c0, TILE), :]
            value = value + tap_sum(padded, taps, c0, lines, size)[:, :nlon]
            value, grad = gelu_pair(value)
            act[at, pl.ds(c0, TILE), :] = value.astype(BF16)
            slope[at, pl.ds(c0, TILE), :] = grad.astype(BF16)

    flat = act[...].reshape(half * depth, nlon)
    spectral = jnp.dot(flat, table[...], preferred_element_type=F32).astype(BF16)
    mixed = []
    for j in range(half):
        line = spectral[j * depth : (j + 1) * depth]
        mixed.append(
            jnp.dot(mixer[0], line[:, :span], preferred_element_type=F32)
            + jnp.dot(mixer[1], line[:, span:], preferred_element_type=F32)
        )
    return mixed


def near_kernel(flags, edge, partial, taps, table, mixer, mixed, slope, padded, act):
    lines = finish_rows(flags[0] == 1, None, edge, partial, taps, table, mixer, slope, padded, act)
    for j, line in enumerate(lines):
        mixed[j] = line


def far_kernel(share, flags, edge, partial, taps, table, mixer, nearer, out, slope, padded, act):
    owners, groups, height, lanes = out.shape
    lines = finish_rows(
        flags[0] != 1, flags[1] == 1, edge, partial, taps, table, mixer, slope, padded, act
    )
    lines = [nearer[j] for j in range(nearer.shape[0])] + lines
    for t in range(groups):
        pieces = [x[:, t * share : (t + 1) * share] for x in lines]
        if lanes > len(lines) * share:
            pieces.append(jnp.zeros((owners * height, lanes - len(lines) * share), F32))
        block = jnp.concatenate(pieces, axis=1)
        for e in range(owners):
            out[e, t] = block[e * height : (e + 1) * height].astype(BF16)


def flip_kernel(kernel, taps):
    spread_taps(kernel, taps, True)


def soft_sign(gaps):
    return gaps * lax.rsqrt(gaps * gaps + smooth_width * smooth_width)


def score_kernel(members, used, rows, halo, got, legendre, target, order, back, grads, spread, gather, picked):
    owners, groups, height, lanes = got.shape
    orders, nlat, degrees = legendre.shape
    slots = target.shape[1]
    ens = owners * members
    for t in range(groups):
        pieces = []
        for e in range(owners):
            block = got[e, t].astype(F32)
            for b in range(members):
                pieces.append(block[b * used : (b + 1) * used])
                if slots > used:
                    pieces.append(jnp.zeros((slots - used, lanes), F32))
        block = jnp.concatenate(pieces, axis=0).T
        at, part = t * rows * orders, halo * orders
        first, second = (at, at + part) if t % 2 else (at + part, at)
        spread[first : first + part, :] = block[:part]
        spread[second : second + part, :] = block[part : 2 * part]
    reorder = jnp.where(
        lax.broadcasted_iota(jnp.int32, (degrees, degrees), 0) == order[...], 1.0, 0.0
    )
    picked[...] = reorder.astype(BF16)
    edge = halo * orders
    gather[:edge, :] = jnp.zeros((edge, ens * slots), F32)
    gather[edge + nlat * orders :, :] = jnp.zeros((edge, ens * slots), F32)

    def score(values, truth):
        own = [values[k * slots : (k + 1) * slots] for k in range(ens)]
        sums = [None] * ens
        for k in range(ens):
            for n in range(k + 1, ens):
                sign = soft_sign(own[k] - own[n])
                sums[k] = sign if sums[k] is None else sums[k] + sign
                sums[n] = -sign if sums[n] is None else sums[n] - sign
        return jnp.concatenate(
            [
                soft_sign(own[k] - truth) * (1.0 / ens) - sums[k] * (1.0 / (ens * (ens - 1)))
                for k in range(ens)
            ],
            axis=0,
        )

    tail = degrees % 128
    packs = tail > 0 and 128 % tail == 0 and orders % (128 // tail) == 0
    step = 128 // tail if packs else 1
    body = degrees - tail if packs else degrees

    @pl.loop(0, orders // step)
    def _(trip):
        numbers = [trip * step + j for j in range(step)]
        coeffs = [
            lax.dot_general(
                spread[pl.ds(m, nlat, stride=orders), :].astype(BF16),
                legendre[m],
                (((0,), (0,)), ((), ())),
                preferred_element_type=F32,
            )
            for m in numbers
        ]
        truths = [target[m].astype(F32) for m in numbers]
        scored = [score(x[:, :body], y[:, :body]) for x, y in zip(coeffs, truths)]
        if packs:
            rest = score(
                jnp.concatenate([x[:, body:] for x in coeffs], axis=1),
                jnp.concatenate([y[:, body:] for y in truths], axis=1),
            )
            scored = [
                jnp.concatenate([x, rest[:, j * tail : (j + 1) * tail]], axis=1)
                for j, x in enumerate(scored)
            ]
        for m, grad in zip(numbers, scored):
            grad = grad.astype(BF16)
            gather[pl.ds(edge + m, nlat, stride=orders), :] = lax.dot_general(
                legendre[m], grad, (((1,), (1,)), ((), ())), preferred_element_type=F32
            )
            at = pl.multiple_of(m * ens * slots, 8)
            ordered = jnp.dot(grad, picked[...], preferred_element_type=F32)
            for j in range(grads.shape[0]):
                last = min(degrees, (j + 1) * 128)
                grads[j, pl.ds(at, ens * slots), : last - j * 128] = ordered[:, j * 128 : last]

    wide = back.shape[3]
    tall = (rows + 2 * halo) * orders
    for t in range(groups):
        at = t * rows * orders
        block = gather[at : at + tall, :]
        if wide > tall:
            block = jnp.concatenate([block, jnp.zeros((wide - tall, ens * slots), F32)], axis=0)
        block = block.T
        for e in range(owners):
            pieces = []
            for b in range(members):
                at = (e * members + b) * slots
                pieces.append(block[at : at + used])
            if height > members * used:
                pieces.append(jnp.zeros((height - members * used, wide), F32))
            back[e, t] = jnp.concatenate(pieces, axis=0).astype(BF16)


def backward_kernel(share, flags, got, near, far, inner, outer, taps, mixer, table, out, padded, flat, stage):
    owners, groups, height, _ = got.shape
    half, depth, nlon = inner.shape
    members, rows, chans, _ = out.shape
    size = math.isqrt(taps.shape[0])
    span = table.shape[1] // 2
    total = rows + 2 * half
    blocks = [
        jnp.concatenate([got[e, t].astype(F32) for e in range(owners)], axis=0) for t in range(groups)
    ]
    lines = []
    for i in range(total):
        pieces = [x[:, i * share : (i + 1) * share] for x in blocks]
        pieces.append(jnp.zeros((owners * height, span - groups * share), F32))
        line = jnp.concatenate(pieces, axis=1).astype(BF16)
        lines.append(
            jnp.concatenate(
                [
                    lax.dot_general(
                        mixer[r], line, (((0,), (0,)), ((), ())), preferred_element_type=F32
                    ).astype(BF16)
                    for r in range(2)
                ],
                axis=1,
            )
        )
    flat[...] = lax.dot_general(
        jnp.concatenate(lines, axis=0),
        table[...],
        (((1,), (1,)), ((), ())),
        preferred_element_type=F32,
    ).reshape(flat.shape)
    odd = flags[0] == 1
    pairs = ((near, far), (inner, outer), (outer, inner), (far, near))
    for part, (one, other) in enumerate(pairs):
        for row in range(half):
            at = part * half + row
            slope = jnp.where(odd, one[row].astype(F32), other[row].astype(F32))
            fill_row(padded, at, flat[at] * slope, half)

    @pl.loop(0, depth // TILE)
    def _(ct):
        c0 = pl.multiple_of(ct * TILE, TILE)

        @pl.loop(0, rows)
        def _(i):
            value = tap_sum(padded, taps, c0, [(i + p, p) for p in range(size)], size)
            value = value + padded[i + half, pl.ds(c0, TILE), :].astype(F32)
            stage[i, pl.ds(c0, TILE), :] = value[:, :nlon]

    for b in range(members):
        for i in range(rows):
            out[b, i] = stage[i, b * chans : (b + 1) * chans, :].astype(BF16)


def pack_kernel(members, used, per_owner, grads, out):
    owners, groups, depth, lanes = out.shape
    share = depth // members
    stride = grads.shape[1] // share
    slots = stride // (owners * members)
    for e in range(owners):
        for b in range(members):
            at = (e * members + b) * slots
            planes = [
                jnp.concatenate(
                    [grads[j, pl.ds(at + s, share, stride=stride), :] for j in range(grads.shape[0])],
                    axis=1,
                )
                for s in range(used)
            ]
            for t in range(groups):
                pieces = [x[:, t * per_owner : (t + 1) * per_owner] for x in planes]
                if lanes > used * per_owner:
                    pieces.append(jnp.zeros((share, lanes - used * per_owner), F32))
                out[e, t, b * share : (b + 1) * share, :] = jnp.concatenate(pieces, axis=1).astype(BF16)


def unpack_kernel(members, got, out):
    owners, groups, depth, lanes = got.shape
    _, chans, per_owner, _, orders = out.shape
    share, chan_share = depth // members, chans // owners
    pair = 2 * per_owner

    def iotas(shape):
        return (lax.broadcasted_iota(jnp.int32, shape, d) for d in range(2))

    row, column = iotas((chan_share * pair, lanes))
    wanted = ((row % 2) * chan_share + row // pair) * per_owner + (row % pair) // 2
    swapped = jnp.where(column == wanted, 1.0, 0.0).astype(BF16)
    row, column = iotas((groups * depth, orders))
    start = (column // share) * depth + column % share
    pickers = [jnp.where(row == start + b * share, 1.0, 0.0).astype(BF16) for b in range(members)]
    for e in range(owners):
        turned = lax.dot_general(
            swapped,
            got[e].reshape(groups * depth, lanes),
            (((1,), (1,)), ((), ())),
            preferred_element_type=F32,
        ).astype(BF16)
        for b in range(members):
            lines = jnp.dot(turned, pickers[b], preferred_element_type=F32)
            for c in range(chan_share):
                block = lines[c * pair : (c + 1) * pair]
                out[b, e * chan_share + c] = block.reshape(per_owner, 2, orders)


def local(fields, depth_kernel, mix_weight, legendre, truth, degree_order):
    ens_parts, groups = lax.axis_size("ens"), lax.axis_size("lat")
    ens_at, lat_at = lax.axis_index("ens"), lax.axis_index("lat")
    members, chans, rows, nlon = fields.shape
    _, orders, degrees = legendre.shape
    ens = members * ens_parts
    nlat = rows * groups
    share, per_owner, chan_share = orders // groups, degrees // groups, chans // ens_parts
    used = 2 * chan_share
    slots = up(used, 8)
    height = up(members * used, 8)
    span = up(orders, 128)
    size = depth_kernel.shape[1]
    halo = size // 2
    wide = up(nlon + 2 * halo, 128)
    depth = members * chans

    table = jnp.asarray(wave_table(nlon, orders, span))
    kernel = depth_kernel.transpose(1, 2, 0)
    flags = place()
    own = fields.transpose(0, 2, 1, 3)
    odd = lat_at % 2
    near, far = partners(
        lax.dynamic_slice_in_dim(own, (1 - odd) * (rows - halo), halo, 1),
        lax.dynamic_slice_in_dim(own, odd * (rows - halo), halo, 1),
    )

    pick = np.zeros((2, members, ens_parts, height, chans), np.float32)
    for r in range(2):
        for b in range(members):
            for o in range(chans):
                at = b * used + r * chan_share + o % chan_share
                pick[r, b, o // chan_share, at, o] = 1.0
    pick = jnp.asarray(pick.reshape(2, members, ens_parts * height, chans).astype(jnp.bfloat16))

    vmem = pltpu.CompilerParams(vmem_limit_bytes=60 * 1024 * 1024)
    scalars = pl.BlockSpec(memory_space=pltpu.SMEM)
    whole = pl.BlockSpec(memory_space=pltpu.VMEM)
    grid_shape = (members, rows, chans, nlon)
    lined = jax.ShapeDtypeStruct((rows, depth, nlon), F32)
    edge = jax.ShapeDtypeStruct((halo, depth, nlon), BF16)
    taps_out = jax.ShapeDtypeStruct((size * size, depth, 128), BF16)

    def call(body, outs, scratch, work, *args):
        specs = [scalars if a is flags else whole for a in args]
        return pl.pallas_call(
            body,
            out_shape=outs,
            in_specs=specs,
            scratch_shapes=scratch,
            compiler_params=vmem,
            cost_estimate=pl.CostEstimate(
                flops=work, transcendentals=0, bytes_accessed=8 * rows * depth * nlon
            ),
        )(*args)

    def swap(x):
        flat = x.reshape((ens_parts * groups,) + x.shape[2:])
        flat = lax.all_to_all(flat, ("ens", "lat"), split_axis=0, concat_axis=0, tiled=True)
        return flat.reshape(x.shape)

    work = 2 * size * size * rows * depth * nlon
    partial, taps, mixer = call(
        prepare_kernel,
        (lined, taps_out, jax.ShapeDtypeStruct((2, ens_parts * height, depth), BF16)),
        [pltpu.VMEM((rows, depth, wide), BF16)],
        work,
        own,
        kernel,
        mix_weight,
        pick,
    )
    target = lax.dynamic_slice(
        truth, (ens_at * chan_share, 0, lat_at * share, 0), (chan_share, 2, share, degrees)
    )
    target = target.transpose(2, 1, 0, 3).reshape(share, used, degrees)
    target = jnp.pad(target, ((0, 0), (0, slots - used), (0, 0)))

    slab = legendre.reshape(rows, groups, share * degrees).transpose(1, 0, 2)
    line = math.gcd(rows * share * degrees, 128)
    slab = slab.reshape(groups, rows * share * degrees // line, line)

    def chunk(lines):
        return jax.ShapeDtypeStruct((ens_parts, groups, height, up(lines * share, 128)), BF16)

    half_scratch = [pltpu.VMEM((halo, depth, wide), BF16), pltpu.VMEM((halo, depth, nlon), BF16)]
    mixed, inner = call(
        near_kernel,
        (jax.ShapeDtypeStruct((halo, ens_parts * height, span), F32), edge),
        half_scratch,
        work // 2,
        flags,
        near,
        partial,
        taps,
        table,
        mixer,
    )
    slab, mixed = lax.optimization_barrier((slab, mixed))
    slab = lax.all_to_all(slab, "lat", split_axis=0, concat_axis=0, tiled=True)
    order_legendre = slab.reshape(nlat, share, degrees).transpose(1, 0, 2)
    sent, outer = call(
        functools.partial(far_kernel, share),
        (chunk(rows), edge),
        half_scratch,
        work // 2,
        flags,
        far,
        partial,
        taps,
        table,
        mixer,
        mixed,
    )
    got = swap(sent)
    near, far = partners(inner, outer)
    back, grads = call(
        functools.partial(score_kernel, members, used, rows, halo),
        (
            chunk(rows + 2 * halo),
            jax.ShapeDtypeStruct((up(degrees, 128) // 128, share * ens * slots, 128), F32),
        ),
        [
            pltpu.VMEM((nlat * share, ens * slots), F32),
            pltpu.VMEM(((nlat + 2 * halo) * share, ens * slots), F32),
            pltpu.VMEM((degrees, degrees), BF16),
        ],
        work,
        got,
        order_legendre,
        target,
        degree_order.reshape(1, degrees),
    )
    returned = swap(back)
    packed = call(
        functools.partial(pack_kernel, members, used, per_owner),
        jax.ShapeDtypeStruct(
            (ens_parts, groups, members * share, up(used * per_owner, 128)), BF16
        ),
        [],
        work,
        grads,
    )
    owned = swap(packed)
    flipped = call(flip_kernel, taps_out, [], work // 8, kernel)
    grad_fields = call(
        functools.partial(backward_kernel, share),
        jax.ShapeDtypeStruct(grid_shape, BF16),
        [
            pltpu.VMEM((rows + 2 * halo, depth, wide), BF16),
            pltpu.VMEM((rows + 2 * halo, depth, nlon), F32),
            pltpu.VMEM((rows, depth, nlon), F32),
        ],
        work,
        flags,
        returned,
        near,
        far,
        inner,
        outer,
        flipped,
        mixer,
        table,
    )
    score_grad = call(
        functools.partial(unpack_kernel, members),
        jax.ShapeDtypeStruct((members, chans, per_owner, 2, orders), F32),
        [],
        work,
        owned,
    )
    return grad_fields.transpose(0, 2, 1, 3), score_grad.transpose(0, 1, 3, 4, 2)


def solution(mesh):
    placed = (P("ens", None, "lat", None), P(), P(), P("lat", None, None), P(), P())

    return jax.shard_map(
        local,
        mesh=mesh,
        in_specs=placed,
        out_specs=(P("ens", None, "lat", None), P("ens", None, None, None, "lat")),
        check_vma=False,
    )
```

```python
import functools
import math

import jax
import jax.numpy as jnp
import numpy as np
from jax import lax
from jax.experimental import pallas as pl
from jax.experimental.pallas import tpu as pltpu
from jax.sharding import PartitionSpec as P


smooth_width = 0.5
TILE = 16
F32 = jnp.float32
BF16 = jnp.bfloat16


def up(value, step):
    return -(-value // step) * step


def wave_table(nlon, orders, span):
    columns = np.arange(nlon, dtype=np.int64)
    number = np.arange(orders, dtype=np.int64)
    angles = (columns[:, None] * number[None, :] % nlon) * (2.0 * math.pi / nlon)
    table = np.zeros((nlon, 2, span), np.float32)
    for part, values in enumerate((np.cos(angles), -np.sin(angles))):
        table[:, part, :orders] = values / math.sqrt(nlon)
    return table.reshape(nlon, 2 * span).astype(jnp.bfloat16)


def partners(inner, outer):
    count = lax.axis_size("lat")
    near = [(i, i ^ 1) for i in range(count)]
    far = [(i, (i + (1 if i % 2 else -1)) % count) for i in range(count)]
    one = lax.ppermute(inner, "lat", near)
    other = lax.ppermute(outer, "lat", far)
    return one, other


def place():
    at, count = lax.axis_index("lat"), lax.axis_size("lat")
    return jnp.stack([at % 2, (at > 0) & (at < count - 1)]).astype(jnp.int32)


def fill_row(padded, row, value, half):
    depth, nlon = value.shape
    wide = padded.shape[-1]
    base = nlon // 128 * 128
    tail = [value[:, base:], value[:, :half]]
    if wide > nlon + 2 * half:
        tail.append(jnp.zeros((depth, wide - nlon - 2 * half), value.dtype))
    tail.append(value[:, nlon - half :])
    padded[row, :, :base] = value[:, :base].astype(padded.dtype)
    padded[row, :, base:] = jnp.concatenate(tail, axis=-1).astype(padded.dtype)


def tap_sum(padded, taps, c0, lines, size):
    wide = padded.shape[-1]
    total = None
    for q in range(size):
        part = None
        for row, p in lines:
            weight = jnp.tile(taps[p * size + q, pl.ds(c0, TILE), :], (1, wide // 128))
            term = weight * padded[row, pl.ds(c0, TILE), :]
            part = term if part is None else part + term
        part = part.astype(F32)
        shift = (size // 2 - q) % wide
        if shift:
            part = pltpu.roll(part, shift, 1)
        total = part if total is None else total + part
    return total


def spread_taps(kernel, taps, flip):
    size, _, chans = kernel.shape
    for p in range(size):
        plane = kernel[p].T
        for q in range(size):
            at = p * size + q
            at = size * size - 1 - at if flip else at
            value = jnp.broadcast_to(plane[:, q : q + 1], (chans, 128))
            value = jnp.concatenate([value] * (taps.shape[1] // chans), axis=0)
            taps[at] = value.astype(taps.dtype)


def joined(block, row):
    return jnp.concatenate([block[b, row].astype(F32) for b in range(block.shape[0])], axis=0)


def gelu_pair(x):
    scale = math.sqrt(2.0 / math.pi)
    square = x * x
    t = jnp.tanh(scale * x * (1.0 + 0.044715 * square))
    half = 0.5 * (1.0 + t)
    slope = half + 0.5 * x * (1.0 - t * t) * (scale * (1.0 + 3 * 0.044715 * square))
    return x * half, slope


def prepare_kernel(own, kernel, weight, pick, partial, taps, mixer, padded):
    members, rows, chans, nlon = own.shape
    depth = members * chans
    size = kernel.shape[0]
    half = size // 2
    spread_taps(kernel, taps, False)
    for row in range(rows):
        fill_row(padded, row, joined(own, row), half)

    @pl.loop(0, depth // TILE)
    def _(ct):
        c0 = pl.multiple_of(ct * TILE, TILE)
        for i in range(rows):
            lines = [(i + p - half, p) for p in range(size) if 0 <= i + p - half < rows]
            total = tap_sum(padded, taps, c0, lines, size)
            total = total + padded[i, pl.ds(c0, TILE), :].astype(F32)
            partial[i, pl.ds(c0, TILE), :] = total[:, :nlon]

    for r in range(2):
        lines = []
        for b in range(members):
            lines.append(jnp.dot(pick[r, b], weight[...], preferred_element_type=F32))
        mixer[r] = jnp.concatenate(lines, axis=1).astype(BF16)


def finish_rows(lower, present, edge, partial, taps, table, mixer, slope, padded, act):
    rows, depth, nlon = partial.shape
    size = math.isqrt(taps.shape[0])
    half = size // 2
    span = table.shape[1] // 2
    for row in range(half):
        at = jnp.where(lower, row, half - 1 - row)
        value = joined(edge, at)
        if present is not None:
            value = jnp.where(present, value, jnp.zeros_like(value))
        fill_row(padded, row, value, half)

    @pl.loop(0, depth // TILE)
    def _(ct):
        c0 = pl.multiple_of(ct * TILE, TILE)
        for j in range(half):
            lines = [
                (row, jnp.where(lower, row - j, size - 1 - (row - j))) for row in range(j, half)
            ]
            at = jnp.where(lower, j, half - 1 - j)
            value = partial[jnp.where(lower, j, rows - 1 - j), pl.ds(c0, TILE), :]
            value = value + tap_sum(padded, taps, c0, lines, size)[:, :nlon]
            value, grad = gelu_pair(value)
            act[at, pl.ds(c0, TILE), :] = value.astype(BF16)
            slope[at, pl.ds(c0, TILE), :] = grad.astype(BF16)

    flat = act[...].reshape(half * depth, nlon)
    spectral = jnp.dot(flat, table[...], preferred_element_type=F32).astype(BF16)
    mixed = []
    for j in range(half):
        line = spectral[j * depth : (j + 1) * depth]
        mixed.append(
            jnp.dot(mixer[0], line[:, :span], preferred_element_type=F32)
            + jnp.dot(mixer[1], line[:, span:], preferred_element_type=F32)
        )
    return mixed


def near_kernel(flags, edge, partial, taps, table, mixer, mixed, slope, padded, act):
    lines = finish_rows(flags[0] == 1, None, edge, partial, taps, table, mixer, slope, padded, act)
    for j, line in enumerate(lines):
        mixed[j] = line


def far_kernel(share, flags, edge, partial, taps, table, mixer, nearer, out, slope, padded, act):
    owners, groups, height, lanes = out.shape
    lines = finish_rows(
        flags[0] != 1, flags[1] == 1, edge, partial, taps, table, mixer, slope, padded, act
    )
    lines = [nearer[j] for j in range(nearer.shape[0])] + lines
    for t in range(groups):
        pieces = [x[:, t * share : (t + 1) * share] for x in lines]
        if lanes > len(lines) * share:
            pieces.append(jnp.zeros((owners * height, lanes - len(lines) * share), F32))
        block = jnp.concatenate(pieces, axis=1)
        for e in range(owners):
            out[e, t] = block[e * height : (e + 1) * height].astype(BF16)


def flip_kernel(kernel, taps):
    spread_taps(kernel, taps, True)


def soft_sign(gaps):
    return gaps * lax.rsqrt(gaps * gaps + smooth_width * smooth_width)


def score_kernel(members, used, rows, halo, got, legendre, target, order, back, grads, spread, gather, picked):
    owners, groups, height, lanes = got.shape
    orders, nlat, degrees = legendre.shape
    slots = target.shape[1]
    ens = owners * members
    for t in range(groups):
        pieces = []
        for e in range(owners):
            block = got[e, t].astype(F32)
            for b in range(members):
                pieces.append(block[b * used : (b + 1) * used])
                if slots > used:
                    pieces.append(jnp.zeros((slots - used, lanes), F32))
        block = jnp.concatenate(pieces, axis=0).T
        at, part = t * rows * orders, halo * orders
        first, second = (at, at + part) if t % 2 else (at + part, at)
        spread[first : first + part, :] = block[:part]
        spread[second : second + part, :] = block[part : 2 * part]
    reorder = jnp.where(
        lax.broadcasted_iota(jnp.int32, (degrees, degrees), 0) == order[...], 1.0, 0.0
    )
    picked[...] = reorder.astype(BF16)
    edge = halo * orders
    gather[:edge, :] = jnp.zeros((edge, ens * slots), F32)
    gather[edge + nlat * orders :, :] = jnp.zeros((edge, ens * slots), F32)

    def score(values, truth):
        own = [values[k * slots : (k + 1) * slots] for k in range(ens)]
        sums = [None] * ens
        for k in range(ens):
            for n in range(k + 1, ens):
                sign = soft_sign(own[k] - own[n])
                sums[k] = sign if sums[k] is None else sums[k] + sign
                sums[n] = -sign if sums[n] is None else sums[n] - sign
        return jnp.concatenate(
            [
                soft_sign(own[k] - truth) * (1.0 / ens) - sums[k] * (1.0 / (ens * (ens - 1)))
                for k in range(ens)
            ],
            axis=0,
        )

    tail = degrees % 128
    packs = tail > 0 and 128 % tail == 0 and orders % (128 // tail) == 0
    step = 128 // tail if packs else 1
    body = degrees - tail if packs else degrees

    @pl.loop(0, orders // step)
    def _(trip):
        numbers = [trip * step + j for j in range(step)]
        coeffs = [
            lax.dot_general(
                spread[pl.ds(m, nlat, stride=orders), :].astype(BF16),
                legendre[m],
                (((0,), (0,)), ((), ())),
                preferred_element_type=F32,
            )
            for m in numbers
        ]
        truths = [target[m].astype(F32) for m in numbers]
        scored = [score(x[:, :body], y[:, :body]) for x, y in zip(coeffs, truths)]
        if packs:
            rest = score(
                jnp.concatenate([x[:, body:] for x in coeffs], axis=1),
                jnp.concatenate([y[:, body:] for y in truths], axis=1),
            )
            scored = [
                jnp.concatenate([x, rest[:, j * tail : (j + 1) * tail]], axis=1)
                for j, x in enumerate(scored)
            ]
        for m, grad in zip(numbers, scored):
            grad = grad.astype(BF16)
            gather[pl.ds(edge + m, nlat, stride=orders), :] = lax.dot_general(
                legendre[m], grad, (((1,), (1,)), ((), ())), preferred_element_type=F32
            )
            at = pl.multiple_of(m * ens * slots, 8)
            ordered = jnp.dot(grad, picked[...], preferred_element_type=F32)
            for j in range(grads.shape[0]):
                last = min(degrees, (j + 1) * 128)
                grads[j, pl.ds(at, ens * slots), : last - j * 128] = ordered[:, j * 128 : last]

    wide = back.shape[3]
    tall = (rows + 2 * halo) * orders
    for t in range(groups):
        at = t * rows * orders
        block = gather[at : at + tall, :]
        if wide > tall:
            block = jnp.concatenate([block, jnp.zeros((wide - tall, ens * slots), F32)], axis=0)
        block = block.T
        for e in range(owners):
            pieces = []
            for b in range(members):
                at = (e * members + b) * slots
                pieces.append(block[at : at + used])
            if height > members * used:
                pieces.append(jnp.zeros((height - members * used, wide), F32))
            back[e, t] = jnp.concatenate(pieces, axis=0).astype(BF16)


def backward_kernel(share, flags, got, near, far, inner, outer, taps, mixer, table, out, padded, flat, stage):
    owners, groups, height, _ = got.shape
    half, depth, nlon = inner.shape
    members, rows, chans, _ = out.shape
    size = math.isqrt(taps.shape[0])
    span = table.shape[1] // 2
    total = rows + 2 * half
    blocks = [
        jnp.concatenate([got[e, t].astype(F32) for e in range(owners)], axis=0) for t in range(groups)
    ]
    lines = []
    for i in range(total):
        pieces = [x[:, i * share : (i + 1) * share] for x in blocks]
        pieces.append(jnp.zeros((owners * height, span - groups * share), F32))
        line = jnp.concatenate(pieces, axis=1).astype(BF16)
        lines.append(
            jnp.concatenate(
                [
                    lax.dot_general(
                        mixer[r], line, (((0,), (0,)), ((), ())), preferred_element_type=F32
                    ).astype(BF16)
                    for r in range(2)
                ],
                axis=1,
            )
        )
    flat[...] = lax.dot_general(
        jnp.concatenate(lines, axis=0),
        table[...],
        (((1,), (1,)), ((), ())),
        preferred_element_type=F32,
    ).reshape(flat.shape)
    odd = flags[0] == 1
    pairs = ((near, far), (inner, outer), (outer, inner), (far, near))
    for part, (one, other) in enumerate(pairs):
        for row in range(half):
            at = part * half + row
            slope = jnp.where(odd, one[row].astype(F32), other[row].astype(F32))
            fill_row(padded, at, flat[at] * slope, half)

    @pl.loop(0, depth // TILE)
    def _(ct):
        c0 = pl.multiple_of(ct * TILE, TILE)

        @pl.loop(0, rows)
        def _(i):
            value = tap_sum(padded, taps, c0, [(i + p, p) for p in range(size)], size)
            value = value + padded[i + half, pl.ds(c0, TILE), :].astype(F32)
            stage[i, pl.ds(c0, TILE), :] = value[:, :nlon]

    for b in range(members):
        for i in range(rows):
            out[b, i] = stage[i, b * chans : (b + 1) * chans, :].astype(BF16)


def pack_kernel(members, used, per_owner, grads, out):
    owners, groups, depth, lanes = out.shape
    share = depth // members
    stride = grads.shape[1] // share
    slots = stride // (owners * members)
    for e in range(owners):
        for b in range(members):
            at = (e * members + b) * slots
            planes = [
                jnp.concatenate(
                    [grads[j, pl.ds(at + s, share, stride=stride), :] for j in range(grads.shape[0])],
                    axis=1,
                )
                for s in range(used)
            ]
            for t in range(groups):
                pieces = [x[:, t * per_owner : (t + 1) * per_owner] for x in planes]
                if lanes > used * per_owner:
                    pieces.append(jnp.zeros((share, lanes - used * per_owner), F32))
                out[e, t, b * share : (b + 1) * share, :] = jnp.concatenate(pieces, axis=1).astype(BF16)


def unpack_kernel(members, got, out):
    owners, groups, depth, lanes = got.shape
    _, chans, per_owner, _, orders = out.shape
    share, chan_share = depth // members, chans // owners
    pair = 2 * per_owner

    def iotas(shape):
        return (lax.broadcasted_iota(jnp.int32, shape, d) for d in range(2))

    row, column = iotas((chan_share * pair, lanes))
    wanted = ((row % 2) * chan_share + row // pair) * per_owner + (row % pair) // 2
    swapped = jnp.where(column == wanted, 1.0, 0.0).astype(BF16)
    row, column = iotas((groups * depth, orders))
    start = (column // share) * depth + column % share
    pickers = [jnp.where(row == start + b * share, 1.0, 0.0).astype(BF16) for b in range(members)]
    for e in range(owners):
        turned = lax.dot_general(
            swapped,
            got[e].reshape(groups * depth, lanes),
            (((1,), (1,)), ((), ())),
            preferred_element_type=F32,
        ).astype(BF16)
        for b in range(members):
            lines = jnp.dot(turned, pickers[b], preferred_element_type=F32)
            for c in range(chan_share):
                block = lines[c * pair : (c + 1) * pair]
                out[b, e * chan_share + c] = block.reshape(per_owner, 2, orders)


def local(fields, depth_kernel, mix_weight, legendre, truth, degree_order):
    ens_parts, groups = lax.axis_size("ens"), lax.axis_size("lat")
    ens_at, lat_at = lax.axis_index("ens"), lax.axis_index("lat")
    members, chans, rows, nlon = fields.shape
    _, orders, degrees = legendre.shape
    ens = members * ens_parts
    nlat = rows * groups
    share, per_owner, chan_share = orders // groups, degrees // groups, chans // ens_parts
    used = 2 * chan_share
    slots = up(used, 8)
    height = up(members * used, 8)
    span = up(orders, 128)
    size = depth_kernel.shape[1]
    halo = size // 2
    wide = up(nlon + 2 * halo, 128)
    depth = members * chans

    table = jnp.asarray(wave_table(nlon, orders, span))
    kernel = depth_kernel.transpose(1, 2, 0)
    flags = place()
    own = fields.transpose(0, 2, 1, 3)
    odd = lat_at % 2
    near, far = partners(
        lax.dynamic_slice_in_dim(own, (1 - odd) * (rows - halo), halo, 1),
        lax.dynamic_slice_in_dim(own, odd * (rows - halo), halo, 1),
    )

    pick = np.zeros((2, members, ens_parts, height, chans), np.float32)
    for r in range(2):
        for b in range(members):
            for o in range(chans):
                at = b * used + r * chan_share + o % chan_share
                pick[r, b, o // chan_share, at, o] = 1.0
    pick = jnp.asarray(pick.reshape(2, members, ens_parts * height, chans).astype(jnp.bfloat16))

    vmem = pltpu.CompilerParams(vmem_limit_bytes=28 * 1024 * 1024)
    scalars = pl.BlockSpec(memory_space=pltpu.SMEM)
    whole = pl.BlockSpec(memory_space=pltpu.VMEM)
    grid_shape = (members, rows, chans, nlon)
    lined = jax.ShapeDtypeStruct((rows, depth, nlon), F32)
    edge = jax.ShapeDtypeStruct((halo, depth, nlon), BF16)
    taps_out = jax.ShapeDtypeStruct((size * size, depth, 128), BF16)

    def call(body, outs, scratch, work, *args):
        specs = [scalars if a is flags else whole for a in args]
        return pl.pallas_call(
            body,
            out_shape=outs,
            in_specs=specs,
            scratch_shapes=scratch,
            compiler_params=vmem,
            cost_estimate=pl.CostEstimate(
                flops=work, transcendentals=0, bytes_accessed=8 * rows * depth * nlon
            ),
        )(*args)

    def swap(x):
        flat = x.reshape((ens_parts * groups,) + x.shape[2:])
        flat = lax.all_to_all(flat, ("ens", "lat"), split_axis=0, concat_axis=0, tiled=True)
        return flat.reshape(x.shape)

    work = 2 * size * size * rows * depth * nlon
    partial, taps, mixer = call(
        prepare_kernel,
        (lined, taps_out, jax.ShapeDtypeStruct((2, ens_parts * height, depth), BF16)),
        [pltpu.VMEM((rows, depth, wide), BF16)],
        work,
        own,
        kernel,
        mix_weight,
        pick,
    )
    target = lax.dynamic_slice(
        truth, (ens_at * chan_share, 0, lat_at * share, 0), (chan_share, 2, share, degrees)
    )
    target = target.transpose(2, 1, 0, 3).reshape(share, used, degrees)
    target = jnp.pad(target, ((0, 0), (0, slots - used), (0, 0)))

    slab = legendre.reshape(rows, groups, share * degrees).transpose(1, 0, 2)
    line = math.gcd(rows * share * degrees, 128)
    slab = slab.reshape(groups, rows * share * degrees // line, line)

    def chunk(lines):
        return jax.ShapeDtypeStruct((ens_parts, groups, height, up(lines * share, 128)), BF16)

    half_scratch = [pltpu.VMEM((halo, depth, wide), BF16), pltpu.VMEM((halo, depth, nlon), BF16)]
    mixed, inner = call(
        near_kernel,
        (jax.ShapeDtypeStruct((halo, ens_parts * height, span), F32), edge),
        half_scratch,
        work // 2,
        flags,
        near,
        partial,
        taps,
        table,
        mixer,
    )
    slab, mixed = lax.optimization_barrier((slab, mixed))
    slab = lax.all_to_all(slab, "lat", split_axis=0, concat_axis=0, tiled=True)
    order_legendre = slab.reshape(nlat, share, degrees).transpose(1, 0, 2)
    sent, outer = call(
        functools.partial(far_kernel, share),
        (chunk(rows), edge),
        half_scratch,
        work // 2,
        flags,
        far,
        partial,
        taps,
        table,
        mixer,
        mixed,
    )
    got = swap(sent)
    got, held = lax.optimization_barrier((got, outer))
    near, far = partners(inner, held)
    back, grads = call(
        functools.partial(score_kernel, members, used, rows, halo),
        (
            chunk(rows + 2 * halo),
            jax.ShapeDtypeStruct((up(degrees, 128) // 128, share * ens * slots, 128), F32),
        ),
        [
            pltpu.VMEM((nlat * share, ens * slots), F32),
            pltpu.VMEM(((nlat + 2 * halo) * share, ens * slots), F32),
            pltpu.VMEM((degrees, degrees), BF16),
        ],
        work,
        got,
        order_legendre,
        target,
        degree_order.reshape(1, degrees),
    )
    returned = swap(back)
    packed = call(
        functools.partial(pack_kernel, members, used, per_owner),
        jax.ShapeDtypeStruct(
            (ens_parts, groups, members * share, up(used * per_owner, 128)), BF16
        ),
        [],
        work,
        grads,
    )
    owned = swap(packed)
    flipped = call(flip_kernel, taps_out, [], work // 8, kernel)
    grad_fields = call(
        functools.partial(backward_kernel, share),
        jax.ShapeDtypeStruct(grid_shape, BF16),
        [
            pltpu.VMEM((rows + 2 * halo, depth, wide), BF16),
            pltpu.VMEM((rows + 2 * halo, depth, nlon), F32),
            pltpu.VMEM((rows, depth, nlon), F32),
        ],
        work,
        flags,
        returned,
        near,
        far,
        inner,
        outer,
        flipped,
        mixer,
        table,
    )
    score_grad = call(
        functools.partial(unpack_kernel, members),
        jax.ShapeDtypeStruct((members, chans, per_owner, 2, orders), F32),
        [],
        work,
        owned,
    )
    return grad_fields.transpose(0, 2, 1, 3), score_grad.transpose(0, 1, 3, 4, 2)


def solution(mesh):
    placed = (P("ens", None, "lat", None), P(), P(), P("lat", None, None), P(), P())

    return jax.shard_map(
        local,
        mesh=mesh,
        in_specs=placed,
        out_specs=(P("ens", None, "lat", None), P("ens", None, None, None, "lat")),
        check_vma=False,
    )
```

```python
import functools
import math

import jax
import jax.numpy as jnp
import numpy as np
from jax import lax
from jax.experimental import pallas as pl
from jax.experimental.pallas import tpu as pltpu
from jax.sharding import PartitionSpec as P


smooth_width = 0.5
TILE = 16
F32 = jnp.float32
BF16 = jnp.bfloat16


def up(value, step):
    return -(-value // step) * step


def wave_table(nlon, orders, span):
    columns = np.arange(nlon, dtype=np.int64)
    number = np.arange(orders, dtype=np.int64)
    angles = (columns[:, None] * number[None, :] % nlon) * (2.0 * math.pi / nlon)
    table = np.zeros((nlon, 2, span), np.float32)
    for part, values in enumerate((np.cos(angles), -np.sin(angles))):
        table[:, part, :orders] = values / math.sqrt(nlon)
    return table.reshape(nlon, 2 * span).astype(jnp.bfloat16)


def partners(inner, outer):
    count = lax.axis_size("lat")
    near = [(i, i ^ 1) for i in range(count)]
    far = [(i, min(max(i + (1 if i % 2 else -1), 0), count - 1)) for i in range(count)]
    one = lax.ppermute(inner, "lat", near)
    other = lax.ppermute(outer, "lat", far)
    return one, other


def place():
    at, count = lax.axis_index("lat"), lax.axis_size("lat")
    return jnp.stack([at % 2, (at > 0) & (at < count - 1)]).astype(jnp.int32)


def fill_row(padded, row, value, half):
    depth, nlon = value.shape
    wide = padded.shape[-1]
    base = nlon // 128 * 128
    tail = [value[:, base:], value[:, :half]]
    if wide > nlon + 2 * half:
        tail.append(jnp.zeros((depth, wide - nlon - 2 * half), value.dtype))
    tail.append(value[:, nlon - half :])
    padded[row, :, :base] = value[:, :base].astype(padded.dtype)
    padded[row, :, base:] = jnp.concatenate(tail, axis=-1).astype(padded.dtype)


def tap_sum(padded, taps, c0, lines, size):
    wide = padded.shape[-1]
    total = None
    for q in range(size):
        part = None
        for row, p in lines:
            weight = jnp.tile(taps[p * size + q, pl.ds(c0, TILE), :], (1, wide // 128))
            term = weight * padded[row, pl.ds(c0, TILE), :]
            part = term if part is None else part + term
        part = part.astype(F32)
        shift = (size // 2 - q) % wide
        if shift:
            part = pltpu.roll(part, shift, 1)
        total = part if total is None else total + part
    return total


def spread_taps(kernel, taps, flip):
    size, _, chans = kernel.shape
    for p in range(size):
        plane = kernel[p].T
        for q in range(size):
            at = p * size + q
            at = size * size - 1 - at if flip else at
            value = jnp.broadcast_to(plane[:, q : q + 1], (chans, 128))
            value = jnp.concatenate([value] * (taps.shape[1] // chans), axis=0)
            taps[at] = value.astype(taps.dtype)


def joined(block, row):
    return jnp.concatenate([block[b, row].astype(F32) for b in range(block.shape[0])], axis=0)


def gelu_pair(x):
    scale = math.sqrt(2.0 / math.pi)
    square = x * x
    t = jnp.tanh(scale * x * (1.0 + 0.044715 * square))
    half = 0.5 * (1.0 + t)
    slope = half + 0.5 * x * (1.0 - t * t) * (scale * (1.0 + 3 * 0.044715 * square))
    return x * half, slope


def prepare_kernel(own, kernel, weight, pick, partial, mixer, padded, taps):
    members, rows, chans, nlon = own.shape
    depth = members * chans
    size = kernel.shape[0]
    half = size // 2
    spread_taps(kernel, taps, False)
    for row in range(rows):
        fill_row(padded, row, joined(own, row), half)

    @pl.loop(0, depth // TILE)
    def _(ct):
        c0 = pl.multiple_of(ct * TILE, TILE)
        for i in range(rows):
            lines = [(i + p - half, p) for p in range(size) if 0 <= i + p - half < rows]
            total = tap_sum(padded, taps, c0, lines, size)
            total = total + padded[i, pl.ds(c0, TILE), :].astype(F32)
            partial[i, pl.ds(c0, TILE), :] = total[:, :nlon]

    for r in range(2):
        lines = []
        for b in range(members):
            lines.append(jnp.dot(pick[r, b], weight[...], preferred_element_type=F32))
        mixer[r] = jnp.concatenate(lines, axis=1).astype(BF16)


def finish_rows(lower, present, edge, partial, kernel, table, mixer, slope, padded, act, taps):
    rows, depth, nlon = partial.shape
    size = kernel.shape[0]
    half = size // 2
    span = table.shape[1] // 2
    spread_taps(kernel, taps, False)
    for row in range(half):
        at = jnp.where(lower, row, half - 1 - row)
        value = joined(edge, at)
        if present is not None:
            value = jnp.where(present, value, jnp.zeros_like(value))
        fill_row(padded, row, value, half)

    @pl.loop(0, depth // TILE)
    def _(ct):
        c0 = pl.multiple_of(ct * TILE, TILE)
        for j in range(half):
            lines = [
                (row, jnp.where(lower, row - j, size - 1 - (row - j))) for row in range(j, half)
            ]
            at = jnp.where(lower, j, half - 1 - j)
            value = partial[jnp.where(lower, j, rows - 1 - j), pl.ds(c0, TILE), :]
            value = value + tap_sum(padded, taps, c0, lines, size)[:, :nlon]
            value, grad = gelu_pair(value)
            act[at, pl.ds(c0, TILE), :] = value.astype(BF16)
            slope[at, pl.ds(c0, TILE), :] = grad.astype(BF16)

    flat = act[...].reshape(half * depth, nlon)
    spectral = jnp.dot(flat, table[...], preferred_element_type=F32).astype(BF16)
    mixed = []
    for j in range(half):
        line = spectral[j * depth : (j + 1) * depth]
        mixed.append(
            jnp.dot(mixer[0], line[:, :span], preferred_element_type=F32)
            + jnp.dot(mixer[1], line[:, span:], preferred_element_type=F32)
        )
    return mixed


def near_kernel(flags, edge, partial, kernel, table, mixer, mixed, slope, padded, act, taps):
    lines = finish_rows(
        flags[0] == 1, None, edge, partial, kernel, table, mixer, slope, padded, act, taps
    )
    for j, line in enumerate(lines):
        mixed[j] = line.astype(BF16)


def far_kernel(share, flags, edge, partial, kernel, table, mixer, nearer, out, slope, padded, act, taps):
    owners, groups, height, lanes = out.shape
    lines = finish_rows(
        flags[0] != 1, flags[1] == 1, edge, partial, kernel, table, mixer, slope, padded, act, taps
    )
    lines = [nearer[j].astype(F32) for j in range(nearer.shape[0])] + lines
    for t in range(groups):
        pieces = [x[:, t * share : (t + 1) * share] for x in lines]
        if lanes > len(lines) * share:
            pieces.append(jnp.zeros((owners * height, lanes - len(lines) * share), F32))
        block = jnp.concatenate(pieces, axis=1)
        for e in range(owners):
            out[e, t] = block[e * height : (e + 1) * height].astype(BF16)


def flip_kernel(kernel, taps):
    spread_taps(kernel, taps, True)


def soft_sign(gaps):
    return gaps * lax.rsqrt(gaps * gaps + smooth_width * smooth_width)


def score_kernel(members, used, rows, halo, got, legendre, target, order, back, grads, spread, gather, picked):
    owners, groups, height, lanes = got.shape
    orders, nlat, degrees = legendre.shape
    slots = target.shape[1]
    ens = owners * members
    for t in range(groups):
        pieces = []
        for e in range(owners):
            block = got[e, t].astype(F32)
            for b in range(members):
                pieces.append(block[b * used : (b + 1) * used])
                if slots > used:
                    pieces.append(jnp.zeros((slots - used, lanes), F32))
        block = jnp.concatenate(pieces, axis=0).T
        at, part = t * rows * orders, halo * orders
        first, second = (at, at + part) if t % 2 else (at + part, at)
        spread[first : first + part, :] = block[:part]
        spread[second : second + part, :] = block[part : 2 * part]
    reorder = jnp.where(
        lax.broadcasted_iota(jnp.int32, (degrees, degrees), 0) == order[...], 1.0, 0.0
    )
    picked[...] = reorder.astype(BF16)
    edge = halo * orders
    gather[:edge, :] = jnp.zeros((edge, ens * slots), F32)
    gather[edge + nlat * orders :, :] = jnp.zeros((edge, ens * slots), F32)

    def score(values, truth):
        own = [values[k * slots : (k + 1) * slots] for k in range(ens)]
        sums = [None] * ens
        for k in range(ens):
            for n in range(k + 1, ens):
                sign = soft_sign(own[k] - own[n])
                sums[k] = sign if sums[k] is None else sums[k] + sign
                sums[n] = -sign if sums[n] is None else sums[n] - sign
        return jnp.concatenate(
            [
                soft_sign(own[k] - truth) * (1.0 / ens) - sums[k] * (1.0 / (ens * (ens - 1)))
                for k in range(ens)
            ],
            axis=0,
        )

    tail = degrees % 128
    packs = tail > 0 and 128 % tail == 0 and orders % (128 // tail) == 0
    step = 128 // tail if packs else 1
    body = degrees - tail if packs else degrees

    @pl.loop(0, orders // step)
    def _(trip):
        numbers = [trip * step + j for j in range(step)]
        coeffs = [
            lax.dot_general(
                spread[pl.ds(m, nlat, stride=orders), :].astype(BF16),
                legendre[m],
                (((0,), (0,)), ((), ())),
                preferred_element_type=F32,
            )
            for m in numbers
        ]
        truths = [target[m].astype(F32) for m in numbers]
        scored = [score(x[:, :body], y[:, :body]) for x, y in zip(coeffs, truths)]
        if packs:
            rest = score(
                jnp.concatenate([x[:, body:] for x in coeffs], axis=1),
                jnp.concatenate([y[:, body:] for y in truths], axis=1),
            )
            scored = [
                jnp.concatenate([x, rest[:, j * tail : (j + 1) * tail]], axis=1)
                for j, x in enumerate(scored)
            ]
        for m, grad in zip(numbers, scored):
            grad = grad.astype(BF16)
            gather[pl.ds(edge + m, nlat, stride=orders), :] = lax.dot_general(
                legendre[m], grad, (((1,), (1,)), ((), ())), preferred_element_type=F32
            )
            at = pl.multiple_of(m * ens * slots, 8)
            ordered = jnp.dot(grad, picked[...], preferred_element_type=F32)
            for j in range(grads.shape[0]):
                last = min(degrees, (j + 1) * 128)
                grads[j, pl.ds(at, ens * slots), : last - j * 128] = ordered[:, j * 128 : last].astype(BF16)

    wide = back.shape[3]
    tall = (rows + 2 * halo) * orders
    for t in range(groups):
        at = t * rows * orders
        block = gather[at : at + tall, :]
        if wide > tall:
            block = jnp.concatenate([block, jnp.zeros((wide - tall, ens * slots), F32)], axis=0)
        block = block.T
        for e in range(owners):
            pieces = []
            for b in range(members):
                at = (e * members + b) * slots
                pieces.append(block[at : at + used])
            if height > members * used:
                pieces.append(jnp.zeros((height - members * used, wide), F32))
            back[e, t] = jnp.concatenate(pieces, axis=0).astype(BF16)


def backward_kernel(share, flags, got, near, far, inner, outer, taps, mixer, table, out, padded, flat, stage):
    owners, groups, height, _ = got.shape
    half, depth, nlon = inner.shape
    members, rows, chans, _ = out.shape
    size = math.isqrt(taps.shape[0])
    span = table.shape[1] // 2
    total = rows + 2 * half
    blocks = [
        jnp.concatenate([got[e, t].astype(F32) for e in range(owners)], axis=0) for t in range(groups)
    ]
    lines = []
    for i in range(total):
        pieces = [x[:, i * share : (i + 1) * share] for x in blocks]
        pieces.append(jnp.zeros((owners * height, span - groups * share), F32))
        line = jnp.concatenate(pieces, axis=1).astype(BF16)
        lines.append(
            jnp.concatenate(
                [
                    lax.dot_general(
                        mixer[r], line, (((0,), (0,)), ((), ())), preferred_element_type=F32
                    ).astype(BF16)
                    for r in range(2)
                ],
                axis=1,
            )
        )
    flat[...] = lax.dot_general(
        jnp.concatenate(lines, axis=0),
        table[...],
        (((1,), (1,)), ((), ())),
        preferred_element_type=F32,
    ).reshape(flat.shape)
    odd = flags[0] == 1
    pairs = ((near, far), (inner, outer), (outer, inner), (far, near))
    for part, (one, other) in enumerate(pairs):
        for row in range(half):
            at = part * half + row
            slope = jnp.where(odd, one[row].astype(F32), other[row].astype(F32))
            fill_row(padded, at, flat[at] * slope, half)

    @pl.loop(0, depth // TILE)
    def _(ct):
        c0 = pl.multiple_of(ct * TILE, TILE)

        @pl.loop(0, rows)
        def _(i):
            value = tap_sum(padded, taps, c0, [(i + p, p) for p in range(size)], size)
            value = value + padded[i + half, pl.ds(c0, TILE), :].astype(F32)
            stage[i, pl.ds(c0, TILE), :] = value[:, :nlon]

    for b in range(members):
        for i in range(rows):
            out[b, i] = stage[i, b * chans : (b + 1) * chans, :].astype(BF16)


def pack_kernel(members, used, per_owner, rounded, out, grads):
    owners, groups, depth, lanes = out.shape
    share = depth // members
    stride = grads.shape[1] // share
    grads[...] = rounded[...].astype(F32)
    slots = stride // (owners * members)
    for e in range(owners):
        for b in range(members):
            at = (e * members + b) * slots
            planes = [
                jnp.concatenate(
                    [grads[j, pl.ds(at + s, share, stride=stride), :] for j in range(grads.shape[0])],
                    axis=1,
                )
                for s in range(used)
            ]
            for t in range(groups):
                pieces = [x[:, t * per_owner : (t + 1) * per_owner] for x in planes]
                if lanes > used * per_owner:
                    pieces.append(jnp.zeros((share, lanes - used * per_owner), F32))
                out[e, t, b * share : (b + 1) * share, :] = jnp.concatenate(pieces, axis=1).astype(BF16)


def unpack_kernel(members, got, out):
    owners, groups, depth, lanes = got.shape
    _, chans, per_owner, _, orders = out.shape
    share, chan_share = depth // members, chans // owners
    pair = 2 * per_owner

    def iotas(shape):
        return (lax.broadcasted_iota(jnp.int32, shape, d) for d in range(2))

    row, column = iotas((chan_share * pair, lanes))
    wanted = ((row % 2) * chan_share + row // pair) * per_owner + (row % pair) // 2
    swapped = jnp.where(column == wanted, 1.0, 0.0).astype(BF16)
    row, column = iotas((groups * depth, orders))
    start = (column // share) * depth + column % share
    pickers = [jnp.where(row == start + b * share, 1.0, 0.0).astype(BF16) for b in range(members)]
    for e in range(owners):
        turned = lax.dot_general(
            swapped,
            got[e].reshape(groups * depth, lanes),
            (((1,), (1,)), ((), ())),
            preferred_element_type=F32,
        ).astype(BF16)
        for b in range(members):
            lines = jnp.dot(turned, pickers[b], preferred_element_type=F32)
            for c in range(chan_share):
                block = lines[c * pair : (c + 1) * pair]
                out[b, e * chan_share + c] = block.reshape(per_owner, 2, orders)


def local(fields, depth_kernel, mix_weight, legendre, truth, degree_order):
    ens_parts, groups = lax.axis_size("ens"), lax.axis_size("lat")
    ens_at, lat_at = lax.axis_index("ens"), lax.axis_index("lat")
    members, chans, rows, nlon = fields.shape
    _, orders, degrees = legendre.shape
    ens = members * ens_parts
    nlat = rows * groups
    share, per_owner, chan_share = orders // groups, degrees // groups, chans // ens_parts
    used = 2 * chan_share
    slots = up(used, 8)
    height = up(members * used, 8)
    span = up(orders, 128)
    size = depth_kernel.shape[1]
    halo = size // 2
    wide = up(nlon + 2 * halo, 128)
    depth = members * chans

    table = jnp.asarray(wave_table(nlon, orders, span))
    kernel = depth_kernel.transpose(1, 2, 0)
    flags = place()
    own = fields.transpose(0, 2, 1, 3)
    odd = lat_at % 2
    near, far = partners(
        lax.dynamic_slice_in_dim(own, (1 - odd) * (rows - halo), halo, 1),
        lax.dynamic_slice_in_dim(own, odd * (rows - halo), halo, 1),
    )

    pick = np.zeros((2, members, ens_parts, height, chans), np.float32)
    for r in range(2):
        for b in range(members):
            for o in range(chans):
                at = b * used + r * chan_share + o % chan_share
                pick[r, b, o // chan_share, at, o] = 1.0
    pick = jnp.asarray(pick.reshape(2, members, ens_parts * height, chans).astype(jnp.bfloat16))

    def grant(mebibytes):
        return pltpu.CompilerParams(vmem_limit_bytes=mebibytes * 1024 * 1024)

    scalars = pl.BlockSpec(memory_space=pltpu.SMEM)
    whole = pl.BlockSpec(memory_space=pltpu.VMEM)
    grid_shape = (members, rows, chans, nlon)
    lined = jax.ShapeDtypeStruct((rows, depth, nlon), F32)
    edge = jax.ShapeDtypeStruct((halo, depth, nlon), BF16)
    taps_out = jax.ShapeDtypeStruct((size * size, depth, 128), BF16)

    def call(body, outs, scratch, name, work, *args):
        specs = [scalars if a is flags else whole for a in args]
        return pl.pallas_call(
            body,
            out_shape=outs,
            in_specs=specs,
            scratch_shapes=scratch,
            compiler_params=grant(60 if name in ("prepare", "nearer", "farther") else 28),
            cost_estimate=pl.CostEstimate(
                flops=work, transcendentals=0, bytes_accessed=8 * rows * depth * nlon
            ),
        )(*args)

    def swap(x):
        flat = x.reshape((ens_parts * groups,) + x.shape[2:])
        flat = lax.all_to_all(flat, ("ens", "lat"), split_axis=0, concat_axis=0, tiled=True)
        return flat.reshape(x.shape)

    work = 2 * size * size * rows * depth * nlon
    partial, mixer = call(
        prepare_kernel,
        (lined, jax.ShapeDtypeStruct((2, ens_parts * height, depth), BF16)),
        [pltpu.VMEM((rows, depth, wide), BF16), pltpu.VMEM(taps_out.shape, BF16)],
        "prepare",
        work,
        own,
        kernel,
        mix_weight,
        pick,
    )
    target = lax.dynamic_slice(
        truth, (ens_at * chan_share, 0, lat_at * share, 0), (chan_share, 2, share, degrees)
    )
    target = target.transpose(2, 1, 0, 3).reshape(share, used, degrees)
    target = jnp.pad(target, ((0, 0), (0, slots - used), (0, 0)))

    slab = legendre.reshape(rows, groups, share * degrees).transpose(1, 0, 2)
    line = math.gcd(rows * share * degrees, 128)
    slab = slab.reshape(groups, rows * share * degrees // line, line)

    def chunk(lines):
        return jax.ShapeDtypeStruct((ens_parts, groups, height, up(lines * share, 128)), BF16)

    half_scratch = [
        pltpu.VMEM((halo, depth, wide), BF16),
        pltpu.VMEM((halo, depth, nlon), BF16),
        pltpu.VMEM(taps_out.shape, BF16),
    ]
    mixed, inner = call(
        near_kernel,
        (jax.ShapeDtypeStruct((halo, ens_parts * height, span), BF16), edge),
        half_scratch,
        "nearer",
        work // 2,
        flags,
        near,
        partial,
        kernel,
        table,
        mixer,
    )
    slab, mixed = lax.optimization_barrier((slab, mixed))
    slab = lax.all_to_all(slab, "lat", split_axis=0, concat_axis=0, tiled=True)
    order_legendre = slab.reshape(nlat, share, degrees).transpose(1, 0, 2)
    sent, outer = call(
        functools.partial(far_kernel, share),
        (chunk(rows), edge),
        half_scratch,
        "farther",
        work // 2,
        flags,
        far,
        partial,
        kernel,
        table,
        mixer,
        mixed,
    )
    got = swap(sent)
    got, held = lax.optimization_barrier((got, outer))
    near, far = partners(inner, held)
    back, grads = call(
        functools.partial(score_kernel, members, used, rows, halo),
        (
            chunk(rows + 2 * halo),
            jax.ShapeDtypeStruct((up(degrees, 128) // 128, share * ens * slots, 128), BF16),
        ),
        [
            pltpu.VMEM((nlat * share, ens * slots), F32),
            pltpu.VMEM(((nlat + 2 * halo) * share, ens * slots), F32),
            pltpu.VMEM((degrees, degrees), BF16),
        ],
        "score",
        work,
        got,
        order_legendre,
        target,
        degree_order.reshape(1, degrees),
    )
    returned = swap(back)
    packed = call(
        functools.partial(pack_kernel, members, used, per_owner),
        jax.ShapeDtypeStruct(
            (ens_parts, groups, members * share, up(used * per_owner, 128)), BF16
        ),
        [pltpu.VMEM(grads.shape, F32)],
        "pack",
        work,
        grads,
    )
    owned = swap(packed)
    flipped = call(flip_kernel, taps_out, [], "flip", work // 8, kernel)
    grad_fields = call(
        functools.partial(backward_kernel, share),
        jax.ShapeDtypeStruct(grid_shape, BF16),
        [
            pltpu.VMEM((rows + 2 * halo, depth, wide), BF16),
            pltpu.VMEM((rows + 2 * halo, depth, nlon), F32),
            pltpu.VMEM((rows, depth, nlon), F32),
        ],
        "backward",
        work,
        flags,
        returned,
        near,
        far,
        inner,
        outer,
        flipped,
        mixer,
        table,
    )
    score_grad = call(
        functools.partial(unpack_kernel, members),
        jax.ShapeDtypeStruct((members, chans, per_owner, 2, orders), F32),
        [],
        "unpack",
        work,
        owned,
    )
    return grad_fields.transpose(0, 2, 1, 3), score_grad.transpose(0, 1, 3, 4, 2)


def solution(mesh):
    placed = (P("ens", None, "lat", None), P(), P(), P("lat", None, None), P(), P())

    return jax.shard_map(
        local,
        mesh=mesh,
        in_specs=placed,
        out_specs=(P("ens", None, "lat", None), P("ens", None, None, None, "lat")),
        check_vma=False,
    )
```

```python
import functools
import math

import jax
import jax.numpy as jnp
import numpy as np
from jax import lax
from jax.experimental import pallas as pl
from jax.experimental.pallas import tpu as pltpu
from jax.sharding import PartitionSpec as P


smooth_width = 0.5
TILE = 16
F32 = jnp.float32
BF16 = jnp.bfloat16


def up(value, step):
    return -(-value // step) * step


def wave_table(nlon, orders, span):
    columns = np.arange(nlon, dtype=np.int64)
    number = np.arange(orders, dtype=np.int64)
    angles = (columns[:, None] * number[None, :] % nlon) * (2.0 * math.pi / nlon)
    table = np.zeros((nlon, 2, span), np.float32)
    for part, values in enumerate((np.cos(angles), -np.sin(angles))):
        table[:, part, :orders] = values / math.sqrt(nlon)
    return table.reshape(nlon, 2 * span).astype(jnp.bfloat16)


def partners(inner, outer):
    count = lax.axis_size("lat")
    near = [(i, i ^ 1) for i in range(count)]
    far = [(i, (i + (1 if i % 2 else -1)) % count) for i in range(count)]
    one = lax.ppermute(inner, "lat", near)
    other = lax.ppermute(outer, "lat", far)
    return one, other


def place():
    at, count = lax.axis_index("lat"), lax.axis_size("lat")
    return jnp.stack([at % 2, (at > 0) & (at < count - 1)]).astype(jnp.int32)


def fill_row(padded, row, value, half):
    depth, nlon = value.shape
    wide = padded.shape[-1]
    base = nlon // 128 * 128
    tail = [value[:, base:], value[:, :half]]
    if wide > nlon + 2 * half:
        tail.append(jnp.zeros((depth, wide - nlon - 2 * half), value.dtype))
    tail.append(value[:, nlon - half :])
    padded[row, :, :base] = value[:, :base].astype(padded.dtype)
    padded[row, :, base:] = jnp.concatenate(tail, axis=-1).astype(padded.dtype)


def tap_sum(padded, taps, c0, lines, size):
    wide = padded.shape[-1]
    total = None
    for q in range(size):
        part = None
        for row, p in lines:
            weight = jnp.tile(taps[p * size + q, pl.ds(c0, TILE), :], (1, wide // 128))
            term = weight * padded[row, pl.ds(c0, TILE), :]
            part = term if part is None else part + term
        part = part.astype(F32)
        shift = (size // 2 - q) % wide
        if shift:
            part = pltpu.roll(part, shift, 1)
        total = part if total is None else total + part
    return total


def spread_taps(kernel, taps, flip):
    size, _, chans = kernel.shape
    for p in range(size):
        plane = kernel[p].T
        for q in range(size):
            at = p * size + q
            at = size * size - 1 - at if flip else at
            value = jnp.broadcast_to(plane[:, q : q + 1], (chans, 128))
            value = jnp.concatenate([value] * (taps.shape[1] // chans), axis=0)
            taps[at] = value.astype(taps.dtype)


def joined(block, row):
    return jnp.concatenate([block[b, row].astype(F32) for b in range(block.shape[0])], axis=0)


def gelu_pair(x):
    scale = math.sqrt(2.0 / math.pi)
    square = x * x
    t = jnp.tanh(scale * x * (1.0 + 0.044715 * square))
    half = 0.5 * (1.0 + t)
    slope = half + 0.5 * x * (1.0 - t * t) * (scale * (1.0 + 3 * 0.044715 * square))
    return x * half, slope


def prepare_kernel(own, kernel, weight, pick, partial, mixer, padded, taps):
    members, rows, chans, nlon = own.shape
    depth = members * chans
    size = kernel.shape[0]
    half = size // 2
    spread_taps(kernel, taps, False)
    for row in range(rows):
        fill_row(padded, row, joined(own, row), half)

    @pl.loop(0, depth // TILE)
    def _(ct):
        c0 = pl.multiple_of(ct * TILE, TILE)
        for i in range(rows):
            lines = [(i + p - half, p) for p in range(size) if 0 <= i + p - half < rows]
            total = tap_sum(padded, taps, c0, lines, size)
            total = total + padded[i, pl.ds(c0, TILE), :].astype(F32)
            partial[i, pl.ds(c0, TILE), :] = total[:, :nlon]

    for r in range(2):
        lines = []
        for b in range(members):
            lines.append(jnp.dot(pick[r, b], weight[...], preferred_element_type=F32))
        mixer[r] = jnp.concatenate(lines, axis=1).astype(BF16)


def finish_rows(lower, present, edge, partial, kernel, table, mixer, slope, padded, act, taps):
    rows, depth, nlon = partial.shape
    size = kernel.shape[0]
    half = size // 2
    span = table.shape[1] // 2
    spread_taps(kernel, taps, False)
    for row in range(half):
        at = jnp.where(lower, row, half - 1 - row)
        value = joined(edge, at)
        if present is not None:
            value = jnp.where(present, value, jnp.zeros_like(value))
        fill_row(padded, row, value, half)

    @pl.loop(0, depth // TILE)
    def _(ct):
        c0 = pl.multiple_of(ct * TILE, TILE)
        for j in range(half):
            lines = [
                (row, jnp.where(lower, row - j, size - 1 - (row - j))) for row in range(j, half)
            ]
            at = jnp.where(lower, j, half - 1 - j)
            value = partial[jnp.where(lower, j, rows - 1 - j), pl.ds(c0, TILE), :]
            value = value + tap_sum(padded, taps, c0, lines, size)[:, :nlon]
            value, grad = gelu_pair(value)
            act[at, pl.ds(c0, TILE), :] = value.astype(BF16)
            slope[at, pl.ds(c0, TILE), :] = grad.astype(BF16)

    flat = act[...].reshape(half * depth, nlon)
    spectral = jnp.dot(flat, table[...], preferred_element_type=F32).astype(BF16)
    mixed = []
    for j in range(half):
        line = spectral[j * depth : (j + 1) * depth]
        mixed.append(
            jnp.dot(mixer[0], line[:, :span], preferred_element_type=F32)
            + jnp.dot(mixer[1], line[:, span:], preferred_element_type=F32)
        )
    return mixed


def near_kernel(flags, edge, partial, kernel, table, mixer, mixed, slope, padded, act, taps):
    lines = finish_rows(
        flags[0] == 1, None, edge, partial, kernel, table, mixer, slope, padded, act, taps
    )
    for j, line in enumerate(lines):
        mixed[j] = line.astype(BF16)


def far_kernel(share, flags, edge, partial, kernel, table, mixer, nearer, out, slope, padded, act, taps):
    owners, groups, height, lanes = out.shape
    lines = finish_rows(
        flags[0] != 1, flags[1] == 1, edge, partial, kernel, table, mixer, slope, padded, act, taps
    )
    lines = [nearer[j].astype(F32) for j in range(nearer.shape[0])] + lines
    for t in range(groups):
        pieces = [x[:, t * share : (t + 1) * share] for x in lines]
        if lanes > len(lines) * share:
            pieces.append(jnp.zeros((owners * height, lanes - len(lines) * share), F32))
        block = jnp.concatenate(pieces, axis=1)
        for e in range(owners):
            out[e, t] = block[e * height : (e + 1) * height].astype(BF16)


def flip_kernel(kernel, taps):
    spread_taps(kernel, taps, True)


def soft_sign(gaps):
    return gaps * lax.rsqrt(gaps * gaps + smooth_width * smooth_width)


def score_kernel(members, used, rows, halo, got, legendre, target, order, back, drained, spread, gather, picked, grads, sent):
    owners, groups, height, lanes = got.shape
    orders, nlat, degrees = legendre.shape
    slots = target.shape[1]
    ens = owners * members
    for t in range(groups):
        pieces = []
        for e in range(owners):
            block = got[e, t].astype(F32)
            for b in range(members):
                pieces.append(block[b * used : (b + 1) * used])
                if slots > used:
                    pieces.append(jnp.zeros((slots - used, lanes), F32))
        block = jnp.concatenate(pieces, axis=0).T
        at, part = t * rows * orders, halo * orders
        first, second = (at, at + part) if t % 2 else (at + part, at)
        spread[first : first + part, :] = block[:part]
        spread[second : second + part, :] = block[part : 2 * part]
    reorder = jnp.where(
        lax.broadcasted_iota(jnp.int32, (degrees, degrees), 0) == order[...], 1.0, 0.0
    )
    picked[...] = reorder.astype(BF16)
    edge = halo * orders
    gather[:edge, :] = jnp.zeros((edge, ens * slots), F32)
    gather[edge + nlat * orders :, :] = jnp.zeros((edge, ens * slots), F32)

    def score(values, truth):
        own = [values[k * slots : (k + 1) * slots] for k in range(ens)]
        sums = [None] * ens
        for k in range(ens):
            for n in range(k + 1, ens):
                sign = soft_sign(own[k] - own[n])
                sums[k] = sign if sums[k] is None else sums[k] + sign
                sums[n] = -sign if sums[n] is None else sums[n] - sign
        return jnp.concatenate(
            [
                soft_sign(own[k] - truth) * (1.0 / ens) - sums[k] * (1.0 / (ens * (ens - 1)))
                for k in range(ens)
            ],
            axis=0,
        )

    tail = degrees % 128
    packs = tail > 0 and 128 % tail == 0 and orders % (128 // tail) == 0
    step = 128 // tail if packs else 1
    body = degrees - tail if packs else degrees

    span = step * ens * slots

    def drain(trip):
        lines = pl.ds(pl.multiple_of(trip * span, 8), span)
        return pltpu.make_async_copy(grads.at[:, lines], drained.at[:, lines], sent.at[trip])

    @pl.loop(0, orders // step)
    def _(trip):
        numbers = [trip * step + j for j in range(step)]
        coeffs = [
            lax.dot_general(
                spread[pl.ds(m, nlat, stride=orders), :].astype(BF16),
                legendre[m],
                (((0,), (0,)), ((), ())),
                preferred_element_type=F32,
            )
            for m in numbers
        ]
        truths = [target[m].astype(F32) for m in numbers]
        scored = [score(x[:, :body], y[:, :body]) for x, y in zip(coeffs, truths)]
        if packs:
            rest = score(
                jnp.concatenate([x[:, body:] for x in coeffs], axis=1),
                jnp.concatenate([y[:, body:] for y in truths], axis=1),
            )
            scored = [
                jnp.concatenate([x, rest[:, j * tail : (j + 1) * tail]], axis=1)
                for j, x in enumerate(scored)
            ]
        for m, grad in zip(numbers, scored):
            grad = grad.astype(BF16)
            gather[pl.ds(edge + m, nlat, stride=orders), :] = lax.dot_general(
                legendre[m], grad, (((1,), (1,)), ((), ())), preferred_element_type=F32
            )
            at = pl.multiple_of(m * ens * slots, 8)
            ordered = jnp.dot(grad, picked[...], preferred_element_type=F32)
            for j in range(grads.shape[0]):
                last = min(degrees, (j + 1) * 128)
                grads[j, pl.ds(at, ens * slots), : last - j * 128] = ordered[:, j * 128 : last].astype(BF16)
        drain(trip).start()

    wide = back.shape[3]
    tall = (rows + 2 * halo) * orders
    for t in range(groups):
        at = t * rows * orders
        block = gather[at : at + tall, :]
        if wide > tall:
            block = jnp.concatenate([block, jnp.zeros((wide - tall, ens * slots), F32)], axis=0)
        block = block.T
        for e in range(owners):
            pieces = []
            for b in range(members):
                at = (e * members + b) * slots
                pieces.append(block[at : at + used])
            if height > members * used:
                pieces.append(jnp.zeros((height - members * used, wide), F32))
            back[e, t] = jnp.concatenate(pieces, axis=0).astype(BF16)

    @pl.loop(0, orders // step)
    def _(trip):
        drain(trip).wait()


def backward_kernel(share, flags, got, near, far, inner, outer, taps, mixer, table, out, padded, flat, stage):
    owners, groups, height, _ = got.shape
    half, depth, nlon = inner.shape
    members, rows, chans, _ = out.shape
    size = math.isqrt(taps.shape[0])
    span = table.shape[1] // 2
    total = rows + 2 * half
    blocks = [
        jnp.concatenate([got[e, t].astype(F32) for e in range(owners)], axis=0) for t in range(groups)
    ]
    lines = []
    for i in range(total):
        pieces = [x[:, i * share : (i + 1) * share] for x in blocks]
        pieces.append(jnp.zeros((owners * height, span - groups * share), F32))
        line = jnp.concatenate(pieces, axis=1).astype(BF16)
        lines.append(
            jnp.concatenate(
                [
                    lax.dot_general(
                        mixer[r], line, (((0,), (0,)), ((), ())), preferred_element_type=F32
                    ).astype(BF16)
                    for r in range(2)
                ],
                axis=1,
            )
        )
    flat[...] = lax.dot_general(
        jnp.concatenate(lines, axis=0),
        table[...],
        (((1,), (1,)), ((), ())),
        preferred_element_type=F32,
    ).reshape(flat.shape)
    odd = flags[0] == 1
    pairs = ((near, far), (inner, outer), (outer, inner), (far, near))
    for part, (one, other) in enumerate(pairs):
        for row in range(half):
            at = part * half + row
            slope = jnp.where(odd, one[row].astype(F32), other[row].astype(F32))
            fill_row(padded, at, flat[at] * slope, half)

    @pl.loop(0, depth // TILE)
    def _(ct):
        c0 = pl.multiple_of(ct * TILE, TILE)

        @pl.loop(0, rows)
        def _(i):
            value = tap_sum(padded, taps, c0, [(i + p, p) for p in range(size)], size)
            value = value + padded[i + half, pl.ds(c0, TILE), :].astype(F32)
            stage[i, pl.ds(c0, TILE), :] = value[:, :nlon]

    for b in range(members):
        for i in range(rows):
            out[b, i] = stage[i, b * chans : (b + 1) * chans, :].astype(BF16)


def pack_kernel(members, used, per_owner, rounded, out, grads):
    owners, groups, depth, lanes = out.shape
    share = depth // members
    stride = grads.shape[1] // share
    grads[...] = rounded[...].astype(F32)
    slots = stride // (owners * members)
    for e in range(owners):
        for b in range(members):
            at = (e * members + b) * slots
            planes = [
                jnp.concatenate(
                    [grads[j, pl.ds(at + s, share, stride=stride), :] for j in range(grads.shape[0])],
                    axis=1,
                )
                for s in range(used)
            ]
            for t in range(groups):
                pieces = [x[:, t * per_owner : (t + 1) * per_owner] for x in planes]
                if lanes > used * per_owner:
                    pieces.append(jnp.zeros((share, lanes - used * per_owner), F32))
                out[e, t, b * share : (b + 1) * share, :] = jnp.concatenate(pieces, axis=1).astype(BF16)


def unpack_kernel(members, got, result, out, sent):
    owners, groups, depth, lanes = got.shape
    _, chans, per_owner, _, orders = out.shape
    share, chan_share = depth // members, chans // owners
    pair = 2 * per_owner

    def iotas(shape):
        return (lax.broadcasted_iota(jnp.int32, shape, d) for d in range(2))

    row, column = iotas((chan_share * pair, lanes))
    wanted = ((row % 2) * chan_share + row // pair) * per_owner + (row % pair) // 2
    swapped = jnp.where(column == wanted, 1.0, 0.0).astype(BF16)
    row, column = iotas((groups * depth, orders))
    start = (column // share) * depth + column % share
    pickers = [jnp.where(row == start + b * share, 1.0, 0.0).astype(BF16) for b in range(members)]
    copies = []
    for e in range(owners):
        turned = lax.dot_general(
            swapped,
            got[e].reshape(groups * depth, lanes),
            (((1,), (1,)), ((), ())),
            preferred_element_type=F32,
        ).astype(BF16)
        for b in range(members):
            lines = jnp.dot(turned, pickers[b], preferred_element_type=F32)
            for c in range(chan_share):
                block = lines[c * pair : (c + 1) * pair]
                out[b, e * chan_share + c] = block.reshape(per_owner, 2, orders)
            place = pl.ds(e * chan_share, chan_share)
            copies.append(
                pltpu.make_async_copy(out.at[b, place], result.at[b, place], sent.at[e, b])
            )
            copies[-1].start()
    for copy in copies:
        copy.wait()


def local(fields, depth_kernel, mix_weight, legendre, truth, degree_order):
    ens_parts, groups = lax.axis_size("ens"), lax.axis_size("lat")
    ens_at, lat_at = lax.axis_index("ens"), lax.axis_index("lat")
    members, chans, rows, nlon = fields.shape
    _, orders, degrees = legendre.shape
    ens = members * ens_parts
    nlat = rows * groups
    share, per_owner, chan_share = orders // groups, degrees // groups, chans // ens_parts
    used = 2 * chan_share
    slots = up(used, 8)
    height = up(members * used, 8)
    span = up(orders, 128)
    size = depth_kernel.shape[1]
    halo = size // 2
    wide = up(nlon + 2 * halo, 128)
    depth = members * chans

    table = jnp.asarray(wave_table(nlon, orders, span))
    kernel = depth_kernel.transpose(1, 2, 0)
    flags = place()
    own = fields.transpose(0, 2, 1, 3)
    odd = lat_at % 2
    near, far = partners(
        lax.dynamic_slice_in_dim(own, (1 - odd) * (rows - halo), halo, 1),
        lax.dynamic_slice_in_dim(own, odd * (rows - halo), halo, 1),
    )

    pick = np.zeros((2, members, ens_parts, height, chans), np.float32)
    for r in range(2):
        for b in range(members):
            for o in range(chans):
                at = b * used + r * chan_share + o % chan_share
                pick[r, b, o // chan_share, at, o] = 1.0
    pick = jnp.asarray(pick.reshape(2, members, ens_parts * height, chans).astype(jnp.bfloat16))

    def grant(mebibytes):
        return pltpu.CompilerParams(vmem_limit_bytes=mebibytes * 1024 * 1024)

    scalars = pl.BlockSpec(memory_space=pltpu.SMEM)
    whole = pl.BlockSpec(memory_space=pltpu.VMEM)
    grid_shape = (members, rows, chans, nlon)
    lined = jax.ShapeDtypeStruct((rows, depth, nlon), F32)
    edge = jax.ShapeDtypeStruct((halo, depth, nlon), BF16)
    taps_out = jax.ShapeDtypeStruct((size * size, depth, 128), BF16)

    def call(body, outs, scratch, name, work, *args, drained=()):
        outs = outs if isinstance(outs, tuple) else (outs,)
        places = [
            pl.BlockSpec(memory_space=pltpu.HBM if i in drained else pltpu.VMEM)
            for i in range(len(outs))
        ]
        specs = [scalars if a is flags else whole for a in args]
        made = pl.pallas_call(
            body,
            out_shape=outs,
            in_specs=specs,
            out_specs=tuple(places),
            scratch_shapes=scratch,
            compiler_params=grant(60 if name in ("prepare", "nearer", "farther") else 28),
            cost_estimate=pl.CostEstimate(
                flops=work, transcendentals=0, bytes_accessed=8 * rows * depth * nlon
            ),
        )(*args)
        return made if len(outs) > 1 else made[0]

    def swap(x):
        flat = x.reshape((ens_parts * groups,) + x.shape[2:])
        flat = lax.all_to_all(flat, ("ens", "lat"), split_axis=0, concat_axis=0, tiled=True)
        return flat.reshape(x.shape)

    work = 2 * size * size * rows * depth * nlon
    partial, mixer = call(
        prepare_kernel,
        (lined, jax.ShapeDtypeStruct((2, ens_parts * height, depth), BF16)),
        [pltpu.VMEM((rows, depth, wide), BF16), pltpu.VMEM(taps_out.shape, BF16)],
        "prepare",
        work,
        own,
        kernel,
        mix_weight,
        pick,
    )
    target = lax.dynamic_slice(
        truth, (ens_at * chan_share, 0, lat_at * share, 0), (chan_share, 2, share, degrees)
    )
    target = target.transpose(2, 1, 0, 3).reshape(share, used, degrees)
    target = jnp.pad(target, ((0, 0), (0, slots - used), (0, 0)))

    slab = legendre.reshape(rows, groups, share * degrees).transpose(1, 0, 2)
    line = math.gcd(rows * share * degrees, 128)
    slab = slab.reshape(groups, rows * share * degrees // line, line)

    def chunk(lines):
        return jax.ShapeDtypeStruct((ens_parts, groups, height, up(lines * share, 128)), BF16)

    half_scratch = [
        pltpu.VMEM((halo, depth, wide), BF16),
        pltpu.VMEM((halo, depth, nlon), BF16),
        pltpu.VMEM(taps_out.shape, BF16),
    ]
    mixed, inner = call(
        near_kernel,
        (jax.ShapeDtypeStruct((halo, ens_parts * height, span), BF16), edge),
        half_scratch,
        "nearer",
        work // 2,
        flags,
        near,
        partial,
        kernel,
        table,
        mixer,
    )
    slab, mixed = lax.optimization_barrier((slab, mixed))
    slab = lax.all_to_all(slab, "lat", split_axis=0, concat_axis=0, tiled=True)
    order_legendre = slab.reshape(nlat, share, degrees).transpose(1, 0, 2)
    sent, outer = call(
        functools.partial(far_kernel, share),
        (chunk(rows), edge),
        half_scratch,
        "farther",
        work // 2,
        flags,
        far,
        partial,
        kernel,
        table,
        mixer,
        mixed,
    )
    got = swap(sent)
    got, held = lax.optimization_barrier((got, outer))
    near, far = partners(inner, held)
    back, grads = call(
        functools.partial(score_kernel, members, used, rows, halo),
        (
            chunk(rows + 2 * halo),
            pltpu.HBM((up(degrees, 128) // 128, share * ens * slots, 128), BF16),
        ),
        [
            pltpu.VMEM((nlat * share, ens * slots), F32),
            pltpu.VMEM(((nlat + 2 * halo) * share, ens * slots), F32),
            pltpu.VMEM((degrees, degrees), BF16),
            pltpu.VMEM((up(degrees, 128) // 128, share * ens * slots, 128), BF16),
            pltpu.SemaphoreType.DMA((share,)),
        ],
        "score",
        work,
        got,
        order_legendre,
        target,
        degree_order.reshape(1, degrees),
        drained=(1,),
    )
    returned = swap(back)
    packed = call(
        functools.partial(pack_kernel, members, used, per_owner),
        jax.ShapeDtypeStruct(
            (ens_parts, groups, members * share, up(used * per_owner, 128)), BF16
        ),
        [pltpu.VMEM(grads.shape, F32)],
        "pack",
        work,
        grads,
    )
    owned = swap(packed)
    flipped = call(flip_kernel, taps_out, [], "flip", work // 8, kernel)
    grad_fields = call(
        functools.partial(backward_kernel, share),
        jax.ShapeDtypeStruct(grid_shape, BF16),
        [
            pltpu.VMEM((rows + 2 * halo, depth, wide), BF16),
            pltpu.VMEM((rows + 2 * halo, depth, nlon), F32),
            pltpu.VMEM((rows, depth, nlon), F32),
        ],
        "backward",
        work,
        flags,
        returned,
        near,
        far,
        inner,
        outer,
        flipped,
        mixer,
        table,
    )
    score_grad = call(
        functools.partial(unpack_kernel, members),
        jax.ShapeDtypeStruct((members, chans, per_owner, 2, orders), F32),
        [
            pltpu.VMEM((members, chans, per_owner, 2, orders), F32),
            pltpu.SemaphoreType.DMA((ens_parts, members)),
        ],
        "unpack",
        work,
        owned,
        drained=(0,),
    )
    return grad_fields.transpose(0, 2, 1, 3), score_grad.transpose(0, 1, 3, 4, 2)


def solution(mesh):
    placed = (P("ens", None, "lat", None), P(), P(), P("lat", None, None), P(), P())

    return jax.shard_map(
        local,
        mesh=mesh,
        in_specs=placed,
        out_specs=(P("ens", None, "lat", None), P("ens", None, None, None, "lat")),
        check_vma=False,
    )
```

```python
import functools
import math

import jax
import jax.numpy as jnp
import numpy as np
from jax import lax
from jax.experimental import pallas as pl
from jax.experimental.pallas import tpu as pltpu
from jax.sharding import PartitionSpec as P


smooth_width = 0.5
TILE = 16
F32 = jnp.float32
BF16 = jnp.bfloat16


def up(value, step):
    return -(-value // step) * step


def wave_table(nlon, orders, span):
    columns = np.arange(nlon, dtype=np.int64)
    number = np.arange(orders, dtype=np.int64)
    angles = (columns[:, None] * number[None, :] % nlon) * (2.0 * math.pi / nlon)
    table = np.zeros((nlon, 2, span), np.float32)
    for part, values in enumerate((np.cos(angles), -np.sin(angles))):
        table[:, part, :orders] = values / math.sqrt(nlon)
    return table.reshape(nlon, 2 * span).astype(jnp.bfloat16)


def partners(inner, outer):
    count = lax.axis_size("lat")
    near = [(i, i ^ 1) for i in range(count)]
    far = [(i, (i + (1 if i % 2 else -1)) % count) for i in range(count)]
    one = lax.ppermute(inner, "lat", near)
    other = lax.ppermute(outer, "lat", far)
    return one, other


def place():
    at, count = lax.axis_index("lat"), lax.axis_size("lat")
    return jnp.stack([at % 2, (at > 0) & (at < count - 1)]).astype(jnp.int32)


def fill_row(padded, row, value, half):
    depth, nlon = value.shape
    wide = padded.shape[-1]
    base = nlon // 128 * 128
    tail = [value[:, base:], value[:, :half]]
    if wide > nlon + 2 * half:
        tail.append(jnp.zeros((depth, wide - nlon - 2 * half), value.dtype))
    tail.append(value[:, nlon - half :])
    padded[row, :, :base] = value[:, :base].astype(padded.dtype)
    padded[row, :, base:] = jnp.concatenate(tail, axis=-1).astype(padded.dtype)


def tap_sum(padded, taps, c0, lines, size):
    wide = padded.shape[-1]
    total = None
    for q in range(size):
        part = None
        for row, p in lines:
            weight = jnp.tile(taps[p * size + q, pl.ds(c0, TILE), :], (1, wide // 128))
            term = weight * padded[row, pl.ds(c0, TILE), :]
            part = term if part is None else part + term
        part = part.astype(F32)
        shift = (size // 2 - q) % wide
        if shift:
            part = pltpu.roll(part, shift, 1)
        total = part if total is None else total + part
    return total


def spread_taps(kernel, taps, flip):
    size, _, chans = kernel.shape
    for p in range(size):
        plane = kernel[p].T
        for q in range(size):
            at = p * size + q
            at = size * size - 1 - at if flip else at
            value = jnp.broadcast_to(plane[:, q : q + 1], (chans, 128))
            value = jnp.concatenate([value] * (taps.shape[1] // chans), axis=0)
            taps[at] = value.astype(taps.dtype)


def joined(block, row):
    return jnp.concatenate([block[b, row].astype(F32) for b in range(block.shape[0])], axis=0)


def gelu_pair(x):
    scale = math.sqrt(2.0 / math.pi)
    square = x * x
    t = jnp.tanh(scale * x * (1.0 + 0.044715 * square))
    half = 0.5 * (1.0 + t)
    slope = half + 0.5 * x * (1.0 - t * t) * (scale * (1.0 + 3 * 0.044715 * square))
    return x * half, slope


def prepare_kernel(own, kernel, weight, pick, partial, mixer, padded, taps):
    members, rows, chans, nlon = own.shape
    depth = members * chans
    size = kernel.shape[0]
    half = size // 2
    spread_taps(kernel, taps, False)
    for row in range(rows):
        fill_row(padded, row, joined(own, row), half)

    @pl.loop(0, depth // TILE)
    def _(ct):
        c0 = pl.multiple_of(ct * TILE, TILE)
        for i in range(rows):
            lines = [(i + p - half, p) for p in range(size) if 0 <= i + p - half < rows]
            total = tap_sum(padded, taps, c0, lines, size)
            total = total + padded[i, pl.ds(c0, TILE), :].astype(F32)
            partial[i, pl.ds(c0, TILE), :] = total[:, :nlon]

    for r in range(2):
        lines = []
        for b in range(members):
            lines.append(jnp.dot(pick[r, b], weight[...], preferred_element_type=F32))
        mixer[r] = jnp.concatenate(lines, axis=1).astype(BF16)


def finish_rows(lower, present, edge, partial, kernel, table, mixer, slope, padded, act, taps, sums, waves, got):
    rows, depth, nlon = partial.shape
    size = kernel.shape[0]
    half = size // 2
    span = table.shape[1] // 2
    start = jnp.where(lower, 0, rows - half)
    fetch_sums = pltpu.make_async_copy(partial.at[pl.ds(start, half)], sums, got.at[0])
    fetch_waves = pltpu.make_async_copy(table, waves, got.at[1])
    fetch_sums.start()
    fetch_waves.start()
    spread_taps(kernel, taps, False)
    for row in range(half):
        at = jnp.where(lower, row, half - 1 - row)
        value = joined(edge, at)
        if present is not None:
            value = jnp.where(present, value, jnp.zeros_like(value))
        fill_row(padded, row, value, half)

    fetch_sums.wait()

    @pl.loop(0, depth // TILE)
    def _(ct):
        c0 = pl.multiple_of(ct * TILE, TILE)
        for j in range(half):
            lines = [
                (row, jnp.where(lower, row - j, size - 1 - (row - j))) for row in range(j, half)
            ]
            at = jnp.where(lower, j, half - 1 - j)
            value = sums[at, pl.ds(c0, TILE), :]
            value = value + tap_sum(padded, taps, c0, lines, size)[:, :nlon]
            value, grad = gelu_pair(value)
            act[at, pl.ds(c0, TILE), :] = value.astype(BF16)
            slope[at, pl.ds(c0, TILE), :] = grad.astype(BF16)

    fetch_waves.wait()
    flat = act[...].reshape(half * depth, nlon)
    spectral = jnp.dot(flat, waves[...], preferred_element_type=F32).astype(BF16)
    mixed = []
    for j in range(half):
        line = spectral[j * depth : (j + 1) * depth]
        mixed.append(
            jnp.dot(mixer[0], line[:, :span], preferred_element_type=F32)
            + jnp.dot(mixer[1], line[:, span:], preferred_element_type=F32)
        )
    return mixed


def near_kernel(flags, edge, partial, kernel, table, mixer, mixed, slope, *scratch):
    lines = finish_rows(
        flags[0] == 1, None, edge, partial, kernel, table, mixer, slope, *scratch
    )
    for j, line in enumerate(lines):
        mixed[j] = line.astype(BF16)


def far_kernel(share, flags, edge, partial, kernel, table, mixer, nearer, out, slope, *scratch):
    owners, groups, height, lanes = out.shape
    lines = finish_rows(
        flags[0] != 1, flags[1] == 1, edge, partial, kernel, table, mixer, slope, *scratch
    )
    lines = [nearer[j].astype(F32) for j in range(nearer.shape[0])] + lines
    for t in range(groups):
        pieces = [x[:, t * share : (t + 1) * share] for x in lines]
        if lanes > len(lines) * share:
            pieces.append(jnp.zeros((owners * height, lanes - len(lines) * share), F32))
        block = jnp.concatenate(pieces, axis=1)
        for e in range(owners):
            out[e, t] = block[e * height : (e + 1) * height].astype(BF16)


def flip_kernel(kernel, taps):
    spread_taps(kernel, taps, True)


def soft_sign(gaps):
    return gaps * lax.rsqrt(gaps * gaps + smooth_width * smooth_width)


def score_kernel(members, used, rows, halo, got, legendre, target, order, back, drained, spread, gather, picked, grads, sent):
    owners, groups, height, lanes = got.shape
    orders, nlat, degrees = legendre.shape
    slots = target.shape[1]
    ens = owners * members
    for t in range(groups):
        pieces = []
        for e in range(owners):
            block = got[e, t].astype(F32)
            for b in range(members):
                pieces.append(block[b * used : (b + 1) * used])
                if slots > used:
                    pieces.append(jnp.zeros((slots - used, lanes), F32))
        block = jnp.concatenate(pieces, axis=0).T
        at, part = t * rows * orders, halo * orders
        first, second = (at, at + part) if t % 2 else (at + part, at)
        spread[first : first + part, :] = block[:part]
        spread[second : second + part, :] = block[part : 2 * part]
    reorder = jnp.where(
        lax.broadcasted_iota(jnp.int32, (degrees, degrees), 0) == order[...], 1.0, 0.0
    )
    picked[...] = reorder.astype(BF16)
    edge = halo * orders
    gather[:edge, :] = jnp.zeros((edge, ens * slots), F32)
    gather[edge + nlat * orders :, :] = jnp.zeros((edge, ens * slots), F32)

    def score(values, truth):
        own = [values[k * slots : (k + 1) * slots] for k in range(ens)]
        sums = [None] * ens
        for k in range(ens):
            for n in range(k + 1, ens):
                sign = soft_sign(own[k] - own[n])
                sums[k] = sign if sums[k] is None else sums[k] + sign
                sums[n] = -sign if sums[n] is None else sums[n] - sign
        return jnp.concatenate(
            [
                soft_sign(own[k] - truth) * (1.0 / ens) - sums[k] * (1.0 / (ens * (ens - 1)))
                for k in range(ens)
            ],
            axis=0,
        )

    tail = degrees % 128
    packs = tail > 0 and 128 % tail == 0 and orders % (128 // tail) == 0
    step = 128 // tail if packs else 1
    body = degrees - tail if packs else degrees

    span = step * ens * slots

    def drain(trip):
        lines = pl.ds(pl.multiple_of(trip * span, 8), span)
        return pltpu.make_async_copy(grads.at[:, lines], drained.at[:, lines], sent.at[trip])

    @pl.loop(0, orders // step)
    def _(trip):
        numbers = [trip * step + j for j in range(step)]
        coeffs = [
            lax.dot_general(
                spread[pl.ds(m, nlat, stride=orders), :].astype(BF16),
                legendre[m],
                (((0,), (0,)), ((), ())),
                preferred_element_type=F32,
            )
            for m in numbers
        ]
        truths = [target[m].astype(F32) for m in numbers]
        scored = [score(x[:, :body], y[:, :body]) for x, y in zip(coeffs, truths)]
        if packs:
            rest = score(
                jnp.concatenate([x[:, body:] for x in coeffs], axis=1),
                jnp.concatenate([y[:, body:] for y in truths], axis=1),
            )
            scored = [
                jnp.concatenate([x, rest[:, j * tail : (j + 1) * tail]], axis=1)
                for j, x in enumerate(scored)
            ]
        for m, grad in zip(numbers, scored):
            grad = grad.astype(BF16)
            gather[pl.ds(edge + m, nlat, stride=orders), :] = lax.dot_general(
                legendre[m], grad, (((1,), (1,)), ((), ())), preferred_element_type=F32
            )
            at = pl.multiple_of(m * ens * slots, 8)
            ordered = jnp.dot(grad, picked[...], preferred_element_type=F32)
            for j in range(grads.shape[0]):
                last = min(degrees, (j + 1) * 128)
                grads[j, pl.ds(at, ens * slots), : last - j * 128] = ordered[:, j * 128 : last].astype(BF16)
        drain(trip).start()

    wide = back.shape[3]
    tall = (rows + 2 * halo) * orders
    for t in range(groups):
        at = t * rows * orders
        block = gather[at : at + tall, :]
        if wide > tall:
            block = jnp.concatenate([block, jnp.zeros((wide - tall, ens * slots), F32)], axis=0)
        block = block.T
        for e in range(owners):
            pieces = []
            for b in range(members):
                at = (e * members + b) * slots
                pieces.append(block[at : at + used])
            if height > members * used:
                pieces.append(jnp.zeros((height - members * used, wide), F32))
            back[e, t] = jnp.concatenate(pieces, axis=0).astype(BF16)

    @pl.loop(0, orders // step)
    def _(trip):
        drain(trip).wait()


def backward_kernel(share, flags, got, near, far, inner, outer, taps, mixer, table, out, padded, flat, stage):
    owners, groups, height, _ = got.shape
    half, depth, nlon = inner.shape
    members, rows, chans, _ = out.shape
    size = math.isqrt(taps.shape[0])
    span = table.shape[1] // 2
    total = rows + 2 * half
    blocks = [
        jnp.concatenate([got[e, t].astype(F32) for e in range(owners)], axis=0) for t in range(groups)
    ]
    lines = []
    for i in range(total):
        pieces = [x[:, i * share : (i + 1) * share] for x in blocks]
        pieces.append(jnp.zeros((owners * height, span - groups * share), F32))
        line = jnp.concatenate(pieces, axis=1).astype(BF16)
        lines.append(
            jnp.concatenate(
                [
                    lax.dot_general(
                        mixer[r], line, (((0,), (0,)), ((), ())), preferred_element_type=F32
                    ).astype(BF16)
                    for r in range(2)
                ],
                axis=1,
            )
        )
    flat[...] = lax.dot_general(
        jnp.concatenate(lines, axis=0),
        table[...],
        (((1,), (1,)), ((), ())),
        preferred_element_type=F32,
    ).reshape(flat.shape)
    odd = flags[0] == 1
    pairs = ((near, far), (inner, outer), (outer, inner), (far, near))
    for part, (one, other) in enumerate(pairs):
        for row in range(half):
            at = part * half + row
            slope = jnp.where(odd, one[row].astype(F32), other[row].astype(F32))
            fill_row(padded, at, flat[at] * slope, half)

    @pl.loop(0, depth // TILE)
    def _(ct):
        c0 = pl.multiple_of(ct * TILE, TILE)

        @pl.loop(0, rows)
        def _(i):
            value = tap_sum(padded, taps, c0, [(i + p, p) for p in range(size)], size)
            value = value + padded[i + half, pl.ds(c0, TILE), :].astype(F32)
            stage[i, pl.ds(c0, TILE), :] = value[:, :nlon]

    for b in range(members):
        for i in range(rows):
            out[b, i] = stage[i, b * chans : (b + 1) * chans, :].astype(BF16)


def pack_kernel(members, used, per_owner, rounded, out, grads):
    owners, groups, depth, lanes = out.shape
    share = depth // members
    stride = grads.shape[1] // share
    grads[...] = rounded[...].astype(F32)
    slots = stride // (owners * members)
    for e in range(owners):
        for b in range(members):
            at = (e * members + b) * slots
            planes = [
                jnp.concatenate(
                    [grads[j, pl.ds(at + s, share, stride=stride), :] for j in range(grads.shape[0])],
                    axis=1,
                )
                for s in range(used)
            ]
            for t in range(groups):
                pieces = [x[:, t * per_owner : (t + 1) * per_owner] for x in planes]
                if lanes > used * per_owner:
                    pieces.append(jnp.zeros((share, lanes - used * per_owner), F32))
                out[e, t, b * share : (b + 1) * share, :] = jnp.concatenate(pieces, axis=1).astype(BF16)


def unpack_kernel(members, got, result, out, sent):
    owners, groups, depth, lanes = got.shape
    _, chans, per_owner, _, orders = out.shape
    share, chan_share = depth // members, chans // owners
    pair = 2 * per_owner

    def iotas(shape):
        return (lax.broadcasted_iota(jnp.int32, shape, d) for d in range(2))

    row, column = iotas((chan_share * pair, lanes))
    wanted = ((row % 2) * chan_share + row // pair) * per_owner + (row % pair) // 2
    swapped = jnp.where(column == wanted, 1.0, 0.0).astype(BF16)
    row, column = iotas((groups * depth, orders))
    start = (column // share) * depth + column % share
    pickers = [jnp.where(row == start + b * share, 1.0, 0.0).astype(BF16) for b in range(members)]
    copies = []
    for e in range(owners):
        turned = lax.dot_general(
            swapped,
            got[e].reshape(groups * depth, lanes),
            (((1,), (1,)), ((), ())),
            preferred_element_type=F32,
        ).astype(BF16)
        for b in range(members):
            lines = jnp.dot(turned, pickers[b], preferred_element_type=F32)
            for c in range(chan_share):
                block = lines[c * pair : (c + 1) * pair]
                out[b, e * chan_share + c] = block.reshape(per_owner, 2, orders)
            place = pl.ds(e * chan_share, chan_share)
            copies.append(
                pltpu.make_async_copy(out.at[b, place], result.at[b, place], sent.at[e, b])
            )
            copies[-1].start()
    for copy in copies:
        copy.wait()


def local(fields, depth_kernel, mix_weight, legendre, truth, degree_order):
    ens_parts, groups = lax.axis_size("ens"), lax.axis_size("lat")
    ens_at, lat_at = lax.axis_index("ens"), lax.axis_index("lat")
    members, chans, rows, nlon = fields.shape
    _, orders, degrees = legendre.shape
    ens = members * ens_parts
    nlat = rows * groups
    share, per_owner, chan_share = orders // groups, degrees // groups, chans // ens_parts
    used = 2 * chan_share
    slots = up(used, 8)
    height = up(members * used, 8)
    span = up(orders, 128)
    size = depth_kernel.shape[1]
    halo = size // 2
    wide = up(nlon + 2 * halo, 128)
    depth = members * chans

    table = jnp.asarray(wave_table(nlon, orders, span))
    kernel = depth_kernel.transpose(1, 2, 0)
    flags = place()
    own = fields.transpose(0, 2, 1, 3)
    odd = lat_at % 2
    near, far = partners(
        lax.dynamic_slice_in_dim(own, (1 - odd) * (rows - halo), halo, 1),
        lax.dynamic_slice_in_dim(own, odd * (rows - halo), halo, 1),
    )

    pick = np.zeros((2, members, ens_parts, height, chans), np.float32)
    for r in range(2):
        for b in range(members):
            for o in range(chans):
                at = b * used + r * chan_share + o % chan_share
                pick[r, b, o // chan_share, at, o] = 1.0
    pick = jnp.asarray(pick.reshape(2, members, ens_parts * height, chans).astype(jnp.bfloat16))

    def grant(mebibytes):
        return pltpu.CompilerParams(vmem_limit_bytes=mebibytes * 1024 * 1024)

    scalars = pl.BlockSpec(memory_space=pltpu.SMEM)
    whole = pl.BlockSpec(memory_space=pltpu.VMEM)
    grid_shape = (members, rows, chans, nlon)
    lined = jax.ShapeDtypeStruct((rows, depth, nlon), F32)
    edge = jax.ShapeDtypeStruct((halo, depth, nlon), BF16)
    taps_out = jax.ShapeDtypeStruct((size * size, depth, 128), BF16)

    def call(body, outs, scratch, name, work, *args, drained=(), fetched=()):
        outs = outs if isinstance(outs, tuple) else (outs,)
        places = [
            pl.BlockSpec(memory_space=pltpu.HBM if i in drained else pltpu.VMEM)
            for i in range(len(outs))
        ]
        specs = [scalars if a is flags else whole for a in args]
        for i in fetched:
            specs[i] = pl.BlockSpec(memory_space=pltpu.HBM)
        made = pl.pallas_call(
            body,
            out_shape=outs,
            in_specs=specs,
            out_specs=tuple(places),
            scratch_shapes=scratch,
            compiler_params=grant(60 if name in ("prepare", "nearer", "farther") else 28),
            cost_estimate=pl.CostEstimate(
                flops=work, transcendentals=0, bytes_accessed=8 * rows * depth * nlon
            ),
        )(*args)
        return made if len(outs) > 1 else made[0]

    def swap(x):
        flat = x.reshape((ens_parts * groups,) + x.shape[2:])
        flat = lax.all_to_all(flat, ("ens", "lat"), split_axis=0, concat_axis=0, tiled=True)
        return flat.reshape(x.shape)

    work = 2 * size * size * rows * depth * nlon
    partial, mixer = call(
        prepare_kernel,
        (lined, jax.ShapeDtypeStruct((2, ens_parts * height, depth), BF16)),
        [pltpu.VMEM((rows, depth, wide), BF16), pltpu.VMEM(taps_out.shape, BF16)],
        "prepare",
        work,
        own,
        kernel,
        mix_weight,
        pick,
    )
    target = lax.dynamic_slice(
        truth, (ens_at * chan_share, 0, lat_at * share, 0), (chan_share, 2, share, degrees)
    )
    target = target.transpose(2, 1, 0, 3).reshape(share, used, degrees)
    target = jnp.pad(target, ((0, 0), (0, slots - used), (0, 0)))

    slab = legendre.reshape(rows, groups, share * degrees).transpose(1, 0, 2)
    line = math.gcd(rows * share * degrees, 128)
    slab = slab.reshape(groups, rows * share * degrees // line, line)

    def chunk(lines):
        return jax.ShapeDtypeStruct((ens_parts, groups, height, up(lines * share, 128)), BF16)

    half_scratch = [
        pltpu.VMEM((halo, depth, wide), BF16),
        pltpu.VMEM((halo, depth, nlon), BF16),
        pltpu.VMEM(taps_out.shape, BF16),
        pltpu.VMEM((halo, depth, nlon), F32),
        pltpu.VMEM(table.shape, BF16),
        pltpu.SemaphoreType.DMA((2,)),
    ]
    mixed, inner = call(
        near_kernel,
        (jax.ShapeDtypeStruct((halo, ens_parts * height, span), BF16), edge),
        half_scratch,
        "nearer",
        work // 2,
        flags,
        near,
        partial,
        kernel,
        table,
        mixer,
        fetched=(2, 4),
    )
    slab, mixed = lax.optimization_barrier((slab, mixed))
    slab = lax.all_to_all(slab, "lat", split_axis=0, concat_axis=0, tiled=True)
    order_legendre = slab.reshape(nlat, share, degrees).transpose(1, 0, 2)
    sent, outer = call(
        functools.partial(far_kernel, share),
        (chunk(rows), edge),
        half_scratch,
        "farther",
        work // 2,
        flags,
        far,
        partial,
        kernel,
        table,
        mixer,
        mixed,
        fetched=(2, 4),
    )
    got = swap(sent)
    got, held = lax.optimization_barrier((got, outer))
    near, far = partners(inner, held)
    back, grads = call(
        functools.partial(score_kernel, members, used, rows, halo),
        (
            chunk(rows + 2 * halo),
            pltpu.HBM((up(degrees, 128) // 128, share * ens * slots, 128), BF16),
        ),
        [
            pltpu.VMEM((nlat * share, ens * slots), F32),
            pltpu.VMEM(((nlat + 2 * halo) * share, ens * slots), F32),
            pltpu.VMEM((degrees, degrees), BF16),
            pltpu.VMEM((up(degrees, 128) // 128, share * ens * slots, 128), BF16),
            pltpu.SemaphoreType.DMA((share,)),
        ],
        "score",
        work,
        got,
        order_legendre,
        target,
        degree_order.reshape(1, degrees),
        drained=(1,),
    )
    returned = swap(back)
    packed = call(
        functools.partial(pack_kernel, members, used, per_owner),
        jax.ShapeDtypeStruct(
            (ens_parts, groups, members * share, up(used * per_owner, 128)), BF16
        ),
        [pltpu.VMEM(grads.shape, F32)],
        "pack",
        work,
        grads,
    )
    owned = swap(packed)
    flipped = call(flip_kernel, taps_out, [], "flip", work // 8, kernel)
    grad_fields = call(
        functools.partial(backward_kernel, share),
        jax.ShapeDtypeStruct(grid_shape, BF16),
        [
            pltpu.VMEM((rows + 2 * halo, depth, wide), BF16),
            pltpu.VMEM((rows + 2 * halo, depth, nlon), F32),
            pltpu.VMEM((rows, depth, nlon), F32),
        ],
        "backward",
        work,
        flags,
        returned,
        near,
        far,
        inner,
        outer,
        flipped,
        mixer,
        table,
    )
    score_grad = call(
        functools.partial(unpack_kernel, members),
        jax.ShapeDtypeStruct((members, chans, per_owner, 2, orders), F32),
        [
            pltpu.VMEM((members, chans, per_owner, 2, orders), F32),
            pltpu.SemaphoreType.DMA((ens_parts, members)),
        ],
        "unpack",
        work,
        owned,
        drained=(0,),
    )
    return grad_fields.transpose(0, 2, 1, 3), score_grad.transpose(0, 1, 3, 4, 2)


def solution(mesh):
    placed = (P("ens", None, "lat", None), P(), P(), P("lat", None, None), P(), P())

    return jax.shard_map(
        local,
        mesh=mesh,
        in_specs=placed,
        out_specs=(P("ens", None, "lat", None), P("ens", None, None, None, "lat")),
        check_vma=False,
    )
```
